32 devices in a mesh: dp: 4 (over z), tx: 2 (over y), ty: 4 (over x, core).
Axes of the slice: x: 2, y: 2, z: 4, core: 2. Of those that a mesh axis runs over, the one named last changes fastest.
Arguments:
- inputs: bfloat16 [8, 1024, 2048], P('dp', 'ty'), may hold values from -6 to 6
- lengths: int32 [8], replicated, may hold values from 1 to 1024, 5120 in all
- prompt_deal: int32 [8], replicated, may hold values from 0 to 7, each once
- block_owner: int32 [4], replicated, may hold values from 0 to 3, each once
- attn_gain: float32 [2048], replicated, may hold values from 0.5 to 1.5
- latent_gain: float32 [512], replicated, may hold values from 0.5 to 1.5
- final_gain: float32 [2048], replicated, may hold values from 0.5 to 1.5
- w_query: float32 [2048, 3072], P('dp', ('tx', 'ty')), may hold values from -4 to 4
- w_down_kv: float32 [2048, 576], P('dp'), may hold values from -0.125 to 0.125
- w_up_kv: float32 [512, 4096], P('dp', ('tx', 'ty')), may hold values from -4 to 4
- w_out: float32 [2048, 2048], P('dp', 'tx'), may hold values from -0.125 to 0.125
- w_vocab: float32 [2048, 57344], P('dp', ('tx', 'ty')), may hold values from -0.125 to 0.125
Outputs:
- hidden_out: bfloat16 [8, 1024, 2048], P('dp', 'ty', 'tx')
- logits: float32 [8, 57344], P('dp', ('tx', 'ty'))
The draws below stay inside these ranges and needn't reach their ends.
Inputs may be any that keep to these rules, and one draw needn't show every extreme that they name: `prompt_deal`: a permutation of the 8 prompts. `block_owner`: a permutation of the 4 row blocks. `lengths`: some prompt has exactly 1024 live tokens.
All inputs are finite; a program needn't handle non-finite values.
Results may differ from the reference program's by a relative error of at most 0.0065.
The reference program's roundings to bfloat16 on the way count: a program that leaves them out, or rounds other values in their place, can miss the bound.
Values may be sent and summed in bfloat16 or wider, within the bound.
A program may use at most 192 MiB of HBM per device.

```python
import math
import jax
import jax.numpy as jnp
import numpy as np
from jax import lax

D = 2048
HEADS = 16
NOPE = 128
ROPE = 64
LATENT = 512
VOCAB = 57344
LEN = 1024
GROUPS = 4
PROMPTS = 8


def draw_w_query(key, part):
    base = jax.random.normal(jax.random.fold_in(key, 1), (D, HEADS * (NOPE + ROPE)), jnp.float32)
    base = jnp.clip(base, -6.0, 6.0) * D ** (-0.5)
    return jnp.clip(base, -4.0, 4.0)


def draw_w_up_kv(key, part):
    base = jax.random.normal(jax.random.fold_in(key, 3), (LATENT, 2 * HEADS * NOPE), jnp.float32)
    base = jnp.clip(base, -6.0, 6.0) * LATENT ** (-0.5)
    return jnp.clip(base, -4.0, 4.0)


def shard_levels(stream_key, extent, pieces, low, top_value):
    def one(dim, shards_of):
        draws = jax.random.uniform(jax.random.fold_in(jax.random.fold_in(stream_key, 6), dim), (shards_of,), jnp.float32, low / len(pieces), top_value / len(pieces))
        return jnp.repeat(jnp.exp(draws), extent[dim] // shards_of).reshape((-1,) + (1,) * (len(extent) - dim - 1))

    loudness = one(*pieces[0])
    for cut in pieces[1:]:
        loudness = loudness * one(*cut)
    return loudness


def split_up(number_of, total, bound, lean):
    weights = [(1 << 20) // math.isqrt(grade ** lean) + 1 for grade in range(2, number_of + 1)]
    rest, given = total - bound - (number_of - 1), [1] * (number_of - 1)
    while rest > 0:
        candidates = [i for i in range(number_of - 1) if given[i] < bound]
        mass, remaining = sum([weights[i] for i in candidates]), rest
        for i in candidates:
            extra = min(bound - given[i], max(1, remaining * weights[i] // mass), rest)
            given[i] = given[i] + extra
            rest = rest - extra
    return np.array([bound] + given)


def ragged_sizes(stream_key, number_of, total, limit, lean):
    if number_of == 2:
        one = jax.random.randint(stream_key, (), max(1, total - limit), min(limit, total - 1) + 1)
        return jnp.stack([one, total - one])
    sizes = jnp.asarray(split_up(number_of, total, limit, lean), jnp.int32)
    couples = (number_of - 1) // 2
    giver, receiver = sizes[1:1 + 2 * couples:2], sizes[2:2 + 2 * couples:2]
    room = jnp.minimum(giver - 1, limit - receiver)
    moved = jax.random.randint(jax.random.fold_in(stream_key, 1), (couples,), 0, 1 << 20) % (room + 1)
    sizes = sizes.at[1:1 + 2 * couples:2].set(giver - moved).at[2:2 + 2 * couples:2].set(receiver + moved)
    return sizes[jax.random.permutation(jax.random.fold_in(stream_key, 2), number_of)]


def scatter_about(own_key, extent, scale, limit, pieces=(), kind=jnp.bfloat16):
    array = scale * jax.random.normal(own_key, extent, jnp.float32)
    if pieces:
        array = array * shard_levels(own_key, extent, pieces, -0.22, 0.18)
    return jnp.clip(array, -limit, limit).astype(kind)


def setup_inputs(seed: int = 0) -> dict:
    key_of = jax.random.split(jax.random.key(seed), 13)
    inputs = scatter_about(key_of[0], (PROMPTS, LEN, D), 1.0, 6.0, ((0, 4), (1, 4)))
    lengths = ragged_sizes(key_of[1], PROMPTS, PROMPTS * LEN * 5 // 8, LEN, 2).astype(jnp.int32)
    prompt_deal = jax.random.permutation(key_of[2], PROMPTS).astype(jnp.int32)
    block_owner = jax.random.permutation(key_of[3], GROUPS).astype(jnp.int32)
    attn_gain = jnp.clip(1.0 + 0.1 * jax.random.normal(key_of[4], (D,), jnp.float32), 0.5, 1.5)
    latent_gain = jnp.clip(1.0 + 0.1 * jax.random.normal(key_of[5], (LATENT,), jnp.float32), 0.5, 1.5)
    final_gain = jnp.clip(1.0 + 0.1 * jax.random.normal(key_of[6], (D,), jnp.float32), 0.5, 1.5)
    w_query = draw_w_query(jax.random.fold_in(key_of[12], 71), 0)
    w_down_kv = scatter_about(key_of[8], (D, LATENT + ROPE), D ** -0.5, 0.125, ((0, 4),), jnp.float32)
    w_up_kv = draw_w_up_kv(jax.random.fold_in(key_of[12], 71), 0)
    w_out = scatter_about(key_of[10], (D, HEADS * NOPE), (HEADS * NOPE) ** -0.5, 0.125, ((0, 4), (1, 2)), jnp.float32)
    w_vocab = scatter_about(key_of[11], (D, VOCAB), D ** -0.5, 0.125, ((0, 4), (1, 8)), jnp.float32)
    return {"inputs": inputs, "lengths": lengths, "prompt_deal": prompt_deal, "block_owner": block_owner, "attn_gain": attn_gain, "latent_gain": latent_gain, "final_gain": final_gain, "w_query": w_query, "w_down_kv": w_down_kv, "w_up_kv": w_up_kv, "w_out": w_out, "w_vocab": w_vocab}


EPS = 1e-06

def normalize(values, gain):
    wide = values.astype(jnp.float32)
    return wide * lax.rsqrt(lax.optimization_barrier(jnp.mean(wide * wide, axis=-1, keepdims=True)) + EPS) * gain

def rotate(values, position):
    half_dim = values.shape[-1] // 2
    frequency = 10000.0 ** (-jnp.arange(half_dim, dtype=jnp.float32) / half_dim)
    angles = position.astype(jnp.float32)[..., None] * frequency
    cosine = jnp.cos(angles)
    sine = jnp.sin(angles)
    first_half = values[..., :half_dim]
    second_half = values[..., half_dim:]
    return jnp.concatenate([first_half * cosine - second_half * sine, first_half * sine + second_half * cosine], axis=-1)

def reference(inputs, lengths, prompt_deal, block_owner, attn_gain, latent_gain, final_gain, w_query, w_down_kv, w_up_kv, w_out, w_vocab):
    inverse = jnp.zeros((GROUPS,), jnp.int32).at[block_owner].set(jnp.arange(GROUPS, dtype=jnp.int32))

    def logical(stored):
        block_rows = stored.shape[0] // GROUPS
        blocks = stored.reshape((GROUPS, block_rows) + stored.shape[1:])
        return jnp.take(blocks, inverse, axis=0).reshape(stored.shape).astype(jnp.bfloat16)
    query_w = logical(w_query)
    down_w = logical(w_down_kv)
    up_w = logical(w_up_kv)
    out_w = logical(w_out)
    vocab_w = logical(w_vocab)
    live_len = jnp.take(lengths, prompt_deal).astype(jnp.int32)
    position = jnp.arange(LEN, dtype=jnp.int32)
    score_scale = (NOPE + ROPE) ** (-0.5)

    def one_prompt(packed):
        tokens, live = packed
        normed = normalize(tokens, attn_gain).astype(jnp.bfloat16)
        queries = jnp.dot(normed, query_w, preferred_element_type=jnp.float32).reshape(LEN, HEADS, NOPE + ROPE)
        queries = jnp.concatenate([queries[..., :NOPE], rotate(queries[..., NOPE:], position[:, None])], axis=-1).astype(jnp.bfloat16)
        down_proj = jnp.dot(normed, down_w, preferred_element_type=jnp.float32)
        latent = normalize(down_proj[:, :LATENT], latent_gain).astype(jnp.bfloat16)
        key_rope = rotate(down_proj[:, LATENT:], position).astype(jnp.bfloat16)
        key_val = jnp.dot(latent, up_w, preferred_element_type=jnp.float32).astype(jnp.bfloat16).reshape(LEN, HEADS, 2, NOPE)
        key_nope = key_val[:, :, 0].astype(jnp.float32)
        values = key_val[:, :, 1].astype(jnp.float32)
        query_wide = queries.astype(jnp.float32)
        scores = (jnp.einsum('qhd,khd->hqk', query_wide[..., :NOPE], key_nope) + jnp.einsum('qhd,kd->hqk', query_wide[..., NOPE:], key_rope.astype(jnp.float32))) * score_scale
        allowed = (position[None, :] <= position[:, None]) & (position[None, :] < live)
        scores = jnp.where(allowed[None], scores, -1e+30)
        top = lax.optimization_barrier(jnp.max(scores, axis=-1, keepdims=True))
        expo = jnp.exp(scores - top)
        softmax_w = (expo / lax.optimization_barrier(jnp.sum(expo, axis=-1, keepdims=True))).astype(jnp.bfloat16)
        attended = jnp.einsum('hqk,khd->qhd', softmax_w.astype(jnp.float32), values).astype(jnp.bfloat16).reshape(LEN, HEADS * NOPE)
        branch = lax.dot_general(attended, out_w, (((1,), (1,)), ((), ())), preferred_element_type=jnp.float32)
        layer_out = (tokens.astype(jnp.float32) + branch).astype(jnp.bfloat16)
        last_row = lax.dynamic_slice_in_dim(layer_out, live - 1, 1, 0)[0]
        return (layer_out, last_row)
    hidden_out, last_rows = lax.map(one_prompt, (inputs, live_len))
    final_rows = normalize(last_rows, final_gain).astype(jnp.bfloat16)
    logits = jnp.dot(final_rows, vocab_w, preferred_element_type=jnp.float32)
    return (hidden_out, logits)
```

```python
import functools

import jax
import jax.numpy as jnp
import numpy as np
from jax import lax
from jax.experimental import pallas as pl
from jax.experimental.pallas import tpu as pltpu
from jax.sharding import PartitionSpec as P

NOPE = 128
ROPE = 64
LATENT = 512
LEN = 1024
TILE = 256
EPS = 1e-06
QCOLS = 384
ACOLS = 640


def normalize(values, gain):
    wide = values.astype(jnp.float32)
    return wide * lax.rsqrt(jnp.mean(wide * wide, axis=-1, keepdims=True) + EPS) * gain


def dot32(left, right):
    return jnp.dot(left, right, preferred_element_type=jnp.float32)


def remote(src, dst, send, recv, **where):
    return pltpu.make_async_remote_copy(
        src_ref=src,
        dst_ref=dst,
        send_sem=send,
        recv_sem=recv,
        device_id=where,
        device_id_type=pl.DeviceIdType.MESH,
    )


def greet(**where):
    pl.semaphore_signal(
        pltpu.get_barrier_semaphore(),
        inc=1,
        device_id=where,
        device_id_type=pl.DeviceIdType.MESH,
    )


def layer_kernel(
    groups, owner_ref, lengths_ref, deal_ref, x_ref, again_ref, lgain_ref, fgain_ref, cos_ref,
    sin_ref, wq_ref, wa_ref, wb_ref, wo_ref, vocab_ref, hidden_ref, out_ref,
    xs, h, wcat, wbs, wbl, woz, give, wos, acc, k_ref, v_ref, o_ref, heard, table, stage,
    wq_f, wa_f, wb_f, wo_f, seen, full, rows_ref, part, incoming, picked_ref,
    local, v_sem, x_send, x_recv, y_send, y_recv, p_send, p_recv, b_send, b_recv,
    z_send, z_recv, a_send, a_recv, o_send, o_recv, w_send, w_recv,
    t_send, t_recv, r_send, r_recv, l_send, l_recv,
):
    dp, tx, ty = lax.axis_index("dp"), lax.axis_index("tx"), lax.axis_index("ty")
    tx_size, ty_size = 2, 4
    per_grp = 2
    partner = ty + 1 - 2 * (ty % 2)
    across = (ty + 2) % 4
    far = (partner + 2) % 4
    other = 1 - tx
    spot = tx * ty_size + ty
    plane = tx_size * ty_size
    steps = groups - 1
    chunks = 4
    quarter, width = x_ref.shape[1], x_ref.shape[2]
    half = width // tx_size
    block = width // groups
    rows = quarter // chunks
    words = vocab_ref.shape[1]
    slab = stage.shape[-1]
    count = words // slab
    piece = 2 * NOPE

    arows = block // ty_size
    loads = [
        pltpu.make_async_copy(
            wa_ref.at[pl.ds(pl.multiple_of(ty * arows, arows), arows)], wa_f, local.at[0]
        ),
        pltpu.make_async_copy(wq_ref, wq_f, local.at[1]),
        pltpu.make_async_copy(wb_ref, wb_f, local.at[2]),
        pltpu.make_async_copy(
            wo_ref.at[:, pl.ds(pl.multiple_of(ty * piece, piece), piece)], wo_f, local.at[3]
        ),
        pltpu.make_async_copy(x_ref, xs.at[ty], local.at[4]),
    ]
    for load in loads:
        load.start()

    def vocab_load(k, slot):
        cols = pl.ds(pl.multiple_of(k * slab, slab), slab)
        return pltpu.make_async_copy(vocab_ref.at[:, cols], stage.at[slot], v_sem.at[slot])

    vocab_load(0, 0).start()

    for k in range(1, plane):
        peer = (spot + k) % plane
        greet(tx=peer // ty_size, ty=peer % ty_size)
    for k in range(1, groups):
        for t in range(tx_size):
            greet(dp=(dp + k) % groups, tx=t)
    pl.semaphore_wait(pltpu.get_barrier_semaphore(), plane - 1 + (groups - 1) * tx_size)

    def cut(slot, prompt, k):
        return xs.at[slot, prompt, pl.ds(k * rows, rows)]

    def crossing(k, slot):
        src = x_ref.at[tx, pl.ds(k * rows, rows)]
        return remote(src, cut(slot, tx, k), x_send.at[k], x_recv.at[k], ty=across)

    def sideways(k, prompt):
        p = cut(across, prompt, k)
        return remote(p, p, y_send.at[k], y_recv.at[k], tx=other)

    def inward(k, side, slot, prompt):
        p = cut(slot, prompt, k)
        return remote(p, p, p_send.at[side, k], p_recv.at[side, k], ty=partner)

    def own_rows(slot):
        return remote(x_ref, xs.at[slot], b_send.at[0], b_recv.at[0], ty=partner)

    A, Q, B, O = range(4)

    def a_part(g, q):
        return wcat.at[g, pl.ds(pl.multiple_of(q * arows, arows), arows), pl.ds(QCOLS, ACOLS)]

    slots = [
        lambda g: a_part(g, ty),
        lambda g: wcat.at[g, :, pl.ds(0, QCOLS)],
        lambda g: wbs.at[g],
        lambda g: woz.at[g],
    ]

    def hop(which, way, step):
        sign = 1 - 2 * way
        g = dp - sign * step
        runs = (g >= 0) & (g < groups) & (dp + sign >= 0) & (dp + sign < groups)
        ref = slots[which](g)
        copy = remote(
            ref, ref, z_send.at[way, which, step], z_recv.at[way, which, step], dp=dp + sign
        )
        return copy, runs

    def arrival(which, way, step):
        sign = 1 - 2 * way
        g = dp - sign * (step + 1)
        ref = slots[which](g)
        copy = remote(
            ref, ref, z_send.at[way, which, step], z_recv.at[way, which, step], dp=dp
        )
        return copy, (g >= 0) & (g < groups)

    def start_hop(which, step):
        for way in range(2):
            copy, runs = hop(which, way, step)
            pl.when(runs)(copy.start)

    def wait_hop(which, step):
        for way in range(2):
            copy, comes = arrival(which, way, step)
            pl.when(comes)(copy.wait_recv)

    def share(n, g, q):
        ref = a_part(g, q)
        where = across if n == 0 else partner
        return remote(ref, ref, a_send.at[n, g], a_recv.at[n, g], ty=where)

    def share_first(g):
        share(0, g, ty).start()
        share(1, g, ty).start()

    def share_second(g):
        share(0, g, across).wait_recv()
        share(2, g, across).start()

    def share_wait(g):
        share(1, g, partner).wait_recv()
        share(2, g, far).wait_recv()

    def arrived(step, act):
        for way in range(2):
            g = dp - (1 - 2 * way) * (step + 1)

            @pl.when((g >= 0) & (g < groups))
            def _():
                act(g)

    for k in range(chunks):
        crossing(k, ty).start()
    own_rows(ty).start()

    loads[0].wait()
    wide_a = wa_f[...].astype(jnp.bfloat16)
    wcat[dp, pl.ds(pl.multiple_of(ty * arows, arows), arows), QCOLS : QCOLS + LATENT] = wide_a[
        :, :LATENT
    ]
    twice = (
        lax.broadcasted_iota(jnp.int32, (ROPE, 2 * ROPE), 0)
        == lax.broadcasted_iota(jnp.int32, (ROPE, 2 * ROPE), 1) % ROPE
    ).astype(jnp.bfloat16)
    wcat[dp, pl.ds(pl.multiple_of(ty * arows, arows), arows), QCOLS + LATENT :] = dot32(
        wide_a[:, LATENT:], twice
    ).astype(jnp.bfloat16)
    start_hop(A, 0)
    share_first(dp)
    loads[1].wait()
    wcat[dp, :, 0:NOPE] = wq_f[:, 0:NOPE].astype(jnp.bfloat16)
    turned = pltpu.roll(wq_f[:, NOPE:], 2 * NOPE - ROPE, 1)
    wcat[dp, :, NOPE:QCOLS] = turned.astype(jnp.bfloat16)
    start_hop(Q, 0)
    loads[2].wait()
    wbs[dp] = wb_f[...].astype(jnp.bfloat16)
    start_hop(B, 0)
    loads[3].wait()
    woz[dp] = wo_f[...].T.astype(jnp.bfloat16)

    def vocab_step(k, _):
        slot = k % 2

        @pl.when(k + 1 < count)
        def _():
            vocab_load(k + 1, 1 - slot).start()

        vocab_load(k, slot).wait()
        cols = pl.ds(pl.multiple_of(k * slab, slab), slab)
        table[:, cols] = stage[slot].astype(jnp.bfloat16)
        return 0

    lax.fori_loop(0, count, vocab_step, 0)

    part_rows = 32

    def norm(slot, prompt):
        def body(i, _):
            at = pl.multiple_of(i * part_rows, part_rows)
            value = normalize(xs[slot, prompt, pl.ds(at, part_rows)], again_ref[...])
            value = value.astype(jnp.bfloat16)
            to = pl.multiple_of(prompt * LEN + slot * quarter + at, part_rows)
            for b in range(groups):
                h[b, pl.ds(to, part_rows)] = value[:, b * block : (b + 1) * block]
            return 0

        lax.fori_loop(0, quarter // part_rows, body, 0)

    loads[4].wait()
    norm(ty, 0)
    wait_hop(A, 0)
    if steps > 1:
        start_hop(A, 1)
    arrived(0, share_first)
    norm(ty, 1)
    for k in range(chunks):
        crossing(k, across).wait_recv()
        sideways(k, tx).start()
        inward(k, 0, across, tx).start()
        if k == 1:
            wait_hop(Q, 0)
            if steps > 1:
                start_hop(Q, 1)
        if k == 2:
            wait_hop(B, 0)
            if steps > 1:
                start_hop(B, 1)
        if k == 0:
            own_rows(partner).wait_recv()
            norm(partner, 0)
        if k == 1:
            norm(partner, 1)
    share_second(dp)
    arrived(0, share_second)
    if steps > 1:
        wait_hop(A, 1)
        if steps > 2:
            start_hop(A, 2)
        arrived(1, share_first)
    norm(across, tx)
    for k in range(chunks):
        inward(k, 0, far, tx).wait_recv()
    norm(far, tx)
    for k in range(chunks):
        sideways(k, other).wait_recv()
        inward(k, 1, across, other).start()
    norm(across, other)
    for k in range(chunks):
        inward(k, 1, far, other).wait_recv()
    norm(far, other)
    if steps > 1:
        for which in (Q, B):
            wait_hop(which, 1)
            if steps > 2:
                start_hop(which, 2)
        arrived(1, share_second)
    start_hop(O, 0)

    span_rows = 512

    def project(g, first):
        share_wait(g)
        own = owner_ref[g]

        def body(i, _):
            at = pl.ds(pl.multiple_of(i * span_rows, span_rows), span_rows)
            term = dot32(h[own, at], wcat[g])
            acc[at] = term if first else acc[at] + term
            return 0

        lax.fori_loop(0, per_grp * LEN // span_rows, body, 0)

    project(dp, True)
    for step in range(steps):
        if step == 2:
            wait_hop(A, 2)
            arrived(2, share_first)
            wait_hop(Q, 2)
            wait_hop(B, 2)
            arrived(2, share_second)

        def both(way, _):
            g = dp - (1 - 2 * way) * (step + 1)

            @pl.when((g >= 0) & (g < groups))
            def _():
                project(g, False)

            return 0

        lax.fori_loop(0, 2, both, 0)

    def stored(b):
        place = jnp.int32(0)
        for g in range(groups):
            place = jnp.where(owner_ref[g] == b, g, place)
        return place

    brows = LATENT // groups
    for b in range(groups):
        wbl[b * brows : (b + 1) * brows] = wbs[stored(b)]

    lane = lax.broadcasted_iota(jnp.int32, (TILE, 2 * ROPE), 1)

    def rotate(values, at):
        swapped = jnp.where(
            lane % ROPE < ROPE // 2,
            pltpu.roll(values, 2 * ROPE - ROPE // 2, 1),
            pltpu.roll(values, ROPE // 2, 1),
        )
        return values * cos_ref[at] + swapped * sin_ref[at]

    heads = 2
    factor = (NOPE + ROPE) ** (-0.5) * 1.4426950408889634
    lives = [lengths_ref[deal_ref[dp * per_grp + p]] for p in range(per_grp)]

    def heads_of(p, to_tx, tile, slot):
        return remote(
            o_ref.at[tile, p], heard.at[p, :, pl.ds(pl.multiple_of(slot * piece, piece), piece)],
            o_send.at[p, to_tx * ty_size + tile], o_recv.at[p, slot], tx=to_tx, ty=tile,
        )

    tile_order = (3, 1, 2, 0)

    def prompt_step(p, _):
        live = jnp.where(p == 0, lives[0], lives[1])
        for t in range(LEN // TILE):
            here = pl.ds(t * TILE, TILE)
            down = acc[pl.ds(pl.multiple_of(p * LEN + t * TILE, TILE), TILE), QCOLS:]
            latent = normalize(down[:, :LATENT], lgain_ref[...]).astype(jnp.bfloat16)
            key_rope = rotate(down[:, LATENT:], here).astype(jnp.bfloat16)
            key_val = dot32(latent, wbl[...]).astype(jnp.bfloat16)
            for head in range(heads):
                k_ref[head, here, :NOPE] = key_val[:, 2 * head * NOPE : (2 * head + 1) * NOPE]
                k_ref[head, here, NOPE:] = key_rope
                v_ref[head, here] = key_val[:, (2 * head + 1) * NOPE : (2 * head + 2) * NOPE]
        for t in tile_order:
            span = (t + 1) * TILE
            values = acc[pl.ds(pl.multiple_of(p * LEN + t * TILE, TILE), TILE), :QCOLS]
            turned = rotate(values[:, 2 * NOPE :], pl.ds(t * TILE, TILE))
            i = lax.broadcasted_iota(jnp.int32, (TILE, span), 0) + t * TILE
            j = lax.broadcasted_iota(jnp.int32, (TILE, span), 1)
            allowed = j <= jnp.minimum(i, live - 1)
            for head in range(heads):
                mine = jnp.where(lane // ROPE == 1 - head, turned, 0.0)
                query = jnp.concatenate(
                    [values[:, head * NOPE : (head + 1) * NOPE], mine], axis=1
                ).astype(jnp.bfloat16)
                score = lax.dot_general(
                    query, k_ref[head, :span], (((1,), (1,)), ((), ())),
                    preferred_element_type=jnp.float32,
                )
                score = jnp.where(allowed, score, -1e30)
                expo = jnp.exp2((score - jnp.max(score, axis=-1, keepdims=True)) * factor)
                prob = expo * (1.0 / jnp.sum(expo, axis=-1, keepdims=True))
                out = dot32(prob.astype(jnp.bfloat16), v_ref[head, :span])
                o_ref[t, p, :, head * NOPE : (head + 1) * NOPE] = out.astype(jnp.bfloat16)

            @pl.when(ty == t)
            def _():
                heard[p, :, pl.ds(pl.multiple_of(spot * piece, piece), piece)] = o_ref[t, p]

            @pl.when(ty != t)
            def _():
                heads_of(p, tx, t, spot).start()

            heads_of(p, other, t, spot).start()

        for way in range(2):
            copy, comes = arrival(O, way, p)
            pl.when(comes)(copy.wait_recv)
        for way in range(2):
            copy, runs = hop(O, way, p + 1)
            pl.when(runs)(copy.start)
        return 0

    lax.fori_loop(0, per_grp, prompt_step, 0)
    wait_hop(O, 2)

    def wide(slot_tx, slot_ty, i):
        slot = slot_tx * ty_size + slot_ty
        return wos.at[pl.ds(pl.multiple_of(slot * piece, piece), piece), pl.ds(i * block, block)]

    def move(n, i, slot_tx, slot_ty, source=None, **where):
        ref = wide(slot_tx, slot_ty, i)
        return remote(
            ref if source is None else source, ref, w_send.at[n, i], w_recv.at[n, i], **where
        )

    share_blocks = groups // tx_size
    for i in range(share_blocks):
        give[i] = woz[stored(share_blocks * other + i)]
        move(0, i, tx, ty, give.at[i], tx=other).start()
        wos[pl.ds(pl.multiple_of(spot * piece, piece), piece), i * block : (i + 1) * block] = woz[
            stored(share_blocks * tx + i)
        ]
        move(1, i, tx, ty, ty=across).start()
        move(2, i, tx, ty, ty=partner).start()
    for i in range(share_blocks):
        move(0, i, other, ty, tx=other).wait_recv()
        move(3, i, other, ty, ty=across).start()
        move(4, i, other, ty, ty=partner).start()
    for i in range(share_blocks):
        move(1, i, tx, across, ty=across).wait_recv()
        move(5, i, tx, across, ty=partner).start()
    for i in range(share_blocks):
        move(3, i, other, across, ty=across).wait_recv()
        move(6, i, other, across, ty=partner).start()
    for p in range(per_grp):
        for k in range(1, plane):
            source = (spot + k) % plane
            heads_of(p, tx, ty, source).wait_recv()
    for i in range(share_blocks):
        move(2, i, tx, partner, ty=partner).wait_recv()
        move(4, i, other, partner, ty=partner).wait_recv()
        move(5, i, tx, far, ty=partner).wait_recv()
        move(6, i, other, far, ty=partner).wait_recv()

    strip = 256
    row = lax.broadcasted_iota(jnp.int32, (quarter, strip), 0)

    def out_step(n, _):
        cols = pl.ds(pl.multiple_of(n * strip, strip), strip)
        wide_cols = pl.ds(pl.multiple_of(tx * half + n * strip, strip), strip)
        for p in range(per_grp):
            total = dot32(heard[p], wos[:, cols])
            hidden = (xs[ty, p, :, wide_cols].astype(jnp.float32) + total).astype(jnp.bfloat16)
            hidden_ref[p, :, cols] = hidden
            last = row == lives[p] - 1 - ty * quarter
            picked_ref[p : p + 1, cols] = jnp.sum(
                jnp.where(last, hidden.astype(jnp.float32), 0.0), axis=0, keepdims=True
            )
        return 0

    lax.fori_loop(0, half // strip, out_step, 0)

    peers = groups * tx_size
    place = dp * tx_size + tx

    def along_ty(k, slot):
        return remote(
            picked_ref, seen.at[slot], t_send.at[k], t_recv.at[k], ty=(ty + k) % ty_size
        )

    for k in range(1, ty_size):
        along_ty(k, ty).start()
    merged = picked_ref[...]
    for k in range(1, ty_size):
        slot = (ty + ty_size - k) % ty_size
        along_ty(k, slot).wait_recv()
        merged = merged + seen[slot]
    full[place] = merged

    def along_peers(k, slot):
        peer = (place + k) % peers
        return remote(
            full.at[place], full.at[slot], r_send.at[k], r_recv.at[k],
            dp=peer // tx_size, tx=peer % tx_size,
        )

    for k in range(1, peers):
        along_peers(k, place).start()
    for k in range(1, peers):
        along_peers(k, (place + peers - k) % peers).wait_recv()
    for g in range(groups):
        for t in range(tx_size):
            rows_ref[g * per_grp : (g + 1) * per_grp, t * half : (t + 1) * half] = full[
                g * tx_size + t
            ]
    final = normalize(rows_ref[...], fgain_ref[...])
    owner = owner_ref[dp]
    mine = jnp.zeros((groups * per_grp, block), jnp.float32)
    for g in range(groups):
        mine = jnp.where(owner == g, final[:, g * block : (g + 1) * block], mine)
    mine = mine.astype(jnp.bfloat16)

    def logit_step(k, _):
        cols = pl.ds(pl.multiple_of(k * slab, slab), slab)
        logits = dot32(mine, table[:, cols])
        for g in range(groups):
            part[g, :, cols] = logits[g * per_grp : (g + 1) * per_grp]
        return 0

    lax.fori_loop(0, count, logit_step, 0)

    def along_dp(k, slot):
        peer = (dp + k) % groups
        return remote(part.at[peer], incoming.at[slot], l_send.at[k], l_recv.at[k], dp=peer)

    for k in range(1, groups):
        along_dp(k, dp).start()
    total = part[dp]
    for k in range(1, groups):
        slot = (dp + groups - k) % groups
        along_dp(k, slot).wait_recv()
        total = total + incoming[slot]
    out_ref[...] = total

    for k in range(chunks):
        crossing(k, ty).wait_send()
        sideways(k, tx).wait_send()
        inward(k, 0, across, tx).wait_send()
        inward(k, 1, across, other).wait_send()
    own_rows(ty).wait_send()
    for step in range(steps):
        for which in range(4):
            for way in range(2):
                copy, runs = hop(which, way, step)
                pl.when(runs)(copy.wait_send)
    for g in range(groups):
        share(0, g, ty).wait_send()
        share(1, g, ty).wait_send()
        share(2, g, across).wait_send()
    for p in range(per_grp):
        for t in range(ty_size):

            @pl.when(ty != t)
            def _():
                heads_of(p, tx, t, spot).wait_send()

            heads_of(p, other, t, spot).wait_send()
    for i in range(share_blocks):
        move(0, i, tx, ty, give.at[i], tx=other).wait_send()
        move(1, i, tx, ty, ty=across).wait_send()
        move(2, i, tx, ty, ty=partner).wait_send()
        move(3, i, other, ty, ty=across).wait_send()
        move(4, i, other, ty, ty=partner).wait_send()
        move(5, i, tx, across, ty=partner).wait_send()
        move(6, i, other, across, ty=partner).wait_send()
    for k in range(1, ty_size):
        along_ty(k, ty).wait_send()
    for k in range(1, peers):
        along_peers(k, place).wait_send()
    for k in range(1, groups):
        along_dp(k, dp).wait_send()


def layer(groups, owner, lengths, deal, x, again, lgain, fgain, wq, wa, wb, wo, vocab):
    per_grp, quarter, width = x.shape
    block, words = vocab.shape
    half = width // 2
    piece = 2 * NOPE
    slab = 512
    steps = groups - 1
    peers = 2 * groups
    position = np.arange(LEN, dtype=np.float32)
    frequency = np.power(
        np.float32(10000.0), -np.arange(ROPE // 2, dtype=np.float32) / np.float32(ROPE // 2)
    ).astype(np.float32)
    angles = (position[:, None] * frequency).astype(np.float32).astype(np.float64)
    cosine, sine = np.cos(angles), np.sin(angles)
    cosine = jnp.asarray(np.concatenate([cosine] * 4, axis=1).astype(np.float32))
    sine = jnp.asarray(np.concatenate([-sine, sine, -sine, sine], axis=1).astype(np.float32))
    dma = pltpu.SemaphoreType.DMA
    vmem = pl.BlockSpec(memory_space=pltpu.VMEM)
    smem = pl.BlockSpec(memory_space=pltpu.SMEM)
    hbm = pl.BlockSpec(memory_space=pl.ANY)
    bf16 = lambda *dims: pltpu.VMEM(dims, jnp.bfloat16)
    f32 = lambda *dims: pltpu.VMEM(dims, jnp.float32)
    return pl.pallas_call(
        functools.partial(layer_kernel, groups),
        in_specs=[smem, smem, smem, hbm, vmem, vmem, vmem, vmem, vmem, hbm, hbm, hbm, hbm, hbm],
        out_specs=[vmem, vmem],
        out_shape=[
            jax.ShapeDtypeStruct((per_grp, quarter, half), jnp.bfloat16),
            jax.ShapeDtypeStruct((per_grp, words), jnp.float32),
        ],
        scratch_shapes=[
            bf16(4, per_grp, quarter, width),
            bf16(groups, per_grp * LEN, block),
            bf16(groups, block, QCOLS + ACOLS),
            bf16(groups, LATENT // groups, 2 * piece),
            bf16(LATENT, 2 * piece),
            bf16(groups, piece, block),
            bf16(2, piece, block),
            bf16(8 * piece, half),
            f32(per_grp * LEN, QCOLS + ACOLS),
            bf16(2, LEN, 2 * NOPE),
            bf16(2, LEN, NOPE),
            bf16(4, per_grp, TILE, piece),
            bf16(per_grp, TILE, 8 * piece),
            bf16(block, words),
            f32(2, block, slab),
            f32(*wq.shape),
            f32(block // 4, wa.shape[1]),
            f32(*wb.shape),
            f32(block, piece),
            f32(4, per_grp, half),
            f32(peers, per_grp, half),
            f32(groups * per_grp, width),
            f32(groups, per_grp, words),
            f32(groups, per_grp, words),
            f32(per_grp, half),
            dma((5,)), dma((2,)),
            dma((4,)), dma((4,)), dma((4,)), dma((4,)), dma((2, 4)), dma((2, 4)), dma((1,)),
            dma((1,)),
            dma((2, 4, steps)), dma((2, 4, steps)), dma((3, groups)), dma((3, groups)),
            dma((per_grp, 8)), dma((per_grp, 8)), dma((7, 2)), dma((7, 2)),
            dma((4,)), dma((4,)), dma((peers,)), dma((peers,)), dma((groups,)), dma((groups,)),
        ],
        compiler_params=pltpu.CompilerParams(
            collective_id=0, has_side_effects=True, vmem_limit_bytes=60 * 1024 * 1024
        ),
        cost_estimate=pl.CostEstimate(
            flops=16_000_000_000, bytes_accessed=24_000_000, transcendentals=3_000_000
        ),
    )(owner, lengths, deal, x, again, lgain, fgain, cosine, sine, wq, wa, wb, wo, vocab)


def load_vocab(vocab_chunk, vocab_ref, table, v_sem):
    loads = []
    for k in range(vocab_ref.shape[1] // vocab_chunk):
        cols = pl.ds(k * vocab_chunk, vocab_chunk)
        loads.append(
            pltpu.make_async_copy(vocab_ref.at[:, cols], table.at[:, cols], v_sem.at[k])
        )
        loads[-1].start()
    return loads


def next_token(
    groups, tx_size, ty_size, vocab_chunk, loads, owner_ref, picked_ref, gain_ref, out_ref, seen, full,
    rows_ref, table, part, incoming, t_send, t_recv, r_send, r_recv, l_send, l_recv,
):
    dp, tx, ty = lax.axis_index("dp"), lax.axis_index("tx"), lax.axis_index("ty")
    per_grp, half = picked_ref.shape
    block = table.shape[0]
    peers = groups * tx_size
    place = dp * tx_size + tx
    count = len(loads)

    def along_ty(k, slot):
        return remote(
            picked_ref, seen.at[slot], t_send.at[k], t_recv.at[k], ty=(ty + k) % ty_size
        )

    for k in range(1, ty_size):
        along_ty(k, ty).start()
    merged = picked_ref[...]
    for k in range(1, ty_size):
        slot = (ty + ty_size - k) % ty_size
        along_ty(k, slot).wait_recv()
        merged = merged + seen[slot]
    full[place] = merged

    def along_peers(k, slot):
        peer = (place + k) % peers
        return remote(
            full.at[place], full.at[slot], r_send.at[k], r_recv.at[k],
            dp=peer // tx_size, tx=peer % tx_size,
        )

    for k in range(1, peers):
        along_peers(k, place).start()
    for k in range(1, peers):
        along_peers(k, (place + peers - k) % peers).wait_recv()
    for g in range(groups):
        for t in range(tx_size):
            rows_ref[g * per_grp : (g + 1) * per_grp, t * half : (t + 1) * half] = full[
                g * tx_size + t
            ]
    final = normalize(rows_ref[...], gain_ref[...])
    owner = owner_ref[dp]
    mine = jnp.zeros((groups * per_grp, block), jnp.float32)
    for g in range(groups):
        mine = jnp.where(owner == g, final[:, g * block : (g + 1) * block], mine)
    mine = mine.astype(jnp.bfloat16)
    for k in range(count):
        loads[k].wait()
        cols = slice(k * vocab_chunk, (k + 1) * vocab_chunk)
        logits = dot32(mine, table[:, cols].astype(jnp.bfloat16))
        for g in range(groups):
            part[g, :, cols] = logits[g * per_grp : (g + 1) * per_grp]

    def along_dp(k, slot):
        peer = (dp + k) % groups
        return remote(part.at[peer], incoming.at[slot], l_send.at[k], l_recv.at[k], dp=peer)

    for k in range(1, groups):
        along_dp(k, dp).start()
    total = part[dp]
    for k in range(1, groups):
        slot = (dp + groups - k) % groups
        along_dp(k, slot).wait_recv()
        total = total + incoming[slot]
    out_ref[...] = total
    for k in range(1, ty_size):
        along_ty(k, ty).wait_send()
    for k in range(1, peers):
        along_peers(k, place).wait_send()
    for k in range(1, groups):
        along_dp(k, dp).wait_send()


def tail_kernel(
    groups, tx_size, ty_size, vocab_chunk, owner_ref, picked_ref, gain_ref, vocab_ref, out_ref,
    seen, full, rows_ref, table, part, incoming, t_send, t_recv, r_send, r_recv, l_send, l_recv,
    v_sem,
):
    dp, tx, ty = lax.axis_index("dp"), lax.axis_index("tx"), lax.axis_index("ty")
    peers = groups * tx_size
    place = dp * tx_size + tx
    loads = load_vocab(vocab_chunk, vocab_ref, table, v_sem)
    for k in range(1, ty_size):
        greet(ty=(ty + k) % ty_size)
    for k in range(1, peers):
        peer = (place + k) % peers
        greet(dp=peer // tx_size, tx=peer % tx_size)
    pl.semaphore_wait(pltpu.get_barrier_semaphore(), ty_size + peers - 2)
    next_token(
        groups, tx_size, ty_size, vocab_chunk, loads, owner_ref, picked_ref, gain_ref, out_ref,
        seen, full, rows_ref, table, part, incoming, t_send, t_recv, r_send, r_recv, l_send,
        l_recv,
    )


def tail(groups, tx_size, ty_size, owner, picked, gain, vocab):
    per_grp, half = picked.shape
    block, words = vocab.shape
    vocab_chunk = 512
    peers = groups * tx_size
    dma = pltpu.SemaphoreType.DMA
    vmem = pl.BlockSpec(memory_space=pltpu.VMEM)
    return pl.pallas_call(
        functools.partial(tail_kernel, groups, tx_size, ty_size, vocab_chunk),
        in_specs=[
            pl.BlockSpec(memory_space=pltpu.SMEM), vmem, vmem, pl.BlockSpec(memory_space=pl.ANY),
        ],
        out_specs=vmem,
        out_shape=jax.ShapeDtypeStruct((per_grp, words), jnp.float32),
        scratch_shapes=[
            pltpu.VMEM((ty_size, per_grp, half), jnp.float32),
            pltpu.VMEM((peers, per_grp, half), jnp.float32),
            pltpu.VMEM((groups * per_grp, half * tx_size), jnp.float32),
            pltpu.VMEM((block, words), jnp.float32),
            pltpu.VMEM((groups, per_grp, words), jnp.float32),
            pltpu.VMEM((groups, per_grp, words), jnp.float32),
            dma((ty_size,)), dma((ty_size,)), dma((peers,)), dma((peers,)),
            dma((groups,)), dma((groups,)), dma((words // vocab_chunk,)),
        ],
        compiler_params=pltpu.CompilerParams(
            collective_id=1, has_side_effects=True, vmem_limit_bytes=40 * 1024 * 1024
        ),
        cost_estimate=pl.CostEstimate(
            flops=100_000_000, bytes_accessed=16_000_000, transcendentals=0
        ),
    )(owner, picked, gain, vocab)


def rotate_half(values, position):
    half_dim = values.shape[-1] // 2
    frequency = 10000.0 ** (-jnp.arange(half_dim, dtype=jnp.float32) / half_dim)
    angles = position.astype(jnp.float32)[..., None] * frequency
    cosine = jnp.cos(angles)
    sine = jnp.sin(angles)
    first_half = values[..., :half_dim]
    second_half = values[..., half_dim:]
    return jnp.concatenate(
        [first_half * cosine - second_half * sine, first_half * sine + second_half * cosine],
        axis=-1,
    )


def split_positions(
    inputs, inverse, live_len, attn_gain, latent_gain, w_query, w_down_kv, w_up_kv, w_out
):
    groups = lax.axis_size("dp")

    def arrange(gathered):
        block_rows = gathered.shape[0] // groups
        return jnp.concatenate(
            [
                lax.dynamic_slice_in_dim(gathered, inverse[g] * block_rows, block_rows, 0)
                for g in range(groups)
            ],
            axis=0,
        )

    query_w, down_w, up_w, out_w = (
        lax.all_gather(w_query.astype(jnp.bfloat16), "dp", axis=0, tiled=True),
        lax.all_gather(w_down_kv.astype(jnp.bfloat16), "dp", axis=0, tiled=True),
        lax.all_gather(w_up_kv.astype(jnp.bfloat16), "dp", axis=0, tiled=True),
        lax.all_gather(w_out.astype(jnp.bfloat16), "dp", axis=0, tiled=True),
    )
    query_w = arrange(query_w)
    down_w = arrange(down_w)
    up_w = arrange(up_w)
    out_w = arrange(out_w)
    query_w, up_w = (
        lax.all_gather(query_w, "ty", axis=1, tiled=True),
        lax.all_gather(up_w, "ty", axis=1, tiled=True),
    )
    per_grp, quarter, width = inputs.shape
    heads = query_w.shape[1] // (NOPE + ROPE)
    position = lax.axis_index("ty") * quarter + jnp.arange(quarter, dtype=jnp.int32)
    flat_rows = inputs.reshape(per_grp * quarter, width)
    normed = normalize(flat_rows, attn_gain).astype(jnp.bfloat16)
    queries = jnp.dot(normed, query_w, preferred_element_type=jnp.float32).reshape(
        per_grp, quarter, heads, NOPE + ROPE
    )
    queries = jnp.concatenate(
        [queries[..., :NOPE], rotate_half(queries[..., NOPE:], position[None, :, None])], axis=-1
    ).astype(jnp.bfloat16)
    down_proj = jnp.dot(normed, down_w, preferred_element_type=jnp.float32).reshape(
        per_grp, quarter, LATENT + ROPE
    )
    latent = normalize(down_proj[..., :LATENT], latent_gain).astype(jnp.bfloat16)
    key_rope = rotate_half(down_proj[..., LATENT:], position[None, :]).astype(jnp.bfloat16)
    gathered = lax.all_gather(
        jnp.concatenate([latent, key_rope], axis=-1), "ty", axis=1, tiled=True
    )
    key_val = jnp.dot(gathered[..., :LATENT], up_w, preferred_element_type=jnp.float32).astype(
        jnp.bfloat16
    )
    rope_all = gathered[..., LATENT:]
    key_val = key_val.reshape(per_grp, LEN, heads, 2, NOPE)
    key_nope = key_val[:, :, :, 0]
    values = key_val[:, :, :, 1]
    score_scale = (NOPE + ROPE) ** (-0.5)
    scores = (
        jnp.einsum(
            "pqhd,pkhd->phqk", queries[..., :NOPE], key_nope, preferred_element_type=jnp.float32
        )
        + jnp.einsum(
            "pqhd,pkd->phqk", queries[..., NOPE:], rope_all, preferred_element_type=jnp.float32
        )
    ) * score_scale
    key_pos = jnp.arange(LEN, dtype=jnp.int32)
    allowed = (key_pos[None, None, :] <= position[None, :, None]) & (
        key_pos[None, None, :] < live_len[:, None, None]
    )
    scores = jnp.where(allowed[:, None], scores, -1e30)
    top = jnp.max(scores, axis=-1, keepdims=True)
    expo = jnp.exp(scores - top)
    softmax_w = (expo / jnp.sum(expo, axis=-1, keepdims=True)).astype(jnp.bfloat16)
    attended = jnp.einsum(
        "phqk,pkhd->pqhd", softmax_w, values, preferred_element_type=jnp.float32
    ).astype(jnp.bfloat16)
    attended = attended.reshape(per_grp * quarter, heads * NOPE)
    own_width = width // lax.axis_size("tx")
    col_start = lax.axis_index("tx") * own_width
    partial_value = lax.dot_general(
        attended, out_w, (((1,), (1,)), ((), ())), preferred_element_type=jnp.float32
    ).reshape(per_grp, quarter, width)
    summed = lax.psum_scatter(partial_value, "tx", scatter_dimension=2, tiled=True)
    residual = lax.dynamic_slice_in_dim(inputs, col_start, own_width, 2)
    layer_out = (residual.astype(jnp.float32) + summed).astype(jnp.bfloat16)
    return layer_out


def shards(
    inputs,
    lengths,
    prompt_deal,
    block_owner,
    attn_gain,
    latent_gain,
    final_gain,
    w_query,
    w_down_kv,
    w_up_kv,
    w_out,
    w_vocab,
):
    groups = lax.axis_size("dp")
    dp, tx, ty = lax.axis_index("dp"), lax.axis_index("tx"), lax.axis_index("ty")
    per_grp, quarter, width = inputs.shape
    half = width // lax.axis_size("tx")
    whole_heads = w_query.shape[1] == QCOLS and w_up_kv.shape[1] == 4 * NOPE
    here = whole_heads and (lax.axis_size("tx"), lax.axis_size("ty"), per_grp) == (2, 4, 2)
    if here and groups == 4 and (quarter, width) == (TILE, 4 * w_query.shape[0]):
        return tuple(
            layer(
                groups, block_owner, lengths, prompt_deal, inputs, attn_gain[None],
                latent_gain[None], final_gain[None], w_query, w_down_kv, w_up_kv, w_out, w_vocab,
            )
        )

    order = jnp.arange(groups, dtype=jnp.int32)
    inverse = jnp.sum(
        jnp.where(block_owner[None, :] == order[:, None], order[None, :], 0), axis=1
    ).astype(jnp.int32)
    slots = dp * per_grp + jnp.arange(per_grp, dtype=jnp.int32)
    names = jnp.arange(lengths.shape[0], dtype=jnp.int32)

    def at_index(values, index):
        return jnp.sum(jnp.where(names[None] == index[:, None], values[None], 0), axis=1)

    live_len = at_index(lengths, at_index(prompt_deal, slots))
    layer_out = split_positions(
        inputs, inverse, live_len, attn_gain, latent_gain, w_query, w_down_kv, w_up_kv, w_out
    )

    at = live_len - 1 - ty * quarter
    picked = jnp.stack(
        [
            lax.dynamic_slice(
                layer_out, (i, jnp.clip(at[i], 0, quarter - 1), 0), (1, 1, half)
            ).reshape(half)
            for i in range(per_grp)
        ]
    ).astype(jnp.float32)
    inside = (at >= 0) & (at < quarter)
    picked = jnp.where(inside[:, None], picked, 0.0)
    logits = tail(
        groups, lax.axis_size("tx"), lax.axis_size("ty"), block_owner, picked, final_gain[None],
        w_vocab,
    )
    return (layer_out, logits)


def solution(mesh):
    placed = (
        P("dp", "ty", None),
        P(),
        P(),
        P(),
        P(),
        P(),
        P(),
        P("dp", ("tx", "ty")),
        P("dp", None),
        P("dp", ("tx", "ty")),
        P("dp", "tx"),
        P("dp", ("tx", "ty")),
    )
    return jax.shard_map(
        shards,
        mesh=mesh,
        in_specs=placed,
        out_specs=(P("dp", "ty", "tx"), P("dp", ("tx", "ty"))),
        check_vma=False,
    )
```

```python
import functools

import jax
import jax.numpy as jnp
import numpy as np
from jax import lax
from jax.experimental import pallas as pl
from jax.experimental.pallas import tpu as pltpu
from jax.sharding import PartitionSpec as P

NOPE = 128
ROPE = 64
LATENT = 512
LEN = 1024
TILE = 256
EPS = 1e-06
QCOLS = 384
ACOLS = 640


def normalize(values, gain):
    wide = values.astype(jnp.float32)
    return wide * lax.rsqrt(jnp.mean(wide * wide, axis=-1, keepdims=True) + EPS) * gain


def dot32(left, right):
    return jnp.dot(left, right, preferred_element_type=jnp.float32)


def remote(src, dst, send, recv, **where):
    return pltpu.make_async_remote_copy(
        src_ref=src,
        dst_ref=dst,
        send_sem=send,
        recv_sem=recv,
        device_id=where,
        device_id_type=pl.DeviceIdType.MESH,
    )


def greet(**where):
    pl.semaphore_signal(
        pltpu.get_barrier_semaphore(),
        inc=1,
        device_id=where,
        device_id_type=pl.DeviceIdType.MESH,
    )


def layer_kernel(
    groups, owner_ref, lengths_ref, deal_ref, x_ref, again_ref, lgain_ref, fgain_ref, cos_ref,
    sin_ref, wq_ref, wa_ref, wb_ref, wo_ref, vocab_ref, hidden_ref, out_ref,
    xs, h, wcat, wbs, wbl, woz, give, wos, acc, k_ref, v_ref, o_ref, heard, table, stage,
    wq_f, wa_f, wb_f, wo_f, seen, full, rows_ref, part, incoming, picked_ref,
    local, v_sem, x_send, x_recv, y_send, y_recv, p_send, p_recv, b_send, b_recv,
    z_send, z_recv, a_send, a_recv, o_send, o_recv, f_send, f_recv, w_send, w_recv,
    t_send, t_recv, r_send, r_recv, l_send, l_recv,
):
    dp, tx, ty = lax.axis_index("dp"), lax.axis_index("tx"), lax.axis_index("ty")
    tx_size, ty_size = 2, 4
    per_grp = 2
    core = ty % 2
    partner = ty + 1 - 2 * core
    across = (ty + 2) % 4
    far = (partner + 2) % 4
    other = 1 - tx
    spot = tx * ty_size + ty
    plane = tx_size * ty_size
    steps = groups - 1
    chunks = 4
    quarter, width = x_ref.shape[1], x_ref.shape[2]
    half = width // tx_size
    block = width // groups
    rows = quarter // chunks
    words = vocab_ref.shape[1]
    slab = stage.shape[-1]
    count = words // slab
    piece = 2 * NOPE
    heads = 2

    loads = [
        pltpu.make_async_copy(wa_ref.at[:, pl.ds(pl.multiple_of((spot // 2) * 128, 128), 128)], wa_f, local.at[0]),
        pltpu.make_async_copy(wb_ref, wb_f, local.at[1]),
        pltpu.make_async_copy(wq_ref, wq_f, local.at[2]),
        pltpu.make_async_copy(
            wo_ref.at[:, pl.ds(pl.multiple_of(ty * piece, piece), piece)], wo_f, local.at[3]
        ),
        pltpu.make_async_copy(x_ref, xs.at[ty], local.at[4]),
    ]
    for load in loads:
        load.start()

    def vocab_load(k, slot):
        cols = pl.ds(pl.multiple_of(k * slab, slab), slab)
        return pltpu.make_async_copy(vocab_ref.at[:, cols], stage.at[slot], v_sem.at[slot])

    vocab_load(0, 0).start()

    for k in range(1, plane):
        peer = (spot + k) % plane
        greet(tx=peer // ty_size, ty=peer % ty_size)
    for k in range(1, groups):
        for t in range(tx_size):
            greet(dp=(dp + k) % groups, tx=t)
    pl.semaphore_wait(pltpu.get_barrier_semaphore(), plane - 1 + (groups - 1) * tx_size)

    def cut(slot, prompt, k):
        return xs.at[slot, prompt, pl.ds(k * rows, rows)]

    def crossing(k, slot):
        src = x_ref.at[tx, pl.ds(k * rows, rows)]
        return remote(src, cut(slot, tx, k), x_send.at[k], x_recv.at[k], ty=across)

    def sideways(k, prompt):
        p = cut(across, prompt, k)
        return remote(p, p, y_send.at[k], y_recv.at[k], tx=other)

    def inward(k, side, slot, prompt):
        p = cut(slot, prompt, k)
        return remote(p, p, p_send.at[side, k], p_recv.at[side, k], ty=partner)

    def own_rows(slot):
        return remote(x_ref, xs.at[slot], b_send.at[0], b_recv.at[0], ty=partner)

    def cross_step(k):
        crossing(k, across).wait_recv()
        sideways(k, tx).start()
        inward(k, 0, across, tx).start()

    def side_step(k):
        sideways(k, other).wait_recv()
        inward(k, 1, across, other).start()

    A, B, Q, R, O = range(5)
    arows = block // plane

    def a_part(g, q):
        return wcat.at[g, pl.ds(pl.multiple_of(q * arows, arows), arows), pl.ds(QCOLS, ACOLS)]

    slots = [
        lambda g: a_part(g, spot),
        lambda g: wbs.at[g],
        lambda g: wcat.at[g, :, pl.ds(NOPE, QCOLS - NOPE)],
        lambda g: wcat.at[g, :, pl.ds(0, NOPE)],
        lambda g: woz.at[g],
    ]

    def hop(which, way, step):
        sign = 1 - 2 * way
        g = dp - sign * step
        runs = (g >= 0) & (g < groups) & (dp + sign >= 0) & (dp + sign < groups)
        ref = slots[which](g)
        copy = remote(
            ref, ref, z_send.at[way, which, step], z_recv.at[way, which, step], dp=dp + sign
        )
        return copy, runs

    def arrival(which, way, step):
        sign = 1 - 2 * way
        g = dp - sign * (step + 1)
        ref = slots[which](g)
        copy = remote(
            ref, ref, z_send.at[way, which, step], z_recv.at[way, which, step], dp=dp
        )
        return copy, (g >= 0) & (g < groups)

    inner = (dp > 0) & (dp < groups - 1)

    def start_hop(which):
        for way in range(2):
            copy, runs = hop(which, way, 0)
            pl.when(runs)(copy.start)

    def forward(which, step):
        for way in range(2):
            copy, comes = arrival(which, way, step)
            onward = hop(which, way, step + 1)[0]

            @pl.when(comes & inner)
            def _():
                copy.wait_recv()
                onward.start()

    def take(which, step):
        for way in range(2):
            copy, comes = arrival(which, way, step)
            pl.when(comes & jnp.logical_not(inner))(copy.wait_recv)

    def both(which, step):
        forward(which, step)
        take(which, step)

    def share(n, g):
        diagonal = core == 0
        q = [
            spot, spot, spot, jnp.where(diagonal, tx * ty_size + across, other * ty_size + ty),
            tx * ty_size + across, other * ty_size + ty, other * ty_size + across,
        ][n]
        where = [
            dict(ty=across), dict(tx=other), dict(ty=partner),
            dict(tx=jnp.where(diagonal, other, tx), ty=jnp.where(diagonal, ty, across)),
            dict(ty=partner), dict(ty=partner), dict(ty=partner),
        ][n]
        ref = a_part(g, q)
        return remote(ref, ref, a_send.at[n, g], a_recv.at[n, g], **where)

    def shared(n, g):
        q = [
            tx * ty_size + across, other * ty_size + ty, tx * ty_size + partner,
            other * ty_size + across, tx * ty_size + far, other * ty_size + partner,
            other * ty_size + far,
        ][n]
        ref = a_part(g, q)
        return remote(ref, ref, a_send.at[n, g], a_recv.at[n, g], ty=partner)

    def share_first(g):
        for n in (0, 1, 2):
            share(n, g).start()

    def share_second(g):
        shared(0, g).wait_recv()
        shared(1, g).wait_recv()
        for n in (3, 4, 5):
            share(n, g).start()

    def share_third(g):
        shared(3, g).wait_recv()
        share(6, g).start()

    def share_wait(g):
        for n in (2, 4, 5, 6):
            shared(n, g).wait_recv()

    def arrived(step, act):
        for way in range(2):
            g = dp - (1 - 2 * way) * (step + 1)

            @pl.when((g >= 0) & (g < groups))
            def _():
                act(g)

    for k in range(chunks):
        crossing(k, ty).start()
    own_rows(ty).start()

    loads[0].wait()
    turned_a = wa_f[...].T
    wide_a = jnp.where(spot % 2 == 0, turned_a[:arows], turned_a[arows:]).astype(jnp.bfloat16)
    here = pl.ds(pl.multiple_of(spot * arows, arows), arows)
    wcat[dp, here, QCOLS : QCOLS + LATENT] = wide_a[:, :LATENT]
    twice = (
        lax.broadcasted_iota(jnp.int32, (ROPE, 2 * ROPE), 0)
        == lax.broadcasted_iota(jnp.int32, (ROPE, 2 * ROPE), 1) % ROPE
    ).astype(jnp.bfloat16)
    wcat[dp, here, QCOLS + LATENT :] = dot32(wide_a[:, LATENT:], twice).astype(jnp.bfloat16)
    start_hop(A)
    loads[1].wait()
    wbs[dp] = wb_f[...].astype(jnp.bfloat16)
    start_hop(B)
    loads[2].wait()
    turned_q = pltpu.roll(wq_f[:, NOPE:], 2 * NOPE - ROPE, 1)
    wcat[dp, :, 2 * NOPE : QCOLS] = turned_q[:, NOPE:].astype(jnp.bfloat16)
    wcat[dp, :, NOPE : 2 * NOPE] = wq_f[:, :NOPE].astype(jnp.bfloat16)
    start_hop(Q)
    wcat[dp, :, 0:NOPE] = turned_q[:, :NOPE].astype(jnp.bfloat16)
    share_first(dp)
    loads[3].wait()
    woz[dp] = wo_f[...].T.astype(jnp.bfloat16)

    def vocab_step(k, _):
        slot = k % 2

        @pl.when(k + 1 < count)
        def _():
            vocab_load(k + 1, 1 - slot).start()

        vocab_load(k, slot).wait()
        cols = pl.ds(pl.multiple_of(k * slab, slab), slab)
        table[:, cols] = stage[slot].astype(jnp.bfloat16)
        return 0

    part_rows = 32

    def norm(slot, prompt):
        def body(i, _):
            at = pl.multiple_of(i * part_rows, part_rows)
            value = normalize(xs[slot, prompt, pl.ds(at, part_rows)], again_ref[...])
            value = value.astype(jnp.bfloat16)
            to = pl.multiple_of(prompt * LEN + slot * quarter + at, part_rows)
            for b in range(groups):
                h[b, pl.ds(to, part_rows)] = value[:, b * block : (b + 1) * block]
            return 0

        lax.fori_loop(0, quarter // part_rows, body, 0)

    span_rows = 512

    def project(g, first, low, high):
        own = owner_ref[g]

        def body(i, _):
            at = pl.ds(pl.multiple_of(i * span_rows, span_rows), span_rows)
            term = dot32(h[own, at], wcat[g, :, low:high])
            acc[at, low:high] = term if first else acc[at, low:high] + term
            return 0

        lax.fori_loop(0, per_grp * LEN // span_rows, body, 0)

    def project_step(step):
        def one(way, _):
            g = dp - (1 - 2 * way) * (step + 1)

            @pl.when((g >= 0) & (g < groups))
            def _():
                share_wait(g)
                project(g, False, NOPE, QCOLS + ACOLS)

            return 0

        lax.fori_loop(0, 2, one, 0)

    lax.fori_loop(0, 7, vocab_step, 0)
    both(A, 0)
    arrived(0, share_first)
    cross_step(0)
    both(B, 0)
    lax.fori_loop(7, count, vocab_step, 0)
    loads[4].wait()
    norm(ty, 0)
    cross_step(1)
    norm(ty, 1)
    both(Q, 0)
    both(A, 1)
    arrived(1, share_first)
    own_rows(partner).wait_recv()
    norm(partner, 0)
    cross_step(2)
    side_step(0)
    both(B, 1)
    norm(partner, 1)
    side_step(1)
    cross_step(3)
    both(Q, 1)
    start_hop(R)
    side_step(2)
    norm(across, tx)
    share_second(dp)
    arrived(0, share_second)
    arrived(1, share_second)
    take(A, 2)
    arrived(2, share_first)
    side_step(3)
    for k in range(chunks):
        inward(k, 0, far, tx).wait_recv()
    norm(far, tx)
    norm(across, other)
    share_third(dp)
    arrived(0, share_third)
    arrived(1, share_third)
    forward(R, 0)
    for k in range(chunks):
        inward(k, 1, far, other).wait_recv()
    norm(far, other)
    start_hop(O)
    share_wait(dp)
    project(dp, True, NOPE, QCOLS + ACOLS)
    arrived(2, share_second)
    project_step(0)
    forward(R, 1)
    arrived(2, share_third)
    project_step(1)
    take(B, 2)
    take(Q, 2)
    project_step(2)

    def stored(b):
        place = jnp.int32(0)
        for g in range(groups):
            place = jnp.where(owner_ref[g] == b, g, place)
        return place

    brows = LATENT // groups
    for b in range(groups):
        wbl[b * brows : (b + 1) * brows] = wbs[stored(b)]

    lane = lax.broadcasted_iota(jnp.int32, (TILE, 2 * ROPE), 1)

    def rotate(values, at):
        swapped = jnp.where(
            lane % ROPE < ROPE // 2,
            pltpu.roll(values, 2 * ROPE - ROPE // 2, 1),
            pltpu.roll(values, ROPE // 2, 1),
        )
        return values * cos_ref[at] + swapped * sin_ref[at]

    factor = (NOPE + ROPE) ** (-0.5) * 1.4426950408889634
    lives = [lengths_ref[deal_ref[dp * per_grp + p]] for p in range(per_grp)]

    def keys(i, _):
        down = acc[pl.ds(pl.multiple_of(i * TILE, TILE), TILE), QCOLS:]
        tile = i % (LEN // TILE)
        p = i // (LEN // TILE)
        to = pl.ds(pl.multiple_of(tile * TILE, TILE), TILE)
        latent = normalize(down[:, :LATENT], lgain_ref[...]).astype(jnp.bfloat16)
        key_rope = rotate(down[:, LATENT:], to).astype(jnp.bfloat16)
        key_val = dot32(latent, wbl[...]).astype(jnp.bfloat16)
        for head in range(heads):
            k_ref[p, head, to, :NOPE] = key_val[:, 2 * head * NOPE : (2 * head + 1) * NOPE]
            k_ref[p, head, to, NOPE:] = key_rope
            v_ref[p, head, to] = key_val[:, (2 * head + 1) * NOPE : (2 * head + 2) * NOPE]
        return 0

    lax.fori_loop(0, per_grp * LEN // TILE, keys, 0)

    def hears(p, slot, head):
        cols = pl.ds(pl.multiple_of(slot * piece + head * NOPE, NOPE), NOPE)
        return heard.at[p, :, cols]

    def heads_of(head, p, tile, slot):
        return remote(
            o_ref.at[head, tile, p], hears(p, tx * ty_size + slot, head),
            o_send.at[head, p, tile], o_recv.at[head, p, slot], ty=tile,
        )

    def passed(head, p, slot, slot_tx, source=None):
        ref = hears(p, slot_tx * ty_size + slot, head)
        return remote(
            ref if source is None else source, ref,
            f_send.at[head, p, slot], f_recv.at[head, p, slot], tx=other,
        )

    def own_passed(head, p, tile):
        return passed(head, p, ty, tx, o_ref.at[head, tile, p])

    def relay(head, p):
        for k in range(1, ty_size):
            slot = (ty + k) % ty_size
            heads_of(head, p, ty, slot).wait_recv()
            passed(head, p, slot, tx).start()

    tile_order = (3, 1, 2, 0)

    def attention(head, p, _):
        live = jnp.where(p == 0, lives[0], lives[1])
        nope_at = (1 - head) * NOPE
        for t in tile_order:
            span = (t + 1) * TILE
            at = pl.ds(pl.multiple_of(p * LEN + t * TILE, TILE), TILE)
            turned = rotate(acc[at, 2 * NOPE : QCOLS], pl.ds(t * TILE, TILE))
            i = lax.broadcasted_iota(jnp.int32, (TILE, span), 0) + t * TILE
            j = lax.broadcasted_iota(jnp.int32, (TILE, span), 1)
            allowed = j <= jnp.minimum(i, live - 1)
            mine = jnp.where(lane // ROPE == 1 - head, turned, 0.0)
            query = jnp.concatenate([acc[at, nope_at : nope_at + NOPE], mine], axis=1)
            score = lax.dot_general(
                query.astype(jnp.bfloat16), k_ref[p, head, :span], (((1,), (1,)), ((), ())),
                preferred_element_type=jnp.float32,
            )
            score = jnp.where(allowed, score, -1e30)
            expo = jnp.exp2((score - jnp.max(score, axis=-1, keepdims=True)) * factor)
            prob = expo * (1.0 / jnp.sum(expo, axis=-1, keepdims=True))
            out = dot32(prob.astype(jnp.bfloat16), v_ref[p, head, :span]).astype(jnp.bfloat16)
            o_ref[head, t, p] = out

            @pl.when(ty == t)
            def _():
                mine_at = pl.multiple_of(spot * piece + head * NOPE, NOPE)
                heard[p, :, pl.ds(mine_at, NOPE)] = out
                own_passed(head, p, t).start()

            @pl.when(ty != t)
            def _():
                heads_of(head, p, t, ty).start()

        if head == 0:
            pl.when(p == 0)(lambda: forward(O, 0))
            pl.when(p == 1)(lambda: relay(0, 0))
        else:
            pl.when(p == 0)(lambda: relay(0, 1))
            pl.when(p == 1)(lambda: relay(1, 0))
        return 0

    lax.fori_loop(0, per_grp, functools.partial(attention, 0), 0)
    for step in range(steps):
        take(R, step)
    for k in range(groups):
        project((dp + k) % groups, k == 0, 0, NOPE)
    forward(O, 1)
    lax.fori_loop(0, per_grp, functools.partial(attention, 1), 0)
    relay(1, 1)

    def wide(j, slot_tx, slot_ty):
        slot = slot_tx * ty_size + slot_ty
        return wos.at[j, pl.ds(pl.multiple_of(slot * piece, piece), piece)]

    def move(n, j, slot_tx, slot_ty, source=None, **where):
        ref = wide(j, slot_tx, slot_ty)
        return remote(
            ref if source is None else source, ref, w_send.at[n, j], w_recv.at[n, j], **where
        )

    early = [jnp.where(dp < groups // 2, k, groups - 1 - k) for k in range(steps)]
    late = jnp.where(dp < groups // 2, groups - 1, 0)

    def aim(g):
        return owner_ref[g] // (groups // tx_size)

    def first_for(side):
        found = early[-1]
        for g in early[-2::-1]:
            found = jnp.where(aim(g) == side, g, found)
        return found

    def first_rows(side):
        found = woz[early[-1]]
        for g in early[-2::-1]:
            found = jnp.where(aim(g) == side, woz[g], found)
        return found

    def second_for(side):
        found = late
        for g in early:
            found = jnp.where((aim(g) == side) & (g != first_for(side)), g, found)
        return found

    mine_at = pl.ds(pl.multiple_of(spot * piece, piece), piece)

    def spread(j, give_rows, keep_rows):
        give[j] = give_rows
        move(0, j, tx, ty, give.at[j], tx=other).start()
        wos[j, mine_at] = keep_rows
        move(1, j, tx, ty, ty=across).start()
        move(2, j, tx, ty, ty=partner).start()

    def spread_on(j):
        move(0, j, other, ty, tx=other).wait_recv()
        move(3, j, other, ty, ty=across).start()
        move(4, j, other, ty, ty=partner).start()

    def spread_in(j):
        move(1, j, tx, across, ty=across).wait_recv()
        move(5, j, tx, across, ty=partner).start()

    def spread_last(j):
        move(3, j, other, across, ty=across).wait_recv()
        move(6, j, other, across, ty=partner).start()

    take(O, 0)
    take(O, 1)
    spread(0, first_rows(other), first_rows(tx))
    take(O, 2)
    spread(1, woz[second_for(other)], woz[second_for(tx)])
    for j in range(2):
        spread_on(j)
        spread_in(j)
    for j in range(2):
        spread_last(j)
    for head in range(heads):
        for p in range(per_grp):
            for k in range(ty_size):
                passed(head, p, (ty + k) % ty_size, other).wait_recv()
    for j in range(2):
        move(2, j, tx, partner, ty=partner).wait_recv()
        move(4, j, other, partner, ty=partner).wait_recv()
        move(5, j, tx, far, ty=partner).wait_recv()
        move(6, j, other, far, ty=partner).wait_recv()

    spots = [jnp.where(owner_ref[first_for(tx)] % 2 == i, 0, 1) for i in range(2)]
    line = lax.broadcasted_iota(jnp.int32, (16, quarter), 0)
    column = lax.broadcasted_iota(jnp.int32, (16, quarter), 1)
    hot = [
        ((line == p) & (column == lives[p] - 1 - ty * quarter)).astype(jnp.bfloat16)
        for p in range(per_grp)
    ]
    chosen = (dot32(hot[0], heard[0]) + dot32(hot[1], heard[1])).astype(jnp.bfloat16)
    for i in range(2):
        model = pl.ds(pl.multiple_of(tx * half + i * block, block), block)
        base = dot32(hot[0], xs[ty, 0, :, model]) + dot32(hot[1], xs[ty, 1, :, model])
        value = (base + dot32(chosen, wos[spots[i]])).astype(jnp.bfloat16)
        picked_ref[:, i * block : (i + 1) * block] = value.astype(jnp.float32)[:per_grp]

    strip = 256

    def out_step(n, _):
        for i in range(2):

            @pl.when(n // 2 == i)
            def _():
                inside = pl.ds(pl.multiple_of((n % 2) * strip, strip), strip)
                cols = pl.ds(pl.multiple_of(n * strip, strip), strip)
                model = pl.ds(pl.multiple_of(tx * half + n * strip, strip), strip)
                for p in range(per_grp):
                    total = dot32(heard[p], wos[spots[i], :, inside])
                    hidden_ref[p, :, cols] = (
                        xs[ty, p, :, model].astype(jnp.float32) + total
                    ).astype(jnp.bfloat16)

        return 0

    peers = groups * tx_size
    place = dp * tx_size + tx

    def along_ty(k, slot):
        return remote(
            picked_ref, seen.at[slot], t_send.at[k], t_recv.at[k], ty=(ty + k) % ty_size
        )

    for k in range(1, ty_size):
        along_ty(k, ty).start()
    lax.fori_loop(0, 2, out_step, 0)
    merged = picked_ref[...]
    for k in range(1, ty_size):
        slot = (ty + ty_size - k) % ty_size
        along_ty(k, slot).wait_recv()
        merged = merged + seen[slot]
    full[place] = merged

    def along_peers(k, slot):
        peer = (place + k) % peers
        return remote(
            full.at[place], full.at[slot], r_send.at[k], r_recv.at[k],
            dp=peer // tx_size, tx=peer % tx_size,
        )

    for k in range(1, peers):
        along_peers(k, place).start()
    lax.fori_loop(2, 4, out_step, 0)
    for k in range(1, peers):
        along_peers(k, (place + peers - k) % peers).wait_recv()
    for g in range(groups):
        for t in range(tx_size):
            rows_ref[g * per_grp : (g + 1) * per_grp, t * half : (t + 1) * half] = full[
                g * tx_size + t
            ]
    final = normalize(rows_ref[...], fgain_ref[...])
    owner = owner_ref[dp]
    mine = jnp.zeros((groups * per_grp, block), jnp.float32)
    for g in range(groups):
        mine = jnp.where(owner == g, final[:, g * block : (g + 1) * block], mine)
    mine = mine.astype(jnp.bfloat16)

    def logit_step(k, _):
        cols = pl.ds(pl.multiple_of(k * slab, slab), slab)
        logits = dot32(mine, table[:, cols])
        for g in range(groups):
            part[g, :, cols] = logits[g * per_grp : (g + 1) * per_grp]
        return 0

    parts = 2
    share_words = words // parts

    def along_dp(n, k, slot):
        peer = (dp + k) % groups
        cols = pl.ds(n * share_words, share_words)
        return remote(
            part.at[peer, :, cols], incoming.at[slot, :, cols], l_send.at[n, k], l_recv.at[n, k],
            dp=peer,
        )

    for n in range(parts):
        lax.fori_loop(n * count // parts, (n + 1) * count // parts, logit_step, 0)
        for k in range(1, groups):
            along_dp(n, k, dp).start()
    for n in range(parts):
        cols = slice(n * share_words, (n + 1) * share_words)
        total = part[dp, :, cols]
        for k in range(1, groups):
            slot = (dp + groups - k) % groups
            along_dp(n, k, slot).wait_recv()
            total = total + incoming[slot, :, cols]
        out_ref[:, cols] = total

    for k in range(chunks):
        crossing(k, ty).wait_send()
        sideways(k, tx).wait_send()
        inward(k, 0, across, tx).wait_send()
        inward(k, 1, across, other).wait_send()
    own_rows(ty).wait_send()
    for step in range(steps):
        for which in range(5):
            for way in range(2):
                copy, runs = hop(which, way, step)
                pl.when(runs)(copy.wait_send)
    for g in range(groups):
        for n in range(7):
            share(n, g).wait_send()
    for head in range(heads):
        for p in range(per_grp):
            own_passed(head, p, ty).wait_send()
            for k in range(1, ty_size):
                slot = (ty + k) % ty_size
                heads_of(head, p, slot, ty).wait_send()
                passed(head, p, slot, tx).wait_send()
    for j in range(2):
        move(0, j, tx, ty, give.at[j], tx=other).wait_send()
        move(1, j, tx, ty, ty=across).wait_send()
        move(2, j, tx, ty, ty=partner).wait_send()
        move(3, j, other, ty, ty=across).wait_send()
        move(4, j, other, ty, ty=partner).wait_send()
        move(5, j, tx, across, ty=partner).wait_send()
        move(6, j, other, across, ty=partner).wait_send()
    for k in range(1, ty_size):
        along_ty(k, ty).wait_send()
    for k in range(1, peers):
        along_peers(k, place).wait_send()
    for n in range(parts):
        for k in range(1, groups):
            along_dp(n, k, dp).wait_send()


def layer(groups, owner, lengths, deal, x, again, lgain, fgain, wq, wa, wb, wo, vocab):
    per_grp, quarter, width = x.shape
    block, words = vocab.shape
    half = width // 2
    piece = 2 * NOPE
    slab = 512
    steps = groups - 1
    peers = 2 * groups
    position = np.arange(LEN, dtype=np.float32)
    frequency = np.power(
        np.float32(10000.0), -np.arange(ROPE // 2, dtype=np.float32) / np.float32(ROPE // 2)
    ).astype(np.float32)
    angles = (position[:, None] * frequency).astype(np.float32).astype(np.float64)
    cosine, sine = np.cos(angles), np.sin(angles)
    cosine = jnp.asarray(np.concatenate([cosine] * 4, axis=1).astype(np.float32))
    sine = jnp.asarray(np.concatenate([-sine, sine, -sine, sine], axis=1).astype(np.float32))
    dma = pltpu.SemaphoreType.DMA
    vmem = pl.BlockSpec(memory_space=pltpu.VMEM)
    smem = pl.BlockSpec(memory_space=pltpu.SMEM)
    hbm = pl.BlockSpec(memory_space=pl.ANY)
    bf16 = lambda *dims: pltpu.VMEM(dims, jnp.bfloat16)
    f32 = lambda *dims: pltpu.VMEM(dims, jnp.float32)
    return pl.pallas_call(
        functools.partial(layer_kernel, groups),
        in_specs=[smem, smem, smem, hbm, vmem, vmem, vmem, vmem, vmem, hbm, hbm, hbm, hbm, hbm],
        out_specs=[vmem, vmem],
        out_shape=[
            jax.ShapeDtypeStruct((per_grp, quarter, half), jnp.bfloat16),
            jax.ShapeDtypeStruct((per_grp, words), jnp.float32),
        ],
        scratch_shapes=[
            bf16(4, per_grp, quarter, width),
            bf16(groups, per_grp * LEN, block),
            bf16(groups, block, QCOLS + ACOLS),
            bf16(groups, LATENT // groups, 2 * piece),
            bf16(LATENT, 2 * piece),
            bf16(groups, piece, block),
            bf16(2, piece, block),
            bf16(2, 8 * piece, block),
            f32(per_grp * LEN, QCOLS + ACOLS),
            bf16(per_grp, 2, LEN, 2 * NOPE),
            bf16(per_grp, 2, LEN, NOPE),
            bf16(2, 4, per_grp, TILE, NOPE),
            bf16(per_grp, TILE, 8 * piece),
            bf16(block, words),
            f32(2, block, slab),
            f32(*wq.shape),
            f32(wa.shape[1], block // 4),
            f32(*wb.shape),
            f32(block, piece),
            f32(4, per_grp, half),
            f32(peers, per_grp, half),
            f32(groups * per_grp, width),
            f32(groups, per_grp, words),
            f32(groups, per_grp, words),
            f32(per_grp, half),
            dma((5,)), dma((2,)),
            dma((4,)), dma((4,)), dma((4,)), dma((4,)), dma((2, 4)), dma((2, 4)), dma((1,)),
            dma((1,)),
            dma((2, 5, steps)), dma((2, 5, steps)), dma((7, groups)), dma((7, groups)),
            dma((2, per_grp, 4)), dma((2, per_grp, 4)), dma((2, per_grp, 4)),
            dma((2, per_grp, 4)), dma((7, 2)), dma((7, 2)),
            dma((4,)), dma((4,)), dma((peers,)), dma((peers,)), dma((2, groups)),
            dma((2, groups)),
        ],
        compiler_params=pltpu.CompilerParams(
            collective_id=0, has_side_effects=True, vmem_limit_bytes=60 * 1024 * 1024
        ),
        cost_estimate=pl.CostEstimate(
            flops=16_000_000_000, bytes_accessed=24_000_000, transcendentals=3_000_000
        ),
    )(owner, lengths, deal, x, again, lgain, fgain, cosine, sine, wq, wa.T, wb, wo, vocab)


def load_vocab(vocab_chunk, vocab_ref, table, v_sem):
    loads = []
    for k in range(vocab_ref.shape[1] // vocab_chunk):
        cols = pl.ds(k * vocab_chunk, vocab_chunk)
        loads.append(
            pltpu.make_async_copy(vocab_ref.at[:, cols], table.at[:, cols], v_sem.at[k])
        )
        loads[-1].start()
    return loads


def next_token(
    groups, tx_size, ty_size, vocab_chunk, loads, owner_ref, picked_ref, gain_ref, out_ref, seen, full,
    rows_ref, table, part, incoming, t_send, t_recv, r_send, r_recv, l_send, l_recv,
):
    dp, tx, ty = lax.axis_index("dp"), lax.axis_index("tx"), lax.axis_index("ty")
    per_grp, half = picked_ref.shape
    block = table.shape[0]
    peers = groups * tx_size
    place = dp * tx_size + tx
    count = len(loads)

    def along_ty(k, slot):
        return remote(
            picked_ref, seen.at[slot], t_send.at[k], t_recv.at[k], ty=(ty + k) % ty_size
        )

    for k in range(1, ty_size):
        along_ty(k, ty).start()
    merged = picked_ref[...]
    for k in range(1, ty_size):
        slot = (ty + ty_size - k) % ty_size
        along_ty(k, slot).wait_recv()
        merged = merged + seen[slot]
    full[place] = merged

    def along_peers(k, slot):
        peer = (place + k) % peers
        return remote(
            full.at[place], full.at[slot], r_send.at[k], r_recv.at[k],
            dp=peer // tx_size, tx=peer % tx_size,
        )

    for k in range(1, peers):
        along_peers(k, place).start()
    for k in range(1, peers):
        along_peers(k, (place + peers - k) % peers).wait_recv()
    for g in range(groups):
        for t in range(tx_size):
            rows_ref[g * per_grp : (g + 1) * per_grp, t * half : (t + 1) * half] = full[
                g * tx_size + t
            ]
    final = normalize(rows_ref[...], gain_ref[...])
    owner = owner_ref[dp]
    mine = jnp.zeros((groups * per_grp, block), jnp.float32)
    for g in range(groups):
        mine = jnp.where(owner == g, final[:, g * block : (g + 1) * block], mine)
    mine = mine.astype(jnp.bfloat16)
    for k in range(count):
        loads[k].wait()
        cols = slice(k * vocab_chunk, (k + 1) * vocab_chunk)
        logits = dot32(mine, table[:, cols].astype(jnp.bfloat16))
        for g in range(groups):
            part[g, :, cols] = logits[g * per_grp : (g + 1) * per_grp]

    def along_dp(k, slot):
        peer = (dp + k) % groups
        return remote(part.at[peer], incoming.at[slot], l_send.at[k], l_recv.at[k], dp=peer)

    for k in range(1, groups):
        along_dp(k, dp).start()
    total = part[dp]
    for k in range(1, groups):
        slot = (dp + groups - k) % groups
        along_dp(k, slot).wait_recv()
        total = total + incoming[slot]
    out_ref[...] = total
    for k in range(1, ty_size):
        along_ty(k, ty).wait_send()
    for k in range(1, peers):
        along_peers(k, place).wait_send()
    for k in range(1, groups):
        along_dp(k, dp).wait_send()


def tail_kernel(
    groups, tx_size, ty_size, vocab_chunk, owner_ref, picked_ref, gain_ref, vocab_ref, out_ref,
    seen, full, rows_ref, table, part, incoming, t_send, t_recv, r_send, r_recv, l_send, l_recv,
    v_sem,
):
    dp, tx, ty = lax.axis_index("dp"), lax.axis_index("tx"), lax.axis_index("ty")
    peers = groups * tx_size
    place = dp * tx_size + tx
    loads = load_vocab(vocab_chunk, vocab_ref, table, v_sem)
    for k in range(1, ty_size):
        greet(ty=(ty + k) % ty_size)
    for k in range(1, peers):
        peer = (place + k) % peers
        greet(dp=peer // tx_size, tx=peer % tx_size)
    pl.semaphore_wait(pltpu.get_barrier_semaphore(), ty_size + peers - 2)
    next_token(
        groups, tx_size, ty_size, vocab_chunk, loads, owner_ref, picked_ref, gain_ref, out_ref,
        seen, full, rows_ref, table, part, incoming, t_send, t_recv, r_send, r_recv, l_send,
        l_recv,
    )


def tail(groups, tx_size, ty_size, owner, picked, gain, vocab):
    per_grp, half = picked.shape
    block, words = vocab.shape
    vocab_chunk = 512
    peers = groups * tx_size
    dma = pltpu.SemaphoreType.DMA
    vmem = pl.BlockSpec(memory_space=pltpu.VMEM)
    return pl.pallas_call(
        functools.partial(tail_kernel, groups, tx_size, ty_size, vocab_chunk),
        in_specs=[
            pl.BlockSpec(memory_space=pltpu.SMEM), vmem, vmem, pl.BlockSpec(memory_space=pl.ANY),
        ],
        out_specs=vmem,
        out_shape=jax.ShapeDtypeStruct((per_grp, words), jnp.float32),
        scratch_shapes=[
            pltpu.VMEM((ty_size, per_grp, half), jnp.float32),
            pltpu.VMEM((peers, per_grp, half), jnp.float32),
            pltpu.VMEM((groups * per_grp, half * tx_size), jnp.float32),
            pltpu.VMEM((block, words), jnp.float32),
            pltpu.VMEM((groups, per_grp, words), jnp.float32),
            pltpu.VMEM((groups, per_grp, words), jnp.float32),
            dma((ty_size,)), dma((ty_size,)), dma((peers,)), dma((peers,)),
            dma((groups,)), dma((groups,)), dma((words // vocab_chunk,)),
        ],
        compiler_params=pltpu.CompilerParams(
            collective_id=1, has_side_effects=True, vmem_limit_bytes=40 * 1024 * 1024
        ),
        cost_estimate=pl.CostEstimate(
            flops=100_000_000, bytes_accessed=16_000_000, transcendentals=0
        ),
    )(owner, picked, gain, vocab)


def rotate_half(values, position):
    half_dim = values.shape[-1] // 2
    frequency = 10000.0 ** (-jnp.arange(half_dim, dtype=jnp.float32) / half_dim)
    angles = position.astype(jnp.float32)[..., None] * frequency
    cosine = jnp.cos(angles)
    sine = jnp.sin(angles)
    first_half = values[..., :half_dim]
    second_half = values[..., half_dim:]
    return jnp.concatenate(
        [first_half * cosine - second_half * sine, first_half * sine + second_half * cosine],
        axis=-1,
    )


def split_positions(
    inputs, inverse, live_len, attn_gain, latent_gain, w_query, w_down_kv, w_up_kv, w_out
):
    groups = lax.axis_size("dp")

    def arrange(gathered):
        block_rows = gathered.shape[0] // groups
        return jnp.concatenate(
            [
                lax.dynamic_slice_in_dim(gathered, inverse[g] * block_rows, block_rows, 0)
                for g in range(groups)
            ],
            axis=0,
        )

    query_w, down_w, up_w, out_w = (
        lax.all_gather(w_query.astype(jnp.bfloat16), "dp", axis=0, tiled=True),
        lax.all_gather(w_down_kv.astype(jnp.bfloat16), "dp", axis=0, tiled=True),
        lax.all_gather(w_up_kv.astype(jnp.bfloat16), "dp", axis=0, tiled=True),
        lax.all_gather(w_out.astype(jnp.bfloat16), "dp", axis=0, tiled=True),
    )
    query_w = arrange(query_w)
    down_w = arrange(down_w)
    up_w = arrange(up_w)
    out_w = arrange(out_w)
    query_w, up_w = (
        lax.all_gather(query_w, "ty", axis=1, tiled=True),
        lax.all_gather(up_w, "ty", axis=1, tiled=True),
    )
    per_grp, quarter, width = inputs.shape
    heads = query_w.shape[1] // (NOPE + ROPE)
    position = lax.axis_index("ty") * quarter + jnp.arange(quarter, dtype=jnp.int32)
    flat_rows = inputs.reshape(per_grp * quarter, width)
    normed = normalize(flat_rows, attn_gain).astype(jnp.bfloat16)
    queries = jnp.dot(normed, query_w, preferred_element_type=jnp.float32).reshape(
        per_grp, quarter, heads, NOPE + ROPE
    )
    queries = jnp.concatenate(
        [queries[..., :NOPE], rotate_half(queries[..., NOPE:], position[None, :, None])], axis=-1
    ).astype(jnp.bfloat16)
    down_proj = jnp.dot(normed, down_w, preferred_element_type=jnp.float32).reshape(
        per_grp, quarter, LATENT + ROPE
    )
    latent = normalize(down_proj[..., :LATENT], latent_gain).astype(jnp.bfloat16)
    key_rope = rotate_half(down_proj[..., LATENT:], position[None, :]).astype(jnp.bfloat16)
    gathered = lax.all_gather(
        jnp.concatenate([latent, key_rope], axis=-1), "ty", axis=1, tiled=True
    )
    key_val = jnp.dot(gathered[..., :LATENT], up_w, preferred_element_type=jnp.float32).astype(
        jnp.bfloat16
    )
    rope_all = gathered[..., LATENT:]
    key_val = key_val.reshape(per_grp, LEN, heads, 2, NOPE)
    key_nope = key_val[:, :, :, 0]
    values = key_val[:, :, :, 1]
    score_scale = (NOPE + ROPE) ** (-0.5)
    scores = (
        jnp.einsum(
            "pqhd,pkhd->phqk", queries[..., :NOPE], key_nope, preferred_element_type=jnp.float32
        )
        + jnp.einsum(
            "pqhd,pkd->phqk", queries[..., NOPE:], rope_all, preferred_element_type=jnp.float32
        )
    ) * score_scale
    key_pos = jnp.arange(LEN, dtype=jnp.int32)
    allowed = (key_pos[None, None, :] <= position[None, :, None]) & (
        key_pos[None, None, :] < live_len[:, None, None]
    )
    scores = jnp.where(allowed[:, None], scores, -1e30)
    top = jnp.max(scores, axis=-1, keepdims=True)
    expo = jnp.exp(scores - top)
    softmax_w = (expo / jnp.sum(expo, axis=-1, keepdims=True)).astype(jnp.bfloat16)
    attended = jnp.einsum(
        "phqk,pkhd->pqhd", softmax_w, values, preferred_element_type=jnp.float32
    ).astype(jnp.bfloat16)
    attended = attended.reshape(per_grp * quarter, heads * NOPE)
    own_width = width // lax.axis_size("tx")
    col_start = lax.axis_index("tx") * own_width
    partial_value = lax.dot_general(
        attended, out_w, (((1,), (1,)), ((), ())), preferred_element_type=jnp.float32
    ).reshape(per_grp, quarter, width)
    summed = lax.psum_scatter(partial_value, "tx", scatter_dimension=2, tiled=True)
    residual = lax.dynamic_slice_in_dim(inputs, col_start, own_width, 2)
    layer_out = (residual.astype(jnp.float32) + summed).astype(jnp.bfloat16)
    return layer_out


def shards(
    inputs,
    lengths,
    prompt_deal,
    block_owner,
    attn_gain,
    latent_gain,
    final_gain,
    w_query,
    w_down_kv,
    w_up_kv,
    w_out,
    w_vocab,
):
    groups = lax.axis_size("dp")
    dp, tx, ty = lax.axis_index("dp"), lax.axis_index("tx"), lax.axis_index("ty")
    per_grp, quarter, width = inputs.shape
    half = width // lax.axis_size("tx")
    whole_heads = w_query.shape[1] == QCOLS and w_up_kv.shape[1] == 4 * NOPE
    here = whole_heads and (lax.axis_size("tx"), lax.axis_size("ty"), per_grp) == (2, 4, 2)
    if here and groups == 4 and (quarter, width) == (TILE, 4 * w_query.shape[0]):
        return tuple(
            layer(
                groups, block_owner, lengths, prompt_deal, inputs, attn_gain[None],
                latent_gain[None], final_gain[None], w_query, w_down_kv, w_up_kv, w_out, w_vocab,
            )
        )

    order = jnp.arange(groups, dtype=jnp.int32)
    inverse = jnp.sum(
        jnp.where(block_owner[None, :] == order[:, None], order[None, :], 0), axis=1
    ).astype(jnp.int32)
    slots = dp * per_grp + jnp.arange(per_grp, dtype=jnp.int32)
    names = jnp.arange(lengths.shape[0], dtype=jnp.int32)

    def at_index(values, index):
        return jnp.sum(jnp.where(names[None] == index[:, None], values[None], 0), axis=1)

    live_len = at_index(lengths, at_index(prompt_deal, slots))
    layer_out = split_positions(
        inputs, inverse, live_len, attn_gain, latent_gain, w_query, w_down_kv, w_up_kv, w_out
    )

    at = live_len - 1 - ty * quarter
    picked = jnp.stack(
        [
            lax.dynamic_slice(
                layer_out, (i, jnp.clip(at[i], 0, quarter - 1), 0), (1, 1, half)
            ).reshape(half)
            for i in range(per_grp)
        ]
    ).astype(jnp.float32)
    inside = (at >= 0) & (at < quarter)
    picked = jnp.where(inside[:, None], picked, 0.0)
    logits = tail(
        groups, lax.axis_size("tx"), lax.axis_size("ty"), block_owner, picked, final_gain[None],
        w_vocab,
    )
    return (layer_out, logits)


def solution(mesh):
    placed = (
        P("dp", "ty", None),
        P(),
        P(),
        P(),
        P(),
        P(),
        P(),
        P("dp", ("tx", "ty")),
        P("dp", None),
        P("dp", ("tx", "ty")),
        P("dp", "tx"),
        P("dp", ("tx", "ty")),
    )
    return jax.shard_map(
        shards,
        mesh=mesh,
        in_specs=placed,
        out_specs=(P("dp", "ty", "tx"), P("dp", ("tx", "ty"))),
        check_vma=False,
    )
```

```python
import functools

import jax
import jax.numpy as jnp
import numpy as np
from jax import lax
from jax.experimental import pallas as pl
from jax.experimental.pallas import tpu as pltpu
from jax.sharding import PartitionSpec as P

NOPE = 128
ROPE = 64
LATENT = 512
LEN = 1024
TILE = 256
EPS = 1e-06
QCOLS = 384
ACOLS = 640


def normalize(values, gain):
    wide = values.astype(jnp.float32)
    return wide * lax.rsqrt(jnp.mean(wide * wide, axis=-1, keepdims=True) + EPS) * gain


def dot32(left, right):
    return jnp.dot(left, right, preferred_element_type=jnp.float32)


def remote(src, dst, send, recv, **where):
    return pltpu.make_async_remote_copy(
        src_ref=src,
        dst_ref=dst,
        send_sem=send,
        recv_sem=recv,
        device_id=where,
        device_id_type=pl.DeviceIdType.MESH,
    )


def greet(**where):
    pl.semaphore_signal(
        pltpu.get_barrier_semaphore(),
        inc=1,
        device_id=where,
        device_id_type=pl.DeviceIdType.MESH,
    )


def layer_kernel(
    groups, owner_ref, lengths_ref, deal_ref, x_ref, again_ref, lgain_ref, fgain_ref, cos_ref,
    sin_ref, wq_ref, wa_ref, wb_ref, wo_ref, vocab_ref, hidden_ref, out_ref,
    xs, h, wcat, wbs, wbl, woz, give, wos, acc, k_ref, v_ref, o_ref, heard, table, stage,
    wq_f, wa_f, wb_f, wo_f, seen, full, rows_ref, part, incoming, picked_ref,
    local, v_sem, x_send, x_recv, y_send, y_recv, p_send, p_recv, b_send, b_recv,
    z_send, z_recv, a_send, a_recv, o_send, o_recv, f_send, f_recv, w_send, w_recv,
    t_send, t_recv, r_send, r_recv, l_send, l_recv,
):
    dp, tx, ty = lax.axis_index("dp"), lax.axis_index("tx"), lax.axis_index("ty")
    tx_size, ty_size = 2, 4
    per_grp = 2
    core = ty % 2
    partner = ty + 1 - 2 * core
    across = (ty + 2) % 4
    far = (partner + 2) % 4
    other = 1 - tx
    spot = tx * ty_size + ty
    plane = tx_size * ty_size
    steps = groups - 1
    chunks = 2
    quarter, width = x_ref.shape[1], x_ref.shape[2]
    half = width // tx_size
    block = width // groups
    rows = quarter // (2 * chunks)
    words = vocab_ref.shape[1]
    slab = stage.shape[-1]
    count = words // slab
    piece = 2 * NOPE
    heads = 2

    loads = [
        pltpu.make_async_copy(wa_ref.at[:, pl.ds(pl.multiple_of((spot // 2) * 128, 128), 128)], wa_f, local.at[0]),
        pltpu.make_async_copy(wb_ref, wb_f, local.at[1]),
        pltpu.make_async_copy(wq_ref, wq_f, local.at[2]),
        pltpu.make_async_copy(
            wo_ref.at[:, pl.ds(pl.multiple_of(ty * piece, piece), piece)], wo_f, local.at[3]
        ),
        pltpu.make_async_copy(x_ref, xs.at[ty], local.at[4]),
    ]
    for load in loads:
        load.start()

    def vocab_load(k, slot):
        cols = pl.ds(pl.multiple_of(k * slab, slab), slab)
        return pltpu.make_async_copy(vocab_ref.at[:, cols], stage.at[slot], v_sem.at[slot])

    vocab_load(0, 0).start()

    for k in range(1, plane):
        peer = (spot + k) % plane
        greet(tx=peer // ty_size, ty=peer % ty_size)
    for k in range(1, groups):
        for t in range(tx_size):
            greet(dp=(dp + k) % groups, tx=t)
    pl.semaphore_wait(pltpu.get_barrier_semaphore(), plane - 1 + (groups - 1) * tx_size)

    def cut(slot, p, side, k):
        at = pl.multiple_of(side * (quarter // 2) + k * rows, rows)
        return xs.at[slot, p, pl.ds(at, rows)]

    def crossing(p, k, slot, side):
        at = pl.multiple_of(side * (quarter // 2) + k * rows, rows)
        src = x_ref.at[p, pl.ds(at, rows)]
        return remote(src, cut(slot, p, side, k), x_send.at[p, k], x_recv.at[p, k], ty=across)

    def sideways(p, k, side):
        ref = cut(across, p, side, k)
        return remote(ref, ref, y_send.at[p, k], y_recv.at[p, k], tx=other)

    def inward(p, k, n, slot, side):
        ref = cut(slot, p, side, k)
        return remote(ref, ref, p_send.at[n, p, k], p_recv.at[n, p, k], ty=partner)

    def own_rows(p, slot):
        return remote(x_ref.at[p], xs.at[slot, p], b_send.at[p], b_recv.at[p], ty=partner)

    def cross_step(p, k):
        crossing(p, k, across, tx).wait_recv()
        sideways(p, k, tx).start()
        inward(p, k, 0, across, tx).start()

    def side_step(p, k):
        sideways(p, k, other).wait_recv()
        inward(p, k, 1, across, other).start()

    def far_wait(p):
        for k in range(chunks):
            inward(p, k, 0, far, tx).wait_recv()
            inward(p, k, 1, far, other).wait_recv()

    A, B, Q, R, O = range(5)
    arows = block // plane

    def a_part(g, q):
        return wcat.at[g, pl.ds(pl.multiple_of(q * arows, arows), arows), pl.ds(QCOLS, ACOLS)]

    slots = [
        lambda g: a_part(g, spot),
        lambda g: wbs.at[g],
        lambda g: wcat.at[g, :, pl.ds(NOPE, QCOLS - NOPE)],
        lambda g: wcat.at[g, :, pl.ds(0, NOPE)],
        lambda g: woz.at[g],
    ]

    def hop(which, way, step):
        sign = 1 - 2 * way
        g = dp - sign * step
        runs = (g >= 0) & (g < groups) & (dp + sign >= 0) & (dp + sign < groups)
        ref = slots[which](g)
        copy = remote(
            ref, ref, z_send.at[way, which, step], z_recv.at[way, which, step], dp=dp + sign
        )
        return copy, runs

    def arrival(which, way, step):
        sign = 1 - 2 * way
        g = dp - sign * (step + 1)
        ref = slots[which](g)
        copy = remote(
            ref, ref, z_send.at[way, which, step], z_recv.at[way, which, step], dp=dp
        )
        return copy, (g >= 0) & (g < groups)

    inner = (dp > 0) & (dp < groups - 1)

    def start_hop(which):
        for way in range(2):
            copy, runs = hop(which, way, 0)
            pl.when(runs)(copy.start)

    def forward(which, step):
        for way in range(2):
            copy, comes = arrival(which, way, step)
            onward = hop(which, way, step + 1)[0]

            @pl.when(comes & inner)
            def _():
                copy.wait_recv()
                onward.start()

    def take(which, step):
        for way in range(2):
            copy, comes = arrival(which, way, step)
            pl.when(comes & jnp.logical_not(inner))(copy.wait_recv)

    def both(which, step):
        forward(which, step)
        take(which, step)

    def share(n, g):
        diagonal = core == 0
        q = [
            spot, spot, spot, jnp.where(diagonal, tx * ty_size + across, other * ty_size + ty),
            tx * ty_size + across, other * ty_size + ty, other * ty_size + across,
        ][n]
        where = [
            dict(ty=across), dict(tx=other), dict(ty=partner),
            dict(tx=jnp.where(diagonal, other, tx), ty=jnp.where(diagonal, ty, across)),
            dict(ty=partner), dict(ty=partner), dict(ty=partner),
        ][n]
        ref = a_part(g, q)
        return remote(ref, ref, a_send.at[n, g], a_recv.at[n, g], **where)

    def shared(n, g):
        q = [
            tx * ty_size + across, other * ty_size + ty, tx * ty_size + partner,
            other * ty_size + across, tx * ty_size + far, other * ty_size + partner,
            other * ty_size + far,
        ][n]
        ref = a_part(g, q)
        return remote(ref, ref, a_send.at[n, g], a_recv.at[n, g], ty=partner)

    def share_first(g):
        for n in (0, 1, 2):
            share(n, g).start()

    def share_second(g):
        shared(0, g).wait_recv()
        shared(1, g).wait_recv()
        for n in (3, 4, 5):
            share(n, g).start()

    def share_third(g):
        shared(3, g).wait_recv()
        share(6, g).start()

    def share_wait(g):
        for n in (2, 4, 5, 6):
            shared(n, g).wait_recv()

    def arrived(step, act):
        for way in range(2):
            g = dp - (1 - 2 * way) * (step + 1)

            @pl.when((g >= 0) & (g < groups))
            def _():
                act(g)

    for k in range(chunks):
        crossing(0, k, ty, tx).start()
    own_rows(0, ty).start()

    loads[0].wait()
    turned_a = wa_f[...].T
    wide_a = jnp.where(spot % 2 == 0, turned_a[:arows], turned_a[arows:]).astype(jnp.bfloat16)
    here = pl.ds(pl.multiple_of(spot * arows, arows), arows)
    wcat[dp, here, QCOLS : QCOLS + LATENT] = wide_a[:, :LATENT]
    twice = (
        lax.broadcasted_iota(jnp.int32, (ROPE, 2 * ROPE), 0)
        == lax.broadcasted_iota(jnp.int32, (ROPE, 2 * ROPE), 1) % ROPE
    ).astype(jnp.bfloat16)
    wcat[dp, here, QCOLS + LATENT :] = dot32(wide_a[:, LATENT:], twice).astype(jnp.bfloat16)
    start_hop(A)
    loads[1].wait()
    wbs[dp] = wb_f[...].astype(jnp.bfloat16)
    start_hop(B)
    loads[2].wait()
    turned_q = pltpu.roll(wq_f[:, NOPE:], 2 * NOPE - ROPE, 1)
    wcat[dp, :, 2 * NOPE : QCOLS] = turned_q[:, NOPE:].astype(jnp.bfloat16)
    wcat[dp, :, NOPE : 2 * NOPE] = wq_f[:, :NOPE].astype(jnp.bfloat16)
    start_hop(Q)
    wcat[dp, :, 0:NOPE] = turned_q[:, :NOPE].astype(jnp.bfloat16)
    share_first(dp)
    loads[3].wait()
    woz[dp] = wo_f[...].T.astype(jnp.bfloat16)

    def vocab_step(k, _):
        slot = k % 2

        @pl.when(k + 1 < count)
        def _():
            vocab_load(k + 1, 1 - slot).start()

        vocab_load(k, slot).wait()
        cols = pl.ds(pl.multiple_of(k * slab, slab), slab)
        table[:, cols] = stage[slot].astype(jnp.bfloat16)
        return 0

    part_rows = 32

    def norm(slot, prompt):
        def body(i, _):
            at = pl.multiple_of(i * part_rows, part_rows)
            value = normalize(xs[slot, prompt, pl.ds(at, part_rows)], again_ref[...])
            value = value.astype(jnp.bfloat16)
            to = pl.multiple_of(prompt * LEN + slot * quarter + at, part_rows)
            for b in range(groups):
                h[b, pl.ds(to, part_rows)] = value[:, b * block : (b + 1) * block]
            return 0

        lax.fori_loop(0, quarter // part_rows, body, 0)

    span_rows = 512

    def project(g, first):
        own = owner_ref[g]

        def body(i, _):
            at = pl.ds(pl.multiple_of(i * span_rows, span_rows), span_rows)
            term = dot32(h[own, at], wcat[g, :, NOPE:])
            acc[at, NOPE:] = term if first else acc[at, NOPE:] + term
            return 0

        lax.fori_loop(0, LEN // span_rows, body, 0)

    def project_step(step):
        def one(way, _):
            g = dp - (1 - 2 * way) * (step + 1)

            @pl.when((g >= 0) & (g < groups))
            def _():
                share_wait(g)
                project(g, False)

            return 0

        lax.fori_loop(0, 2, one, 0)

    def project_all(p, low, high):
        def body(i, _):
            at = pl.ds(pl.multiple_of(p * LEN + i * span_rows, span_rows), span_rows)
            total = dot32(h[owner_ref[0], at], wcat[0, :, low:high])
            for g in range(1, groups):
                total = total + dot32(h[owner_ref[g], at], wcat[g, :, low:high])
            acc[at, low:high] = total
            return 0

        lax.fori_loop(0, LEN // span_rows, body, 0)

    lax.fori_loop(0, 7, vocab_step, 0)
    both(A, 0)
    arrived(0, share_first)
    crossing(1, 0, ty, tx).start()
    own_rows(1, ty).start()
    loads[4].wait()
    norm(ty, 0)
    both(B, 0)
    cross_step(0, 0)
    own_rows(0, partner).wait_recv()
    norm(partner, 0)
    cross_step(0, 1)
    lax.fori_loop(7, count, vocab_step, 0)
    both(Q, 0)
    both(A, 1)
    arrived(1, share_first)
    crossing(1, 1, ty, tx).start()
    norm(ty, 1)
    side_step(0, 0)
    both(B, 1)
    side_step(0, 1)
    norm(across, 0)
    share_second(dp)
    arrived(0, share_second)
    far_wait(0)
    norm(far, 0)
    both(Q, 1)
    start_hop(R)
    share_third(dp)
    arrived(0, share_third)
    cross_step(1, 0)
    share_wait(dp)
    project(dp, True)
    take(A, 2)
    arrived(2, share_first)
    arrived(1, share_second)
    side_step(1, 0)
    project_step(0)
    forward(R, 0)
    start_hop(O)
    arrived(1, share_third)
    cross_step(1, 1)
    own_rows(1, partner).wait_recv()
    norm(partner, 1)
    project_step(1)
    forward(R, 1)
    arrived(2, share_second)
    side_step(1, 1)
    arrived(2, share_third)

    def stored(b):
        place = jnp.int32(0)
        for g in range(groups):
            place = jnp.where(owner_ref[g] == b, g, place)
        return place

    brows = LATENT // groups

    lane = lax.broadcasted_iota(jnp.int32, (TILE, 2 * ROPE), 1)

    def rotate(values, at):
        swapped = jnp.where(
            lane % ROPE < ROPE // 2,
            pltpu.roll(values, 2 * ROPE - ROPE // 2, 1),
            pltpu.roll(values, ROPE // 2, 1),
        )
        return values * cos_ref[at] + swapped * sin_ref[at]

    factor = (NOPE + ROPE) ** (-0.5) * 1.4426950408889634
    lives = [lengths_ref[deal_ref[dp * per_grp + p]] for p in range(per_grp)]

    def keys(p, tile, _):
        down = acc[pl.ds(pl.multiple_of(p * LEN + tile * TILE, TILE), TILE), QCOLS:]
        to = pl.ds(pl.multiple_of(tile * TILE, TILE), TILE)
        latent = normalize(down[:, :LATENT], lgain_ref[...]).astype(jnp.bfloat16)
        key_rope = rotate(down[:, LATENT:], to).astype(jnp.bfloat16)
        key_val = dot32(latent, wbl[...]).astype(jnp.bfloat16)
        for head in range(heads):
            k_ref[p, head, to, :NOPE] = key_val[:, 2 * head * NOPE : (2 * head + 1) * NOPE]
            k_ref[p, head, to, NOPE:] = key_rope
            v_ref[p, head, to] = key_val[:, (2 * head + 1) * NOPE : (2 * head + 2) * NOPE]
        return 0


    def hears(p, slot, head):
        cols = pl.ds(pl.multiple_of(slot * piece + head * NOPE, NOPE), NOPE)
        return heard.at[p, :, cols]

    def heads_of(head, p, tile, slot):
        return remote(
            o_ref.at[head, tile, p], hears(p, tx * ty_size + slot, head),
            o_send.at[head, p, tile], o_recv.at[head, p, slot], ty=tile,
        )

    def passed(head, p, slot, slot_tx, source=None):
        ref = hears(p, slot_tx * ty_size + slot, head)
        return remote(
            ref if source is None else source, ref,
            f_send.at[head, p, slot], f_recv.at[head, p, slot], tx=other,
        )

    def own_passed(head, p, tile):
        return passed(head, p, ty, tx, o_ref.at[head, tile, p])

    def relay(head, p):
        for k in range(1, ty_size):
            slot = (ty + k) % ty_size
            heads_of(head, p, ty, slot).wait_recv()
            passed(head, p, slot, tx).start()

    tile_order = (3, 1, 2, 0)

    def attention(head, p):
        live = jnp.where(p == 0, lives[0], lives[1])
        nope_at = (1 - head) * NOPE
        for t in tile_order:
            span = (t + 1) * TILE
            at = pl.ds(pl.multiple_of(p * LEN + t * TILE, TILE), TILE)
            turned = rotate(acc[at, 2 * NOPE : QCOLS], pl.ds(t * TILE, TILE))
            i = lax.broadcasted_iota(jnp.int32, (TILE, span), 0) + t * TILE
            j = lax.broadcasted_iota(jnp.int32, (TILE, span), 1)
            allowed = j <= jnp.minimum(i, live - 1)
            mine = jnp.where(lane // ROPE == 1 - head, turned, 0.0)
            query = jnp.concatenate([acc[at, nope_at : nope_at + NOPE], mine], axis=1)
            score = lax.dot_general(
                query.astype(jnp.bfloat16), k_ref[p, head, :span], (((1,), (1,)), ((), ())),
                preferred_element_type=jnp.float32,
            )
            score = jnp.where(allowed, score, -1e30)
            expo = jnp.exp2((score - jnp.max(score, axis=-1, keepdims=True)) * factor)
            prob = expo * (1.0 / jnp.sum(expo, axis=-1, keepdims=True))
            out = dot32(prob.astype(jnp.bfloat16), v_ref[p, head, :span]).astype(jnp.bfloat16)
            o_ref[head, t, p] = out

            @pl.when(ty == t)
            def _():
                mine_at = pl.multiple_of(spot * piece + head * NOPE, NOPE)
                heard[p, :, pl.ds(mine_at, NOPE)] = out
                own_passed(head, p, t).start()

            @pl.when(ty != t)
            def _():
                heads_of(head, p, t, ty).start()

    def wide(j, slot_tx, slot_ty):
        slot = slot_tx * ty_size + slot_ty
        return wos.at[j, pl.ds(pl.multiple_of(slot * piece, piece), piece)]

    def move(n, j, slot_tx, slot_ty, source=None, **where):
        ref = wide(j, slot_tx, slot_ty)
        return remote(
            ref if source is None else source, ref, w_send.at[n, j], w_recv.at[n, j], **where
        )

    early = [jnp.where(dp < groups // 2, k, groups - 1 - k) for k in range(steps)]
    late = jnp.where(dp < groups // 2, groups - 1, 0)

    def aim(g):
        return owner_ref[g] // (groups // tx_size)

    def first_for(side):
        found = early[-1]
        for g in early[-2::-1]:
            found = jnp.where(aim(g) == side, g, found)
        return found

    def first_rows(side):
        found = woz[early[-1]]
        for g in early[-2::-1]:
            found = jnp.where(aim(g) == side, woz[g], found)
        return found

    def second_for(side):
        found = late
        for g in early:
            found = jnp.where((aim(g) == side) & (g != first_for(side)), g, found)
        return found

    mine_at = pl.ds(pl.multiple_of(spot * piece, piece), piece)

    def spread(j, give_rows, keep_rows):
        give[j] = give_rows
        move(0, j, tx, ty, give.at[j], tx=other).start()
        wos[j, mine_at] = keep_rows
        move(1, j, tx, ty, ty=across).start()
        move(2, j, tx, ty, ty=partner).start()

    def spread_on(j):
        move(0, j, other, ty, tx=other).wait_recv()
        move(3, j, other, ty, ty=across).start()
        move(4, j, other, ty, ty=partner).start()

    def spread_in(j):
        move(1, j, tx, across, ty=across).wait_recv()
        move(5, j, tx, across, ty=partner).start()

    def spread_last(j):
        move(3, j, other, across, ty=across).wait_recv()
        move(6, j, other, across, ty=partner).start()

    def prompt_step(p, _):
        @pl.when(p == 0)
        def _():
            take(B, 2)
            take(Q, 2)
            project_step(2)
            for b in range(groups):
                wbl[b * brows : (b + 1) * brows] = wbs[stored(b)]

        @pl.when(p == 1)
        def _():
            norm(across, 1)
            far_wait(1)
            norm(far, 1)
            relay(1, 0)
            project_all(1, 0, QCOLS + ACOLS)

        lax.fori_loop(0, LEN // TILE, functools.partial(keys, p), 0)
        attention(0, p)

        @pl.when(p == 0)
        def _():
            forward(O, 0)
            for step in range(steps):
                take(R, step)
            project_all(0, 0, NOPE)

        @pl.when(p == 1)
        def _():
            take(O, 0)
            take(O, 1)
            spread(0, first_rows(other), first_rows(tx))

        relay(0, p)
        attention(1, p)
        pl.when(p == 0)(lambda: forward(O, 1))
        return 0

    lax.fori_loop(0, per_grp, prompt_step, 0)
    take(O, 2)
    spread(1, woz[second_for(other)], woz[second_for(tx)])
    relay(1, 1)
    for j in range(2):
        spread_on(j)
        spread_in(j)
    for j in range(2):
        spread_last(j)
    for head in range(heads):
        for p in range(per_grp):
            for k in range(ty_size):
                passed(head, p, (ty + k) % ty_size, other).wait_recv()
    for j in range(2):
        move(2, j, tx, partner, ty=partner).wait_recv()
        move(4, j, other, partner, ty=partner).wait_recv()
        move(5, j, tx, far, ty=partner).wait_recv()
        move(6, j, other, far, ty=partner).wait_recv()

    spots = [jnp.where(owner_ref[first_for(tx)] % 2 == i, 0, 1) for i in range(2)]
    line = lax.broadcasted_iota(jnp.int32, (16, quarter), 0)
    column = lax.broadcasted_iota(jnp.int32, (16, quarter), 1)
    hot = [
        ((line == p) & (column == lives[p] - 1 - ty * quarter)).astype(jnp.bfloat16)
        for p in range(per_grp)
    ]
    chosen = (dot32(hot[0], heard[0]) + dot32(hot[1], heard[1])).astype(jnp.bfloat16)
    for i in range(2):
        model = pl.ds(pl.multiple_of(tx * half + i * block, block), block)
        base = dot32(hot[0], xs[ty, 0, :, model]) + dot32(hot[1], xs[ty, 1, :, model])
        value = (base + dot32(chosen, wos[spots[i]])).astype(jnp.bfloat16)
        picked_ref[:, i * block : (i + 1) * block] = value.astype(jnp.float32)[:per_grp]

    strip = 256

    def out_step(n, _):
        for i in range(2):

            @pl.when(n // 2 == i)
            def _():
                inside = pl.ds(pl.multiple_of((n % 2) * strip, strip), strip)
                cols = pl.ds(pl.multiple_of(n * strip, strip), strip)
                model = pl.ds(pl.multiple_of(tx * half + n * strip, strip), strip)
                for p in range(per_grp):
                    total = dot32(heard[p], wos[spots[i], :, inside])
                    hidden_ref[p, :, cols] = (
                        xs[ty, p, :, model].astype(jnp.float32) + total
                    ).astype(jnp.bfloat16)

        return 0

    peers = groups * tx_size
    place = dp * tx_size + tx

    def along_ty(k, slot):
        return remote(
            picked_ref, seen.at[slot], t_send.at[k], t_recv.at[k], ty=(ty + k) % ty_size
        )

    for k in range(1, ty_size):
        along_ty(k, ty).start()
    lax.fori_loop(0, 2, out_step, 0)
    merged = picked_ref[...]
    for k in range(1, ty_size):
        slot = (ty + ty_size - k) % ty_size
        along_ty(k, slot).wait_recv()
        merged = merged + seen[slot]
    full[place] = merged

    def along_peers(k, slot):
        peer = (place + k) % peers
        return remote(
            full.at[place], full.at[slot], r_send.at[k], r_recv.at[k],
            dp=peer // tx_size, tx=peer % tx_size,
        )

    for k in range(1, peers):
        along_peers(k, place).start()
    lax.fori_loop(2, 4, out_step, 0)
    for k in range(1, peers):
        along_peers(k, (place + peers - k) % peers).wait_recv()
    for g in range(groups):
        for t in range(tx_size):
            rows_ref[g * per_grp : (g + 1) * per_grp, t * half : (t + 1) * half] = full[
                g * tx_size + t
            ]
    final = normalize(rows_ref[...], fgain_ref[...])
    owner = owner_ref[dp]
    mine = jnp.zeros((groups * per_grp, block), jnp.float32)
    for g in range(groups):
        mine = jnp.where(owner == g, final[:, g * block : (g + 1) * block], mine)
    mine = mine.astype(jnp.bfloat16)

    def logit_step(k, _):
        cols = pl.ds(pl.multiple_of(k * slab, slab), slab)
        logits = dot32(mine, table[:, cols])
        for g in range(groups):
            part[g, :, cols] = logits[g * per_grp : (g + 1) * per_grp]
        return 0

    parts = 2
    share_words = words // parts

    def along_dp(n, k, slot):
        peer = (dp + k) % groups
        cols = pl.ds(n * share_words, share_words)
        return remote(
            part.at[peer, :, cols], incoming.at[slot, :, cols], l_send.at[n, k], l_recv.at[n, k],
            dp=peer,
        )

    for n in range(parts):
        lax.fori_loop(n * count // parts, (n + 1) * count // parts, logit_step, 0)
        for k in range(1, groups):
            along_dp(n, k, dp).start()
    for n in range(parts):
        cols = slice(n * share_words, (n + 1) * share_words)
        total = part[dp, :, cols]
        for k in range(1, groups):
            slot = (dp + groups - k) % groups
            along_dp(n, k, slot).wait_recv()
            total = total + incoming[slot, :, cols]
        out_ref[:, cols] = total

    for p in range(per_grp):
        for k in range(chunks):
            crossing(p, k, ty, tx).wait_send()
            sideways(p, k, tx).wait_send()
            inward(p, k, 0, across, tx).wait_send()
            inward(p, k, 1, across, other).wait_send()
        own_rows(p, ty).wait_send()
    for step in range(steps):
        for which in range(5):
            for way in range(2):
                copy, runs = hop(which, way, step)
                pl.when(runs)(copy.wait_send)
    for g in range(groups):
        for n in range(7):
            share(n, g).wait_send()
    for head in range(heads):
        for p in range(per_grp):
            own_passed(head, p, ty).wait_send()
            for k in range(1, ty_size):
                slot = (ty + k) % ty_size
                heads_of(head, p, slot, ty).wait_send()
                passed(head, p, slot, tx).wait_send()
    for j in range(2):
        move(0, j, tx, ty, give.at[j], tx=other).wait_send()
        move(1, j, tx, ty, ty=across).wait_send()
        move(2, j, tx, ty, ty=partner).wait_send()
        move(3, j, other, ty, ty=across).wait_send()
        move(4, j, other, ty, ty=partner).wait_send()
        move(5, j, tx, across, ty=partner).wait_send()
        move(6, j, other, across, ty=partner).wait_send()
    for k in range(1, ty_size):
        along_ty(k, ty).wait_send()
    for k in range(1, peers):
        along_peers(k, place).wait_send()
    for n in range(parts):
        for k in range(1, groups):
            along_dp(n, k, dp).wait_send()


def layer(groups, owner, lengths, deal, x, again, lgain, fgain, wq, wa, wb, wo, vocab):
    per_grp, quarter, width = x.shape
    block, words = vocab.shape
    half = width // 2
    piece = 2 * NOPE
    slab = 512
    steps = groups - 1
    peers = 2 * groups
    position = np.arange(LEN, dtype=np.float32)
    frequency = np.power(
        np.float32(10000.0), -np.arange(ROPE // 2, dtype=np.float32) / np.float32(ROPE // 2)
    ).astype(np.float32)
    angles = (position[:, None] * frequency).astype(np.float32).astype(np.float64)
    cosine, sine = np.cos(angles), np.sin(angles)
    cosine = jnp.asarray(np.concatenate([cosine] * 4, axis=1).astype(np.float32))
    sine = jnp.asarray(np.concatenate([-sine, sine, -sine, sine], axis=1).astype(np.float32))
    dma = pltpu.SemaphoreType.DMA
    vmem = pl.BlockSpec(memory_space=pltpu.VMEM)
    smem = pl.BlockSpec(memory_space=pltpu.SMEM)
    hbm = pl.BlockSpec(memory_space=pl.ANY)
    bf16 = lambda *dims: pltpu.VMEM(dims, jnp.bfloat16)
    f32 = lambda *dims: pltpu.VMEM(dims, jnp.float32)
    return pl.pallas_call(
        functools.partial(layer_kernel, groups),
        in_specs=[smem, smem, smem, hbm, vmem, vmem, vmem, vmem, vmem, hbm, hbm, hbm, hbm, hbm],
        out_specs=[vmem, vmem],
        out_shape=[
            jax.ShapeDtypeStruct((per_grp, quarter, half), jnp.bfloat16),
            jax.ShapeDtypeStruct((per_grp, words), jnp.float32),
        ],
        scratch_shapes=[
            bf16(4, per_grp, quarter, width),
            bf16(groups, per_grp * LEN, block),
            bf16(groups, block, QCOLS + ACOLS),
            bf16(groups, LATENT // groups, 2 * piece),
            bf16(LATENT, 2 * piece),
            bf16(groups, piece, block),
            bf16(2, piece, block),
            bf16(2, 8 * piece, block),
            f32(per_grp * LEN, QCOLS + ACOLS),
            bf16(per_grp, 2, LEN, 2 * NOPE),
            bf16(per_grp, 2, LEN, NOPE),
            bf16(2, 4, per_grp, TILE, NOPE),
            bf16(per_grp, TILE, 8 * piece),
            bf16(block, words),
            f32(2, block, slab),
            f32(*wq.shape),
            f32(wa.shape[1], block // 4),
            f32(*wb.shape),
            f32(block, piece),
            f32(4, per_grp, half),
            f32(peers, per_grp, half),
            f32(groups * per_grp, width),
            f32(groups, per_grp, words),
            f32(groups, per_grp, words),
            f32(per_grp, half),
            dma((5,)), dma((2,)),
            dma((per_grp, 2)), dma((per_grp, 2)), dma((per_grp, 2)), dma((per_grp, 2)),
            dma((2, per_grp, 2)), dma((2, per_grp, 2)), dma((per_grp,)), dma((per_grp,)),
            dma((2, 5, steps)), dma((2, 5, steps)), dma((7, groups)), dma((7, groups)),
            dma((2, per_grp, 4)), dma((2, per_grp, 4)), dma((2, per_grp, 4)),
            dma((2, per_grp, 4)), dma((7, 2)), dma((7, 2)),
            dma((4,)), dma((4,)), dma((peers,)), dma((peers,)), dma((2, groups)),
            dma((2, groups)),
        ],
        compiler_params=pltpu.CompilerParams(
            collective_id=0, has_side_effects=True, vmem_limit_bytes=60 * 1024 * 1024
        ),
        cost_estimate=pl.CostEstimate(
            flops=16_000_000_000, bytes_accessed=24_000_000, transcendentals=3_000_000
        ),
    )(owner, lengths, deal, x, again, lgain, fgain, cosine, sine, wq, wa.T, wb, wo, vocab)


def load_vocab(vocab_chunk, vocab_ref, table, v_sem):
    loads = []
    for k in range(vocab_ref.shape[1] // vocab_chunk):
        cols = pl.ds(k * vocab_chunk, vocab_chunk)
        loads.append(
            pltpu.make_async_copy(vocab_ref.at[:, cols], table.at[:, cols], v_sem.at[k])
        )
        loads[-1].start()
    return loads


def next_token(
    groups, tx_size, ty_size, vocab_chunk, loads, owner_ref, picked_ref, gain_ref, out_ref, seen, full,
    rows_ref, table, part, incoming, t_send, t_recv, r_send, r_recv, l_send, l_recv,
):
    dp, tx, ty = lax.axis_index("dp"), lax.axis_index("tx"), lax.axis_index("ty")
    per_grp, half = picked_ref.shape
    block = table.shape[0]
    peers = groups * tx_size
    place = dp * tx_size + tx
    count = len(loads)

    def along_ty(k, slot):
        return remote(
            picked_ref, seen.at[slot], t_send.at[k], t_recv.at[k], ty=(ty + k) % ty_size
        )

    for k in range(1, ty_size):
        along_ty(k, ty).start()
    merged = picked_ref[...]
    for k in range(1, ty_size):
        slot = (ty + ty_size - k) % ty_size
        along_ty(k, slot).wait_recv()
        merged = merged + seen[slot]
    full[place] = merged

    def along_peers(k, slot):
        peer = (place + k) % peers
        return remote(
            full.at[place], full.at[slot], r_send.at[k], r_recv.at[k],
            dp=peer // tx_size, tx=peer % tx_size,
        )

    for k in range(1, peers):
        along_peers(k, place).start()
    for k in range(1, peers):
        along_peers(k, (place + peers - k) % peers).wait_recv()
    for g in range(groups):
        for t in range(tx_size):
            rows_ref[g * per_grp : (g + 1) * per_grp, t * half : (t + 1) * half] = full[
                g * tx_size + t
            ]
    final = normalize(rows_ref[...], gain_ref[...])
    owner = owner_ref[dp]
    mine = jnp.zeros((groups * per_grp, block), jnp.float32)
    for g in range(groups):
        mine = jnp.where(owner == g, final[:, g * block : (g + 1) * block], mine)
    mine = mine.astype(jnp.bfloat16)
    for k in range(count):
        loads[k].wait()
        cols = slice(k * vocab_chunk, (k + 1) * vocab_chunk)
        logits = dot32(mine, table[:, cols].astype(jnp.bfloat16))
        for g in range(groups):
            part[g, :, cols] = logits[g * per_grp : (g + 1) * per_grp]

    def along_dp(k, slot):
        peer = (dp + k) % groups
        return remote(part.at[peer], incoming.at[slot], l_send.at[k], l_recv.at[k], dp=peer)

    for k in range(1, groups):
        along_dp(k, dp).start()
    total = part[dp]
    for k in range(1, groups):
        slot = (dp + groups - k) % groups
        along_dp(k, slot).wait_recv()
        total = total + incoming[slot]
    out_ref[...] = total
    for k in range(1, ty_size):
        along_ty(k, ty).wait_send()
    for k in range(1, peers):
        along_peers(k, place).wait_send()
    for k in range(1, groups):
        along_dp(k, dp).wait_send()


def tail_kernel(
    groups, tx_size, ty_size, vocab_chunk, owner_ref, picked_ref, gain_ref, vocab_ref, out_ref,
    seen, full, rows_ref, table, part, incoming, t_send, t_recv, r_send, r_recv, l_send, l_recv,
    v_sem,
):
    dp, tx, ty = lax.axis_index("dp"), lax.axis_index("tx"), lax.axis_index("ty")
    peers = groups * tx_size
    place = dp * tx_size + tx
    loads = load_vocab(vocab_chunk, vocab_ref, table, v_sem)
    for k in range(1, ty_size):
        greet(ty=(ty + k) % ty_size)
    for k in range(1, peers):
        peer = (place + k) % peers
        greet(dp=peer // tx_size, tx=peer % tx_size)
    pl.semaphore_wait(pltpu.get_barrier_semaphore(), ty_size + peers - 2)
    next_token(
        groups, tx_size, ty_size, vocab_chunk, loads, owner_ref, picked_ref, gain_ref, out_ref,
        seen, full, rows_ref, table, part, incoming, t_send, t_recv, r_send, r_recv, l_send,
        l_recv,
    )


def tail(groups, tx_size, ty_size, owner, picked, gain, vocab):
    per_grp, half = picked.shape
    block, words = vocab.shape
    vocab_chunk = 512
    peers = groups * tx_size
    dma = pltpu.SemaphoreType.DMA
    vmem = pl.BlockSpec(memory_space=pltpu.VMEM)
    return pl.pallas_call(
        functools.partial(tail_kernel, groups, tx_size, ty_size, vocab_chunk),
        in_specs=[
            pl.BlockSpec(memory_space=pltpu.SMEM), vmem, vmem, pl.BlockSpec(memory_space=pl.ANY),
        ],
        out_specs=vmem,
        out_shape=jax.ShapeDtypeStruct((per_grp, words), jnp.float32),
        scratch_shapes=[
            pltpu.VMEM((ty_size, per_grp, half), jnp.float32),
            pltpu.VMEM((peers, per_grp, half), jnp.float32),
            pltpu.VMEM((groups * per_grp, half * tx_size), jnp.float32),
            pltpu.VMEM((block, words), jnp.float32),
            pltpu.VMEM((groups, per_grp, words), jnp.float32),
            pltpu.VMEM((groups, per_grp, words), jnp.float32),
            dma((ty_size,)), dma((ty_size,)), dma((peers,)), dma((peers,)),
            dma((groups,)), dma((groups,)), dma((words // vocab_chunk,)),
        ],
        compiler_params=pltpu.CompilerParams(
            collective_id=1, has_side_effects=True, vmem_limit_bytes=40 * 1024 * 1024
        ),
        cost_estimate=pl.CostEstimate(
            flops=100_000_000, bytes_accessed=16_000_000, transcendentals=0
        ),
    )(owner, picked, gain, vocab)


def rotate_half(values, position):
    half_dim = values.shape[-1] // 2
    frequency = 10000.0 ** (-jnp.arange(half_dim, dtype=jnp.float32) / half_dim)
    angles = position.astype(jnp.float32)[..., None] * frequency
    cosine = jnp.cos(angles)
    sine = jnp.sin(angles)
    first_half = values[..., :half_dim]
    second_half = values[..., half_dim:]
    return jnp.concatenate(
        [first_half * cosine - second_half * sine, first_half * sine + second_half * cosine],
        axis=-1,
    )


def split_positions(
    inputs, inverse, live_len, attn_gain, latent_gain, w_query, w_down_kv, w_up_kv, w_out
):
    groups = lax.axis_size("dp")

    def arrange(gathered):
        block_rows = gathered.shape[0] // groups
        return jnp.concatenate(
            [
                lax.dynamic_slice_in_dim(gathered, inverse[g] * block_rows, block_rows, 0)
                for g in range(groups)
            ],
            axis=0,
        )

    query_w, down_w, up_w, out_w = (
        lax.all_gather(w_query.astype(jnp.bfloat16), "dp", axis=0, tiled=True),
        lax.all_gather(w_down_kv.astype(jnp.bfloat16), "dp", axis=0, tiled=True),
        lax.all_gather(w_up_kv.astype(jnp.bfloat16), "dp", axis=0, tiled=True),
        lax.all_gather(w_out.astype(jnp.bfloat16), "dp", axis=0, tiled=True),
    )
    query_w = arrange(query_w)
    down_w = arrange(down_w)
    up_w = arrange(up_w)
    out_w = arrange(out_w)
    query_w, up_w = (
        lax.all_gather(query_w, "ty", axis=1, tiled=True),
        lax.all_gather(up_w, "ty", axis=1, tiled=True),
    )
    per_grp, quarter, width = inputs.shape
    heads = query_w.shape[1] // (NOPE + ROPE)
    position = lax.axis_index("ty") * quarter + jnp.arange(quarter, dtype=jnp.int32)
    flat_rows = inputs.reshape(per_grp * quarter, width)
    normed = normalize(flat_rows, attn_gain).astype(jnp.bfloat16)
    queries = jnp.dot(normed, query_w, preferred_element_type=jnp.float32).reshape(
        per_grp, quarter, heads, NOPE + ROPE
    )
    queries = jnp.concatenate(
        [queries[..., :NOPE], rotate_half(queries[..., NOPE:], position[None, :, None])], axis=-1
    ).astype(jnp.bfloat16)
    down_proj = jnp.dot(normed, down_w, preferred_element_type=jnp.float32).reshape(
        per_grp, quarter, LATENT + ROPE
    )
    latent = normalize(down_proj[..., :LATENT], latent_gain).astype(jnp.bfloat16)
    key_rope = rotate_half(down_proj[..., LATENT:], position[None, :]).astype(jnp.bfloat16)
    gathered = lax.all_gather(
        jnp.concatenate([latent, key_rope], axis=-1), "ty", axis=1, tiled=True
    )
    key_val = jnp.dot(gathered[..., :LATENT], up_w, preferred_element_type=jnp.float32).astype(
        jnp.bfloat16
    )
    rope_all = gathered[..., LATENT:]
    key_val = key_val.reshape(per_grp, LEN, heads, 2, NOPE)
    key_nope = key_val[:, :, :, 0]
    values = key_val[:, :, :, 1]
    score_scale = (NOPE + ROPE) ** (-0.5)
    scores = (
        jnp.einsum(
            "pqhd,pkhd->phqk", queries[..., :NOPE], key_nope, preferred_element_type=jnp.float32
        )
        + jnp.einsum(
            "pqhd,pkd->phqk", queries[..., NOPE:], rope_all, preferred_element_type=jnp.float32
        )
    ) * score_scale
    key_pos = jnp.arange(LEN, dtype=jnp.int32)
    allowed = (key_pos[None, None, :] <= position[None, :, None]) & (
        key_pos[None, None, :] < live_len[:, None, None]
    )
    scores = jnp.where(allowed[:, None], scores, -1e30)
    top = jnp.max(scores, axis=-1, keepdims=True)
    expo = jnp.exp(scores - top)
    softmax_w = (expo / jnp.sum(expo, axis=-1, keepdims=True)).astype(jnp.bfloat16)
    attended = jnp.einsum(
        "phqk,pkhd->pqhd", softmax_w, values, preferred_element_type=jnp.float32
    ).astype(jnp.bfloat16)
    attended = attended.reshape(per_grp * quarter, heads * NOPE)
    own_width = width // lax.axis_size("tx")
    col_start = lax.axis_index("tx") * own_width
    partial_value = lax.dot_general(
        attended, out_w, (((1,), (1,)), ((), ())), preferred_element_type=jnp.float32
    ).reshape(per_grp, quarter, width)
    summed = lax.psum_scatter(partial_value, "tx", scatter_dimension=2, tiled=True)
    residual = lax.dynamic_slice_in_dim(inputs, col_start, own_width, 2)
    layer_out = (residual.astype(jnp.float32) + summed).astype(jnp.bfloat16)
    return layer_out


def shards(
    inputs,
    lengths,
    prompt_deal,
    block_owner,
    attn_gain,
    latent_gain,
    final_gain,
    w_query,
    w_down_kv,
    w_up_kv,
    w_out,
    w_vocab,
):
    groups = lax.axis_size("dp")
    dp, tx, ty = lax.axis_index("dp"), lax.axis_index("tx"), lax.axis_index("ty")
    per_grp, quarter, width = inputs.shape
    half = width // lax.axis_size("tx")
    whole_heads = w_query.shape[1] == QCOLS and w_up_kv.shape[1] == 4 * NOPE
    here = whole_heads and (lax.axis_size("tx"), lax.axis_size("ty"), per_grp) == (2, 4, 2)
    if here and groups == 4 and (quarter, width) == (TILE, 4 * w_query.shape[0]):
        return tuple(
            layer(
                groups, block_owner, lengths, prompt_deal, inputs, attn_gain[None],
                latent_gain[None], final_gain[None], w_query, w_down_kv, w_up_kv, w_out, w_vocab,
            )
        )

    order = jnp.arange(groups, dtype=jnp.int32)
    inverse = jnp.sum(
        jnp.where(block_owner[None, :] == order[:, None], order[None, :], 0), axis=1
    ).astype(jnp.int32)
    slots = dp * per_grp + jnp.arange(per_grp, dtype=jnp.int32)
    names = jnp.arange(lengths.shape[0], dtype=jnp.int32)

    def at_index(values, index):
        return jnp.sum(jnp.where(names[None] == index[:, None], values[None], 0), axis=1)

    live_len = at_index(lengths, at_index(prompt_deal, slots))
    layer_out = split_positions(
        inputs, inverse, live_len, attn_gain, latent_gain, w_query, w_down_kv, w_up_kv, w_out
    )

    at = live_len - 1 - ty * quarter
    picked = jnp.stack(
        [
            lax.dynamic_slice(
                layer_out, (i, jnp.clip(at[i], 0, quarter - 1), 0), (1, 1, half)
            ).reshape(half)
            for i in range(per_grp)
        ]
    ).astype(jnp.float32)
    inside = (at >= 0) & (at < quarter)
    picked = jnp.where(inside[:, None], picked, 0.0)
    logits = tail(
        groups, lax.axis_size("tx"), lax.axis_size("ty"), block_owner, picked, final_gain[None],
        w_vocab,
    )
    return (layer_out, logits)


def solution(mesh):
    placed = (
        P("dp", "ty", None),
        P(),
        P(),
        P(),
        P(),
        P(),
        P(),
        P("dp", ("tx", "ty")),
        P("dp", None),
        P("dp", ("tx", "ty")),
        P("dp", "tx"),
        P("dp", ("tx", "ty")),
    )
    return jax.shard_map(
        shards,
        mesh=mesh,
        in_specs=placed,
        out_specs=(P("dp", "ty", "tx"), P("dp", ("tx", "ty"))),
        check_vma=False,
    )
```

```python
import functools

import jax
import jax.numpy as jnp
import numpy as np
from jax import lax
from jax.experimental import pallas as pl
from jax.experimental.pallas import tpu as pltpu
from jax.sharding import PartitionSpec as P

NOPE = 128
ROPE = 64
LATENT = 512
LEN = 1024
TILE = 256
EPS = 1e-06
QCOLS = 384
ACOLS = 640


def normalize(values, gain):
    wide = values.astype(jnp.float32)
    return wide * lax.rsqrt(jnp.mean(wide * wide, axis=-1, keepdims=True) + EPS) * gain


def dot32(left, right):
    return jnp.dot(left, right, preferred_element_type=jnp.float32)


def remote(src, dst, send, recv, **where):
    return pltpu.make_async_remote_copy(
        src_ref=src,
        dst_ref=dst,
        send_sem=send,
        recv_sem=recv,
        device_id=where,
        device_id_type=pl.DeviceIdType.MESH,
    )


def greet(**where):
    pl.semaphore_signal(
        pltpu.get_barrier_semaphore(),
        inc=1,
        device_id=where,
        device_id_type=pl.DeviceIdType.MESH,
    )


def layer_kernel(
    groups, owner_ref, lengths_ref, deal_ref, x_ref, again_ref, lgain_ref, fgain_ref, cos_ref,
    sin_ref, wq_ref, wa_ref, wb_ref, wo_ref, vocab_ref, hidden_ref, out_ref,
    xs, h, wcat, wbs, wbl, woz, give, wos, acc, k_ref, v_ref, o_ref, heard, table, stage,
    wq_f, wa_f, wb_f, wo_f, ends_ref, base_ref, line_ref, full, rows_ref, part, incoming,
    local, v_sem, x_send, x_recv, y_send, y_recv, p_send, p_recv, b_send, b_recv,
    z_send, z_recv, a_send, a_recv, o_send, o_recv, f_send, f_recv, w_send, w_recv,
    e_send, e_recv, r_send, r_recv, l_send, l_recv,
):
    dp, tx, ty = lax.axis_index("dp"), lax.axis_index("tx"), lax.axis_index("ty")
    tx_size, ty_size = 2, 4
    per_grp = 2
    core = ty % 2
    partner = ty + 1 - 2 * core
    across = (ty + 2) % 4
    far = (partner + 2) % 4
    other = 1 - tx
    spot = tx * ty_size + ty
    plane = tx_size * ty_size
    steps = groups - 1
    chunks = 2
    quarter, width = x_ref.shape[1], x_ref.shape[2]
    half = width // tx_size
    block = width // groups
    rows = quarter // (2 * chunks)
    words = vocab_ref.shape[1]
    slab = stage.shape[-1]
    count = words // slab
    piece = 2 * NOPE
    heads = 2

    loads = [
        pltpu.make_async_copy(wa_ref.at[:, pl.ds(pl.multiple_of((spot // 2) * 128, 128), 128)], wa_f, local.at[0]),
        pltpu.make_async_copy(wb_ref, wb_f, local.at[1]),
        pltpu.make_async_copy(wq_ref, wq_f, local.at[2]),
        pltpu.make_async_copy(
            wo_ref.at[:, pl.ds(pl.multiple_of(ty * piece, piece), piece)], wo_f, local.at[3]
        ),
        pltpu.make_async_copy(x_ref, xs.at[ty], local.at[4]),
    ]
    for load in loads:
        load.start()

    def vocab_load(k, slot):
        cols = pl.ds(pl.multiple_of(k * slab, slab), slab)
        return pltpu.make_async_copy(vocab_ref.at[:, cols], stage.at[slot], v_sem.at[slot])

    vocab_load(0, 0).start()

    for k in range(1, plane):
        peer = (spot + k) % plane
        greet(tx=peer // ty_size, ty=peer % ty_size)
    for k in range(1, groups):
        for t in range(tx_size):
            greet(dp=(dp + k) % groups, tx=t)
    pl.semaphore_wait(pltpu.get_barrier_semaphore(), plane - 1 + (groups - 1) * tx_size)

    def cut(slot, p, side, k):
        at = pl.multiple_of(side * (quarter // 2) + k * rows, rows)
        return xs.at[slot, p, pl.ds(at, rows)]

    def crossing(p, k, slot, side):
        at = pl.multiple_of(side * (quarter // 2) + k * rows, rows)
        src = x_ref.at[p, pl.ds(at, rows)]
        return remote(src, cut(slot, p, side, k), x_send.at[p, k], x_recv.at[p, k], ty=across)

    def sideways(p, k, side):
        ref = cut(across, p, side, k)
        return remote(ref, ref, y_send.at[p, k], y_recv.at[p, k], tx=other)

    def inward(p, k, n, slot, side):
        ref = cut(slot, p, side, k)
        return remote(ref, ref, p_send.at[n, p, k], p_recv.at[n, p, k], ty=partner)

    def own_rows(p, slot):
        return remote(x_ref.at[p], xs.at[slot, p], b_send.at[p], b_recv.at[p], ty=partner)

    def cross_step(p, k):
        crossing(p, k, across, tx).wait_recv()
        sideways(p, k, tx).start()
        inward(p, k, 0, across, tx).start()

    def side_step(p, k):
        sideways(p, k, other).wait_recv()
        inward(p, k, 1, across, other).start()

    def far_wait(p):
        for k in range(chunks):
            inward(p, k, 0, far, tx).wait_recv()
            inward(p, k, 1, far, other).wait_recv()

    A, B, Q, R, O = range(5)
    arows = block // plane

    def a_part(g, q):
        return wcat.at[g, pl.ds(pl.multiple_of(q * arows, arows), arows), pl.ds(QCOLS, ACOLS)]

    slots = [
        lambda g: a_part(g, spot),
        lambda g: wbs.at[g],
        lambda g: wcat.at[g, :, pl.ds(NOPE, QCOLS - NOPE)],
        lambda g: wcat.at[g, :, pl.ds(0, NOPE)],
        lambda g: woz.at[g],
    ]

    def hop(which, way, step):
        sign = 1 - 2 * way
        g = dp - sign * step
        runs = (g >= 0) & (g < groups) & (dp + sign >= 0) & (dp + sign < groups)
        ref = slots[which](g)
        copy = remote(
            ref, ref, z_send.at[way, which, step], z_recv.at[way, which, step], dp=dp + sign
        )
        return copy, runs

    def arrival(which, way, step):
        sign = 1 - 2 * way
        g = dp - sign * (step + 1)
        ref = slots[which](g)
        copy = remote(
            ref, ref, z_send.at[way, which, step], z_recv.at[way, which, step], dp=dp
        )
        return copy, (g >= 0) & (g < groups)

    inner = (dp > 0) & (dp < groups - 1)

    def start_hop(which):
        for way in range(2):
            copy, runs = hop(which, way, 0)
            pl.when(runs)(copy.start)

    def forward(which, step):
        for way in range(2):
            copy, comes = arrival(which, way, step)
            onward = hop(which, way, step + 1)[0]

            @pl.when(comes & inner)
            def _():
                copy.wait_recv()
                onward.start()

    def take(which, step):
        for way in range(2):
            copy, comes = arrival(which, way, step)
            pl.when(comes & jnp.logical_not(inner))(copy.wait_recv)

    def both(which, step):
        forward(which, step)
        take(which, step)

    def share(n, g):
        diagonal = core == 0
        q = [
            spot, spot, spot, jnp.where(diagonal, tx * ty_size + across, other * ty_size + ty),
            tx * ty_size + across, other * ty_size + ty, other * ty_size + across,
        ][n]
        where = [
            dict(ty=across), dict(tx=other), dict(ty=partner),
            dict(tx=jnp.where(diagonal, other, tx), ty=jnp.where(diagonal, ty, across)),
            dict(ty=partner), dict(ty=partner), dict(ty=partner),
        ][n]
        ref = a_part(g, q)
        return remote(ref, ref, a_send.at[n, g], a_recv.at[n, g], **where)

    def shared(n, g):
        q = [
            tx * ty_size + across, other * ty_size + ty, tx * ty_size + partner,
            other * ty_size + across, tx * ty_size + far, other * ty_size + partner,
            other * ty_size + far,
        ][n]
        ref = a_part(g, q)
        return remote(ref, ref, a_send.at[n, g], a_recv.at[n, g], ty=partner)

    def share_first(g):
        for n in (0, 1, 2):
            share(n, g).start()

    def share_second(g):
        shared(0, g).wait_recv()
        shared(1, g).wait_recv()
        for n in (3, 4, 5):
            share(n, g).start()

    def share_third(g):
        shared(3, g).wait_recv()
        share(6, g).start()

    def share_wait(g):
        for n in (2, 4, 5, 6):
            shared(n, g).wait_recv()

    def arrived(step, act):
        for way in range(2):
            g = dp - (1 - 2 * way) * (step + 1)

            @pl.when((g >= 0) & (g < groups))
            def _():
                act(g)

    for k in range(chunks):
        crossing(0, k, ty, tx).start()
    own_rows(0, ty).start()

    loads[0].wait()
    turned_a = wa_f[...].T
    wide_a = jnp.where(spot % 2 == 0, turned_a[:arows], turned_a[arows:]).astype(jnp.bfloat16)
    here = pl.ds(pl.multiple_of(spot * arows, arows), arows)
    wcat[dp, here, QCOLS : QCOLS + LATENT] = wide_a[:, :LATENT]
    twice = (
        lax.broadcasted_iota(jnp.int32, (ROPE, 2 * ROPE), 0)
        == lax.broadcasted_iota(jnp.int32, (ROPE, 2 * ROPE), 1) % ROPE
    ).astype(jnp.bfloat16)
    wcat[dp, here, QCOLS + LATENT :] = dot32(wide_a[:, LATENT:], twice).astype(jnp.bfloat16)
    start_hop(A)
    loads[1].wait()
    wbs[dp] = wb_f[...].astype(jnp.bfloat16)
    start_hop(B)
    loads[2].wait()
    turned_q = pltpu.roll(wq_f[:, NOPE:], 2 * NOPE - ROPE, 1)
    wcat[dp, :, 2 * NOPE : QCOLS] = turned_q[:, NOPE:].astype(jnp.bfloat16)
    wcat[dp, :, NOPE : 2 * NOPE] = wq_f[:, :NOPE].astype(jnp.bfloat16)
    start_hop(Q)
    wcat[dp, :, 0:NOPE] = turned_q[:, :NOPE].astype(jnp.bfloat16)
    share_first(dp)
    loads[3].wait()
    woz[dp] = wo_f[...].T.astype(jnp.bfloat16)

    def vocab_step(k, _):
        slot = k % 2

        @pl.when(k + 1 < count)
        def _():
            vocab_load(k + 1, 1 - slot).start()

        vocab_load(k, slot).wait()
        cols = pl.ds(pl.multiple_of(k * slab, slab), slab)
        table[:, cols] = stage[slot].astype(jnp.bfloat16)
        return 0

    part_rows = 32

    def norm(slot, prompt):
        def body(i, _):
            at = pl.multiple_of(i * part_rows, part_rows)
            value = normalize(xs[slot, prompt, pl.ds(at, part_rows)], again_ref[...])
            value = value.astype(jnp.bfloat16)
            to = pl.multiple_of(prompt * LEN + slot * quarter + at, part_rows)
            for b in range(groups):
                h[b, pl.ds(to, part_rows)] = value[:, b * block : (b + 1) * block]
            return 0

        lax.fori_loop(0, quarter // part_rows, body, 0)

    span_rows = 512

    def project(g, first):
        own = owner_ref[g]

        def body(i, _):
            at = pl.ds(pl.multiple_of(i * span_rows, span_rows), span_rows)
            term = dot32(h[own, at], wcat[g, :, NOPE:])
            acc[at, NOPE:] = term if first else acc[at, NOPE:] + term
            return 0

        lax.fori_loop(0, LEN // span_rows, body, 0)

    def project_step(step):
        def one(way, _):
            g = dp - (1 - 2 * way) * (step + 1)

            @pl.when((g >= 0) & (g < groups))
            def _():
                share_wait(g)
                project(g, False)

            return 0

        lax.fori_loop(0, 2, one, 0)

    def project_all(p, low, high):
        def body(i, _):
            at = pl.ds(pl.multiple_of(p * LEN + i * span_rows, span_rows), span_rows)
            total = dot32(h[owner_ref[0], at], wcat[0, :, low:high])
            for g in range(1, groups):
                total = total + dot32(h[owner_ref[g], at], wcat[g, :, low:high])
            acc[at, low:high] = total
            return 0

        lax.fori_loop(0, LEN // span_rows, body, 0)

    lax.fori_loop(0, 7, vocab_step, 0)
    both(A, 0)
    arrived(0, share_first)
    crossing(1, 0, ty, tx).start()
    own_rows(1, ty).start()
    loads[4].wait()
    norm(ty, 0)
    cross_step(0, 0)
    both(B, 0)
    own_rows(0, partner).wait_recv()
    norm(partner, 0)
    both(Q, 0)
    cross_step(0, 1)
    lax.fori_loop(7, count, vocab_step, 0)
    side_step(0, 0)
    both(A, 1)
    arrived(1, share_first)
    share_second(dp)
    arrived(0, share_second)
    both(B, 1)
    norm(ty, 1)
    side_step(0, 1)
    norm(across, 0)
    share_third(dp)
    arrived(0, share_third)
    far_wait(0)
    norm(far, 0)
    cross_step(1, 0)
    both(Q, 1)
    start_hop(R)
    arrived(1, share_second)
    take(A, 2)
    arrived(2, share_first)
    crossing(1, 1, ty, tx).start()
    share_wait(dp)
    project(dp, True)
    arrived(1, share_third)
    project_step(0)
    forward(R, 0)
    start_hop(O)
    side_step(1, 0)
    arrived(2, share_second)
    project_step(1)
    cross_step(1, 1)
    arrived(2, share_third)
    forward(R, 1)
    own_rows(1, partner).wait_recv()
    norm(partner, 1)

    def stored(b):
        place = jnp.int32(0)
        for g in range(groups):
            place = jnp.where(owner_ref[g] == b, g, place)
        return place

    brows = LATENT // groups

    lane = lax.broadcasted_iota(jnp.int32, (TILE, 2 * ROPE), 1)

    def rotate(values, at):
        swapped = jnp.where(
            lane % ROPE < ROPE // 2,
            pltpu.roll(values, 2 * ROPE - ROPE // 2, 1),
            pltpu.roll(values, ROPE // 2, 1),
        )
        return values * cos_ref[at] + swapped * sin_ref[at]

    factor = (NOPE + ROPE) ** (-0.5) * 1.4426950408889634
    lives = [lengths_ref[deal_ref[dp * per_grp + p]] for p in range(per_grp)]

    def keys(p, tile, _):
        down = acc[pl.ds(pl.multiple_of(p * LEN + tile * TILE, TILE), TILE), QCOLS:]
        to = pl.ds(pl.multiple_of(tile * TILE, TILE), TILE)
        latent = normalize(down[:, :LATENT], lgain_ref[...]).astype(jnp.bfloat16)
        key_rope = rotate(down[:, LATENT:], to).astype(jnp.bfloat16)
        key_val = dot32(latent, wbl[...]).astype(jnp.bfloat16)
        for head in range(heads):
            k_ref[p, head, to, :NOPE] = key_val[:, 2 * head * NOPE : (2 * head + 1) * NOPE]
            k_ref[p, head, to, NOPE:] = key_rope
            v_ref[p, head, to] = key_val[:, (2 * head + 1) * NOPE : (2 * head + 2) * NOPE]
        return 0


    def hears(p, slot, head):
        cols = pl.ds(pl.multiple_of(slot * piece + head * NOPE, NOPE), NOPE)
        return heard.at[p, :, cols]

    def heads_of(head, p, tile, slot):
        return remote(
            o_ref.at[head, tile, p], hears(p, tx * ty_size + slot, head),
            o_send.at[head, p, tile], o_recv.at[head, p, slot], ty=tile,
        )

    def passed(head, p, slot, slot_tx, source=None):
        ref = hears(p, slot_tx * ty_size + slot, head)
        return remote(
            ref if source is None else source, ref,
            f_send.at[head, p, slot], f_recv.at[head, p, slot], tx=other,
        )

    def own_passed(head, p, tile):
        return passed(head, p, ty, tx, o_ref.at[head, tile, p])

    def relay(head, p):
        for k in range(1, ty_size):
            slot = (ty + k) % ty_size
            heads_of(head, p, ty, slot).wait_recv()
            passed(head, p, slot, tx).start()

    tile_order = (3, 1, 2, 0)

    def attention(head, p):
        live = jnp.where(p == 0, lives[0], lives[1])
        last = jnp.zeros((1, NOPE), jnp.float32)
        nope_at = (1 - head) * NOPE
        for t in tile_order:
            span = (t + 1) * TILE
            at = pl.ds(pl.multiple_of(p * LEN + t * TILE, TILE), TILE)
            turned = rotate(acc[at, 2 * NOPE : QCOLS], pl.ds(t * TILE, TILE))
            i = lax.broadcasted_iota(jnp.int32, (TILE, span), 0) + t * TILE
            j = lax.broadcasted_iota(jnp.int32, (TILE, span), 1)
            allowed = j <= jnp.minimum(i, live - 1)
            mine = jnp.where(lane // ROPE == 1 - head, turned, 0.0)
            query = jnp.concatenate([acc[at, nope_at : nope_at + NOPE], mine], axis=1)
            score = lax.dot_general(
                query.astype(jnp.bfloat16), k_ref[p, head, :span], (((1,), (1,)), ((), ())),
                preferred_element_type=jnp.float32,
            )
            score = jnp.where(allowed, score, -1e30)
            expo = jnp.exp2((score - jnp.max(score, axis=-1, keepdims=True)) * factor)
            prob = expo * (1.0 / jnp.sum(expo, axis=-1, keepdims=True))
            out = dot32(prob.astype(jnp.bfloat16), v_ref[p, head, :span]).astype(jnp.bfloat16)
            o_ref[head, t, p] = out
            at_last = lax.broadcasted_iota(jnp.int32, (TILE, NOPE), 0) + t * TILE == live - 1
            last = last + jnp.sum(
                jnp.where(at_last, out.astype(jnp.float32), 0.0), axis=0, keepdims=True
            )

            @pl.when(ty == t)
            def _():
                mine_at = pl.multiple_of(spot * piece + head * NOPE, NOPE)
                heard[p, :, pl.ds(mine_at, NOPE)] = out
                own_passed(head, p, t).start()

            @pl.when(ty != t)
            def _():
                heads_of(head, p, t, ty).start()

        for k in range(per_grp):

            @pl.when(p == k)
            def _():
                ends_ref[spot, k : k + 1, head * NOPE : (head + 1) * NOPE] = last

    def wide(j, slot_tx, slot_ty):
        slot = slot_tx * ty_size + slot_ty
        return wos.at[j, pl.ds(pl.multiple_of(slot * piece, piece), piece)]

    def move(n, j, slot_tx, slot_ty, source=None, **where):
        ref = wide(j, slot_tx, slot_ty)
        return remote(
            ref if source is None else source, ref, w_send.at[n, j], w_recv.at[n, j], **where
        )

    early = [jnp.where(dp < groups // 2, k, groups - 1 - k) for k in range(steps)]
    late = jnp.where(dp < groups // 2, groups - 1, 0)

    def aim(g):
        return owner_ref[g] // (groups // tx_size)

    def first_for(side):
        found = early[-1]
        for g in early[-2::-1]:
            found = jnp.where(aim(g) == side, g, found)
        return found

    def first_rows(side):
        found = woz[early[-1]]
        for g in early[-2::-1]:
            found = jnp.where(aim(g) == side, woz[g], found)
        return found

    def second_for(side):
        found = late
        for g in early:
            found = jnp.where((aim(g) == side) & (g != first_for(side)), g, found)
        return found

    mine_at = pl.ds(pl.multiple_of(spot * piece, piece), piece)

    def spread(j, give_rows, keep_rows):
        give[j] = give_rows
        move(0, j, tx, ty, give.at[j], tx=other).start()
        wos[j, mine_at] = keep_rows
        move(1, j, tx, ty, ty=across).start()
        move(2, j, tx, ty, ty=partner).start()

    def spread_on(j):
        move(0, j, other, ty, tx=other).wait_recv()
        move(3, j, other, ty, ty=across).start()
        move(4, j, other, ty, ty=partner).start()

    def spread_in(j):
        move(1, j, tx, across, ty=across).wait_recv()
        move(5, j, tx, across, ty=partner).start()

    def spread_last(j):
        move(3, j, other, across, ty=across).wait_recv()
        move(6, j, other, across, ty=partner).start()

    def prompt_step(p, _):
        @pl.when(p == 0)
        def _():
            take(B, 2)
            take(Q, 2)
            project_step(2)
            for b in range(groups):
                wbl[b * brows : (b + 1) * brows] = wbs[stored(b)]

        @pl.when(p == 1)
        def _():
            side_step(1, 1)
            norm(across, 1)
            far_wait(1)
            norm(far, 1)
            relay(1, 0)
            project_all(1, 0, QCOLS + ACOLS)

        lax.fori_loop(0, LEN // TILE, functools.partial(keys, p), 0)
        attention(0, p)

        @pl.when(p == 0)
        def _():
            forward(O, 0)
            for step in range(steps):
                take(R, step)
            project_all(0, 0, NOPE)

        @pl.when(p == 1)
        def _():
            take(O, 0)
            take(O, 1)
            spread(0, first_rows(other), first_rows(tx))

        relay(0, p)
        attention(1, p)
        pl.when(p == 0)(lambda: forward(O, 1))
        return 0

    lax.fori_loop(0, per_grp, prompt_step, 0)

    def row_of(k, slot):
        peer = (spot + k) % plane
        return remote(
            ends_ref.at[spot], ends_ref.at[slot], e_send.at[k], e_recv.at[k],
            tx=peer // ty_size, ty=peer % ty_size,
        )

    for k in range(1, plane):
        row_of(k, spot).start()
    for p in range(per_grp):
        tile = (lives[p] - 1) // quarter
        inside = lax.broadcasted_iota(jnp.int32, (quarter, half), 0) + tile * quarter
        tokens = xs[jnp.maximum(tile, 0), p, :, pl.ds(pl.multiple_of(tx * half, half), half)]
        base_ref[p : p + 1] = jnp.sum(
            jnp.where(inside == lives[p] - 1, tokens.astype(jnp.float32), 0.0),
            axis=0, keepdims=True,
        )
    take(O, 2)
    spread(1, woz[second_for(other)], woz[second_for(tx)])
    relay(1, 1)
    for j in range(2):
        spread_on(j)
        spread_in(j)
    for j in range(2):
        spread_last(j)
    for k in range(1, plane):
        row_of(k, (spot + plane - k) % plane).wait_recv()
    line_ref[...] = jnp.zeros_like(line_ref)
    for slot in range(plane):
        line_ref[0:per_grp, slot * piece : (slot + 1) * piece] = ends_ref[slot]
    for head in range(heads):
        for p in range(per_grp):
            for k in range(ty_size):
                passed(head, p, (ty + k) % ty_size, other).wait_recv()
    for j in range(2):
        move(2, j, tx, partner, ty=partner).wait_recv()
        move(4, j, other, partner, ty=partner).wait_recv()
        move(5, j, tx, far, ty=partner).wait_recv()
        move(6, j, other, far, ty=partner).wait_recv()

    spots = [jnp.where(owner_ref[first_for(tx)] % 2 == i, 0, 1) for i in range(2)]
    chosen = line_ref[...].astype(jnp.bfloat16)
    peers = groups * tx_size
    place = dp * tx_size + tx
    for i in range(2):
        cols = slice(i * block, (i + 1) * block)
        value = base_ref[:, cols] + dot32(chosen, wos[spots[i]])[:per_grp]
        full[place, :, cols] = value.astype(jnp.bfloat16).astype(jnp.float32)

    def along_peers(k, slot):
        peer = (place + k) % peers
        return remote(
            full.at[place], full.at[slot], r_send.at[k], r_recv.at[k],
            dp=peer // tx_size, tx=peer % tx_size,
        )

    for k in range(1, peers):
        along_peers(k, place).start()

    strip = 256

    def out_step(n, _):
        for i in range(2):

            @pl.when(n // 2 == i)
            def _():
                inside = pl.ds(pl.multiple_of((n % 2) * strip, strip), strip)
                cols = pl.ds(pl.multiple_of(n * strip, strip), strip)
                model = pl.ds(pl.multiple_of(tx * half + n * strip, strip), strip)
                for p in range(per_grp):
                    total = dot32(heard[p], wos[spots[i], :, inside])
                    hidden_ref[p, :, cols] = (
                        xs[ty, p, :, model].astype(jnp.float32) + total
                    ).astype(jnp.bfloat16)

        return 0

    lax.fori_loop(0, 4, out_step, 0)

    for k in range(1, peers):
        along_peers(k, (place + peers - k) % peers).wait_recv()
    for g in range(groups):
        for t in range(tx_size):
            rows_ref[g * per_grp : (g + 1) * per_grp, t * half : (t + 1) * half] = full[
                g * tx_size + t
            ]
    final = normalize(rows_ref[...], fgain_ref[...])
    owner = owner_ref[dp]
    mine = jnp.zeros((groups * per_grp, block), jnp.float32)
    for g in range(groups):
        mine = jnp.where(owner == g, final[:, g * block : (g + 1) * block], mine)
    mine = mine.astype(jnp.bfloat16)

    def logit_step(k, _):
        cols = pl.ds(pl.multiple_of(k * slab, slab), slab)
        logits = dot32(mine, table[:, cols])
        for g in range(groups):
            part[g, :, cols] = logits[g * per_grp : (g + 1) * per_grp]
        return 0

    parts = 2
    share_words = words // parts

    def along_dp(n, k, slot):
        peer = (dp + k) % groups
        cols = pl.ds(n * share_words, share_words)
        return remote(
            part.at[peer, :, cols], incoming.at[slot, :, cols], l_send.at[n, k], l_recv.at[n, k],
            dp=peer,
        )

    for n in range(parts):
        lax.fori_loop(n * count // parts, (n + 1) * count // parts, logit_step, 0)
        for k in range(1, groups):
            along_dp(n, k, dp).start()
    for n in range(parts):
        cols = slice(n * share_words, (n + 1) * share_words)
        total = part[dp, :, cols]
        for k in range(1, groups):
            slot = (dp + groups - k) % groups
            along_dp(n, k, slot).wait_recv()
            total = total + incoming[slot, :, cols]
        out_ref[:, cols] = total

    for p in range(per_grp):
        for k in range(chunks):
            crossing(p, k, ty, tx).wait_send()
            sideways(p, k, tx).wait_send()
            inward(p, k, 0, across, tx).wait_send()
            inward(p, k, 1, across, other).wait_send()
        own_rows(p, ty).wait_send()
    for step in range(steps):
        for which in range(5):
            for way in range(2):
                copy, runs = hop(which, way, step)
                pl.when(runs)(copy.wait_send)
    for g in range(groups):
        for n in range(7):
            share(n, g).wait_send()
    for head in range(heads):
        for p in range(per_grp):
            own_passed(head, p, ty).wait_send()
            for k in range(1, ty_size):
                slot = (ty + k) % ty_size
                heads_of(head, p, slot, ty).wait_send()
                passed(head, p, slot, tx).wait_send()
    for j in range(2):
        move(0, j, tx, ty, give.at[j], tx=other).wait_send()
        move(1, j, tx, ty, ty=across).wait_send()
        move(2, j, tx, ty, ty=partner).wait_send()
        move(3, j, other, ty, ty=across).wait_send()
        move(4, j, other, ty, ty=partner).wait_send()
        move(5, j, tx, across, ty=partner).wait_send()
        move(6, j, other, across, ty=partner).wait_send()
    for k in range(1, plane):
        row_of(k, spot).wait_send()
    for k in range(1, peers):
        along_peers(k, place).wait_send()
    for n in range(parts):
        for k in range(1, groups):
            along_dp(n, k, dp).wait_send()


def hand_on_kernel(hidden_ref, logits_ref, hidden_out, logits_out, sem):
    copies = [
        pltpu.make_async_copy(hidden_ref, hidden_out, sem.at[0]),
        pltpu.make_async_copy(logits_ref, logits_out, sem.at[1]),
    ]
    for copy in copies:
        copy.start()
    for copy in copies:
        copy.wait()


def hand_on(hidden, logits):
    hbm = pl.BlockSpec(memory_space=pl.ANY)
    return pl.pallas_call(
        hand_on_kernel,
        in_specs=[hbm, hbm],
        out_specs=[hbm, hbm],
        out_shape=[
            jax.ShapeDtypeStruct(hidden.shape, hidden.dtype),
            jax.ShapeDtypeStruct(logits.shape, logits.dtype),
        ],
        scratch_shapes=[pltpu.SemaphoreType.DMA((2,))],
    )(hidden, logits)


def layer(groups, owner, lengths, deal, x, again, lgain, fgain, wq, wa, wb, wo, vocab):
    per_grp, quarter, width = x.shape
    block, words = vocab.shape
    half = width // 2
    piece = 2 * NOPE
    slab = 512
    steps = groups - 1
    peers = 2 * groups
    position = np.arange(LEN, dtype=np.float32)
    frequency = np.power(
        np.float32(10000.0), -np.arange(ROPE // 2, dtype=np.float32) / np.float32(ROPE // 2)
    ).astype(np.float32)
    angles = (position[:, None] * frequency).astype(np.float32).astype(np.float64)
    cosine, sine = np.cos(angles), np.sin(angles)
    cosine = jnp.asarray(np.concatenate([cosine] * 4, axis=1).astype(np.float32))
    sine = jnp.asarray(np.concatenate([-sine, sine, -sine, sine], axis=1).astype(np.float32))
    dma = pltpu.SemaphoreType.DMA
    vmem = pl.BlockSpec(memory_space=pltpu.VMEM)
    smem = pl.BlockSpec(memory_space=pltpu.SMEM)
    hbm = pl.BlockSpec(memory_space=pl.ANY)
    bf16 = lambda *dims: pltpu.VMEM(dims, jnp.bfloat16)
    f32 = lambda *dims: pltpu.VMEM(dims, jnp.float32)
    return pl.pallas_call(
        functools.partial(layer_kernel, groups),
        in_specs=[smem, smem, smem, hbm, vmem, vmem, vmem, vmem, vmem, hbm, hbm, hbm, hbm, hbm],
        out_specs=[vmem, vmem],
        out_shape=[
            jax.ShapeDtypeStruct((per_grp, quarter, half), jnp.bfloat16),
            jax.ShapeDtypeStruct((per_grp, words), jnp.float32),
        ],
        scratch_shapes=[
            bf16(4, per_grp, quarter, width),
            bf16(groups, per_grp * LEN, block),
            bf16(groups, block, QCOLS + ACOLS),
            bf16(groups, LATENT // groups, 2 * piece),
            bf16(LATENT, 2 * piece),
            bf16(groups, piece, block),
            bf16(2, piece, block),
            bf16(2, 8 * piece, block),
            f32(per_grp * LEN, QCOLS + ACOLS),
            bf16(per_grp, 2, LEN, 2 * NOPE),
            bf16(per_grp, 2, LEN, NOPE),
            bf16(2, 4, per_grp, TILE, NOPE),
            bf16(per_grp, TILE, 8 * piece),
            bf16(block, words),
            f32(2, block, slab),
            f32(*wq.shape),
            f32(wa.shape[1], block // 4),
            f32(*wb.shape),
            f32(block, piece),
            f32(8, per_grp, piece),
            f32(per_grp, half),
            f32(8, width),
            f32(peers, per_grp, half),
            f32(groups * per_grp, width),
            f32(groups, per_grp, words),
            f32(groups, per_grp, words),
            dma((5,)), dma((2,)),
            dma((per_grp, 2)), dma((per_grp, 2)), dma((per_grp, 2)), dma((per_grp, 2)),
            dma((2, per_grp, 2)), dma((2, per_grp, 2)), dma((per_grp,)), dma((per_grp,)),
            dma((2, 5, steps)), dma((2, 5, steps)), dma((7, groups)), dma((7, groups)),
            dma((2, per_grp, 4)), dma((2, per_grp, 4)), dma((2, per_grp, 4)),
            dma((2, per_grp, 4)), dma((7, 2)), dma((7, 2)),
            dma((8,)), dma((8,)), dma((peers,)), dma((peers,)), dma((2, groups)),
            dma((2, groups)),
        ],
        compiler_params=pltpu.CompilerParams(
            collective_id=0, has_side_effects=True, vmem_limit_bytes=60 * 1024 * 1024
        ),
        cost_estimate=pl.CostEstimate(
            flops=16_000_000_000, bytes_accessed=24_000_000, transcendentals=3_000_000
        ),
    )(owner, lengths, deal, x, again, lgain, fgain, cosine, sine, wq, wa.T, wb, wo, vocab)


def load_vocab(vocab_chunk, vocab_ref, table, v_sem):
    loads = []
    for k in range(vocab_ref.shape[1] // vocab_chunk):
        cols = pl.ds(k * vocab_chunk, vocab_chunk)
        loads.append(
            pltpu.make_async_copy(vocab_ref.at[:, cols], table.at[:, cols], v_sem.at[k])
        )
        loads[-1].start()
    return loads


def next_token(
    groups, tx_size, ty_size, vocab_chunk, loads, owner_ref, picked_ref, gain_ref, out_ref, seen, full,
    rows_ref, table, part, incoming, t_send, t_recv, r_send, r_recv, l_send, l_recv,
):
    dp, tx, ty = lax.axis_index("dp"), lax.axis_index("tx"), lax.axis_index("ty")
    per_grp, half = picked_ref.shape
    block = table.shape[0]
    peers = groups * tx_size
    place = dp * tx_size + tx
    count = len(loads)

    def along_ty(k, slot):
        return remote(
            picked_ref, seen.at[slot], t_send.at[k], t_recv.at[k], ty=(ty + k) % ty_size
        )

    for k in range(1, ty_size):
        along_ty(k, ty).start()
    merged = picked_ref[...]
    for k in range(1, ty_size):
        slot = (ty + ty_size - k) % ty_size
        along_ty(k, slot).wait_recv()
        merged = merged + seen[slot]
    full[place] = merged

    def along_peers(k, slot):
        peer = (place + k) % peers
        return remote(
            full.at[place], full.at[slot], r_send.at[k], r_recv.at[k],
            dp=peer // tx_size, tx=peer % tx_size,
        )

    for k in range(1, peers):
        along_peers(k, place).start()
    for k in range(1, peers):
        along_peers(k, (place + peers - k) % peers).wait_recv()
    for g in range(groups):
        for t in range(tx_size):
            rows_ref[g * per_grp : (g + 1) * per_grp, t * half : (t + 1) * half] = full[
                g * tx_size + t
            ]
    final = normalize(rows_ref[...], gain_ref[...])
    owner = owner_ref[dp]
    mine = jnp.zeros((groups * per_grp, block), jnp.float32)
    for g in range(groups):
        mine = jnp.where(owner == g, final[:, g * block : (g + 1) * block], mine)
    mine = mine.astype(jnp.bfloat16)
    for k in range(count):
        loads[k].wait()
        cols = slice(k * vocab_chunk, (k + 1) * vocab_chunk)
        logits = dot32(mine, table[:, cols].astype(jnp.bfloat16))
        for g in range(groups):
            part[g, :, cols] = logits[g * per_grp : (g + 1) * per_grp]

    def along_dp(k, slot):
        peer = (dp + k) % groups
        return remote(part.at[peer], incoming.at[slot], l_send.at[k], l_recv.at[k], dp=peer)

    for k in range(1, groups):
        along_dp(k, dp).start()
    total = part[dp]
    for k in range(1, groups):
        slot = (dp + groups - k) % groups
        along_dp(k, slot).wait_recv()
        total = total + incoming[slot]
    out_ref[...] = total
    for k in range(1, ty_size):
        along_ty(k, ty).wait_send()
    for k in range(1, peers):
        along_peers(k, place).wait_send()
    for k in range(1, groups):
        along_dp(k, dp).wait_send()


def tail_kernel(
    groups, tx_size, ty_size, vocab_chunk, owner_ref, picked_ref, gain_ref, vocab_ref, out_ref,
    seen, full, rows_ref, table, part, incoming, t_send, t_recv, r_send, r_recv, l_send, l_recv,
    v_sem,
):
    dp, tx, ty = lax.axis_index("dp"), lax.axis_index("tx"), lax.axis_index("ty")
    peers = groups * tx_size
    place = dp * tx_size + tx
    loads = load_vocab(vocab_chunk, vocab_ref, table, v_sem)
    for k in range(1, ty_size):
        greet(ty=(ty + k) % ty_size)
    for k in range(1, peers):
        peer = (place + k) % peers
        greet(dp=peer // tx_size, tx=peer % tx_size)
    pl.semaphore_wait(pltpu.get_barrier_semaphore(), ty_size + peers - 2)
    next_token(
        groups, tx_size, ty_size, vocab_chunk, loads, owner_ref, picked_ref, gain_ref, out_ref,
        seen, full, rows_ref, table, part, incoming, t_send, t_recv, r_send, r_recv, l_send,
        l_recv,
    )


def tail(groups, tx_size, ty_size, owner, picked, gain, vocab):
    per_grp, half = picked.shape
    block, words = vocab.shape
    vocab_chunk = 512
    peers = groups * tx_size
    dma = pltpu.SemaphoreType.DMA
    vmem = pl.BlockSpec(memory_space=pltpu.VMEM)
    return pl.pallas_call(
        functools.partial(tail_kernel, groups, tx_size, ty_size, vocab_chunk),
        in_specs=[
            pl.BlockSpec(memory_space=pltpu.SMEM), vmem, vmem, pl.BlockSpec(memory_space=pl.ANY),
        ],
        out_specs=vmem,
        out_shape=jax.ShapeDtypeStruct((per_grp, words), jnp.float32),
        scratch_shapes=[
            pltpu.VMEM((ty_size, per_grp, half), jnp.float32),
            pltpu.VMEM((peers, per_grp, half), jnp.float32),
            pltpu.VMEM((groups * per_grp, half * tx_size), jnp.float32),
            pltpu.VMEM((block, words), jnp.float32),
            pltpu.VMEM((groups, per_grp, words), jnp.float32),
            pltpu.VMEM((groups, per_grp, words), jnp.float32),
            dma((ty_size,)), dma((ty_size,)), dma((peers,)), dma((peers,)),
            dma((groups,)), dma((groups,)), dma((words // vocab_chunk,)),
        ],
        compiler_params=pltpu.CompilerParams(
            collective_id=1, has_side_effects=True, vmem_limit_bytes=40 * 1024 * 1024
        ),
        cost_estimate=pl.CostEstimate(
            flops=100_000_000, bytes_accessed=16_000_000, transcendentals=0
        ),
    )(owner, picked, gain, vocab)


def rotate_half(values, position):
    half_dim = values.shape[-1] // 2
    frequency = 10000.0 ** (-jnp.arange(half_dim, dtype=jnp.float32) / half_dim)
    angles = position.astype(jnp.float32)[..., None] * frequency
    cosine = jnp.cos(angles)
    sine = jnp.sin(angles)
    first_half = values[..., :half_dim]
    second_half = values[..., half_dim:]
    return jnp.concatenate(
        [first_half * cosine - second_half * sine, first_half * sine + second_half * cosine],
        axis=-1,
    )


def split_positions(
    inputs, inverse, live_len, attn_gain, latent_gain, w_query, w_down_kv, w_up_kv, w_out
):
    groups = lax.axis_size("dp")

    def arrange(gathered):
        block_rows = gathered.shape[0] // groups
        return jnp.concatenate(
            [
                lax.dynamic_slice_in_dim(gathered, inverse[g] * block_rows, block_rows, 0)
                for g in range(groups)
            ],
            axis=0,
        )

    query_w, down_w, up_w, out_w = (
        lax.all_gather(w_query.astype(jnp.bfloat16), "dp", axis=0, tiled=True),
        lax.all_gather(w_down_kv.astype(jnp.bfloat16), "dp", axis=0, tiled=True),
        lax.all_gather(w_up_kv.astype(jnp.bfloat16), "dp", axis=0, tiled=True),
        lax.all_gather(w_out.astype(jnp.bfloat16), "dp", axis=0, tiled=True),
    )
    query_w = arrange(query_w)
    down_w = arrange(down_w)
    up_w = arrange(up_w)
    out_w = arrange(out_w)
    query_w, up_w = (
        lax.all_gather(query_w, "ty", axis=1, tiled=True),
        lax.all_gather(up_w, "ty", axis=1, tiled=True),
    )
    per_grp, quarter, width = inputs.shape
    heads = query_w.shape[1] // (NOPE + ROPE)
    position = lax.axis_index("ty") * quarter + jnp.arange(quarter, dtype=jnp.int32)
    flat_rows = inputs.reshape(per_grp * quarter, width)
    normed = normalize(flat_rows, attn_gain).astype(jnp.bfloat16)
    queries = jnp.dot(normed, query_w, preferred_element_type=jnp.float32).reshape(
        per_grp, quarter, heads, NOPE + ROPE
    )
    queries = jnp.concatenate(
        [queries[..., :NOPE], rotate_half(queries[..., NOPE:], position[None, :, None])], axis=-1
    ).astype(jnp.bfloat16)
    down_proj = jnp.dot(normed, down_w, preferred_element_type=jnp.float32).reshape(
        per_grp, quarter, LATENT + ROPE
    )
    latent = normalize(down_proj[..., :LATENT], latent_gain).astype(jnp.bfloat16)
    key_rope = rotate_half(down_proj[..., LATENT:], position[None, :]).astype(jnp.bfloat16)
    gathered = lax.all_gather(
        jnp.concatenate([latent, key_rope], axis=-1), "ty", axis=1, tiled=True
    )
    key_val = jnp.dot(gathered[..., :LATENT], up_w, preferred_element_type=jnp.float32).astype(
        jnp.bfloat16
    )
    rope_all = gathered[..., LATENT:]
    key_val = key_val.reshape(per_grp, LEN, heads, 2, NOPE)
    key_nope = key_val[:, :, :, 0]
    values = key_val[:, :, :, 1]
    score_scale = (NOPE + ROPE) ** (-0.5)
    scores = (
        jnp.einsum(
            "pqhd,pkhd->phqk", queries[..., :NOPE], key_nope, preferred_element_type=jnp.float32
        )
        + jnp.einsum(
            "pqhd,pkd->phqk", queries[..., NOPE:], rope_all, preferred_element_type=jnp.float32
        )
    ) * score_scale
    key_pos = jnp.arange(LEN, dtype=jnp.int32)
    allowed = (key_pos[None, None, :] <= position[None, :, None]) & (
        key_pos[None, None, :] < live_len[:, None, None]
    )
    scores = jnp.where(allowed[:, None], scores, -1e30)
    top = jnp.max(scores, axis=-1, keepdims=True)
    expo = jnp.exp(scores - top)
    softmax_w = (expo / jnp.sum(expo, axis=-1, keepdims=True)).astype(jnp.bfloat16)
    attended = jnp.einsum(
        "phqk,pkhd->pqhd", softmax_w, values, preferred_element_type=jnp.float32
    ).astype(jnp.bfloat16)
    attended = attended.reshape(per_grp * quarter, heads * NOPE)
    own_width = width // lax.axis_size("tx")
    col_start = lax.axis_index("tx") * own_width
    partial_value = lax.dot_general(
        attended, out_w, (((1,), (1,)), ((), ())), preferred_element_type=jnp.float32
    ).reshape(per_grp, quarter, width)
    summed = lax.psum_scatter(partial_value, "tx", scatter_dimension=2, tiled=True)
    residual = lax.dynamic_slice_in_dim(inputs, col_start, own_width, 2)
    layer_out = (residual.astype(jnp.float32) + summed).astype(jnp.bfloat16)
    return layer_out


def shards(
    inputs,
    lengths,
    prompt_deal,
    block_owner,
    attn_gain,
    latent_gain,
    final_gain,
    w_query,
    w_down_kv,
    w_up_kv,
    w_out,
    w_vocab,
):
    groups = lax.axis_size("dp")
    dp, tx, ty = lax.axis_index("dp"), lax.axis_index("tx"), lax.axis_index("ty")
    per_grp, quarter, width = inputs.shape
    half = width // lax.axis_size("tx")
    whole_heads = w_query.shape[1] == QCOLS and w_up_kv.shape[1] == 4 * NOPE
    here = whole_heads and (lax.axis_size("tx"), lax.axis_size("ty"), per_grp) == (2, 4, 2)
    if here and groups == 4 and (quarter, width) == (TILE, 4 * w_query.shape[0]):
        return hand_on(
            *layer(
                groups, block_owner, lengths, prompt_deal, inputs, attn_gain[None],
                latent_gain[None], final_gain[None], w_query, w_down_kv, w_up_kv, w_out, w_vocab,
            )
        )

    order = jnp.arange(groups, dtype=jnp.int32)
    inverse = jnp.sum(
        jnp.where(block_owner[None, :] == order[:, None], order[None, :], 0), axis=1
    ).astype(jnp.int32)
    slots = dp * per_grp + jnp.arange(per_grp, dtype=jnp.int32)
    names = jnp.arange(lengths.shape[0], dtype=jnp.int32)

    def at_index(values, index):
        return jnp.sum(jnp.where(names[None] == index[:, None], values[None], 0), axis=1)

    live_len = at_index(lengths, at_index(prompt_deal, slots))
    layer_out = split_positions(
        inputs, inverse, live_len, attn_gain, latent_gain, w_query, w_down_kv, w_up_kv, w_out
    )

    at = live_len - 1 - ty * quarter
    picked = jnp.stack(
        [
            lax.dynamic_slice(
                layer_out, (i, jnp.clip(at[i], 0, quarter - 1), 0), (1, 1, half)
            ).reshape(half)
            for i in range(per_grp)
        ]
    ).astype(jnp.float32)
    inside = (at >= 0) & (at < quarter)
    picked = jnp.where(inside[:, None], picked, 0.0)
    logits = tail(
        groups, lax.axis_size("tx"), lax.axis_size("ty"), block_owner, picked, final_gain[None],
        w_vocab,
    )
    return (layer_out, logits)


def solution(mesh):
    placed = (
        P("dp", "ty", None),
        P(),
        P(),
        P(),
        P(),
        P(),
        P(),
        P("dp", ("tx", "ty")),
        P("dp", None),
        P("dp", ("tx", "ty")),
        P("dp", "tx"),
        P("dp", ("tx", "ty")),
    )
    return jax.shard_map(
        shards,
        mesh=mesh,
        in_specs=placed,
        out_specs=(P("dp", "ty", "tx"), P("dp", ("tx", "ty"))),
        check_vma=False,
    )
```

```python
import functools

import jax
import jax.numpy as jnp
import numpy as np
from jax import lax
from jax.experimental import pallas as pl
from jax.experimental.pallas import tpu as pltpu
from jax.sharding import PartitionSpec as P

NOPE = 128
ROPE = 64
LATENT = 512
LEN = 1024
TILE = 256
EPS = 1e-06
QCOLS = 384
ACOLS = 640


def normalize(values, gain):
    wide = values.astype(jnp.float32)
    return wide * lax.rsqrt(jnp.mean(wide * wide, axis=-1, keepdims=True) + EPS) * gain


def dot32(left, right):
    return jnp.dot(left, right, preferred_element_type=jnp.float32)


def remote(src, dst, send, recv, **where):
    return pltpu.make_async_remote_copy(
        src_ref=src,
        dst_ref=dst,
        send_sem=send,
        recv_sem=recv,
        device_id=where,
        device_id_type=pl.DeviceIdType.MESH,
    )


def greet(**where):
    pl.semaphore_signal(
        pltpu.get_barrier_semaphore(),
        inc=1,
        device_id=where,
        device_id_type=pl.DeviceIdType.MESH,
    )


def layer_kernel(
    groups, owner_ref, lengths_ref, deal_ref, x_ref, again_ref, lgain_ref, fgain_ref, cos_ref,
    sin_ref, wq_ref, wa_ref, wb_ref, wo_ref, vocab_ref, hidden_ref, out_ref,
    xs, h, wrs, wqs, was, wbs, wbl, woz, give, wos, acc, k_ref, v_ref, o_ref, heard, mixed, table, stage,
    wq_f, wa_f, wb_f, wo_f, ends_ref, base_ref, line_ref, full, rows_ref, part, incoming,
    local, v_sem, x_send, x_recv, y_send, y_recv, p_send, p_recv, b_send, b_recv,
    z_send, z_recv, a_send, a_recv, o_send, o_recv, f_send, f_recv, w_send, w_recv,
    e_send, e_recv, r_send, r_recv, l_send, l_recv,
):
    dp, tx, ty = lax.axis_index("dp"), lax.axis_index("tx"), lax.axis_index("ty")
    tx_size, ty_size = 2, 4
    per_grp = 2
    core = ty % 2
    partner = ty + 1 - 2 * core
    across = (ty + 2) % 4
    far = (partner + 2) % 4
    other = 1 - tx
    spot = tx * ty_size + ty
    plane = tx_size * ty_size
    steps = groups - 1
    chunks = 2
    quarter, width = x_ref.shape[1], x_ref.shape[2]
    half = width // tx_size
    block = width // groups
    rows = quarter // (2 * chunks)
    words = vocab_ref.shape[1]
    slab = stage.shape[-1]
    count = words // slab
    piece = 2 * NOPE
    heads = 2

    loads = [
        pltpu.make_async_copy(wa_ref.at[:, pl.ds(pl.multiple_of((spot // 2) * 128, 128), 128)], wa_f, local.at[0]),
        pltpu.make_async_copy(wb_ref, wb_f, local.at[1]),
        pltpu.make_async_copy(wq_ref, wq_f, local.at[2]),
        pltpu.make_async_copy(
            wo_ref.at[:, pl.ds(pl.multiple_of(ty * piece, piece), piece)], wo_f, local.at[3]
        ),
        pltpu.make_async_copy(x_ref, xs.at[ty], local.at[4]),
    ]
    for load in loads:
        load.start()

    def vocab_load(k, slot):
        cols = pl.ds(pl.multiple_of(k * slab, slab), slab)
        return pltpu.make_async_copy(vocab_ref.at[:, cols], stage.at[slot], v_sem.at[slot])

    vocab_load(0, 0).start()

    for k in range(1, plane):
        peer = (spot + k) % plane
        greet(tx=peer // ty_size, ty=peer % ty_size)
    for k in range(1, groups):
        for t in range(tx_size):
            greet(dp=(dp + k) % groups, tx=t)
    pl.semaphore_wait(pltpu.get_barrier_semaphore(), plane - 1 + (groups - 1) * tx_size)

    def cut(slot, p, side, k):
        at = pl.multiple_of(side * (quarter // 2) + k * rows, rows)
        return xs.at[slot, p, pl.ds(at, rows)]

    def crossing(p, k, slot, side):
        at = pl.multiple_of(side * (quarter // 2) + k * rows, rows)
        src = x_ref.at[p, pl.ds(at, rows)]
        return remote(src, cut(slot, p, side, k), x_send.at[p, k], x_recv.at[p, k], ty=across)

    def sideways(p, k, side):
        ref = cut(across, p, side, k)
        return remote(ref, ref, y_send.at[p, k], y_recv.at[p, k], tx=other)

    def inward(p, k, n, slot, side):
        ref = cut(slot, p, side, k)
        return remote(ref, ref, p_send.at[n, p, k], p_recv.at[n, p, k], ty=partner)

    def own_rows(p, slot):
        return remote(x_ref.at[p], xs.at[slot, p], b_send.at[p], b_recv.at[p], ty=partner)

    def cross_step(p, k):
        crossing(p, k, across, tx).wait_recv()
        sideways(p, k, tx).start()
        inward(p, k, 0, across, tx).start()

    def side_step(p, k):
        sideways(p, k, other).wait_recv()
        inward(p, k, 1, across, other).start()

    def far_wait(p):
        for k in range(chunks):
            inward(p, k, 0, far, tx).wait_recv()
            inward(p, k, 1, far, other).wait_recv()

    A, B, Q, R, O = range(5)
    arows = block // plane

    def a_part(g, q):
        return was.at[g, pl.ds(pl.multiple_of(q * arows, arows), arows)]

    slots = [
        lambda g: a_part(g, spot),
        lambda g: wbs.at[g],
        lambda g: wqs.at[g],
        lambda g: wrs.at[g],
        lambda g: woz.at[g],
    ]

    def hop(which, way, step):
        sign = 1 - 2 * way
        g = dp - sign * step
        runs = (g >= 0) & (g < groups) & (dp + sign >= 0) & (dp + sign < groups)
        ref = slots[which](g)
        copy = remote(
            ref, ref, z_send.at[way, which, step], z_recv.at[way, which, step], dp=dp + sign
        )
        return copy, runs

    def arrival(which, way, step):
        sign = 1 - 2 * way
        g = dp - sign * (step + 1)
        ref = slots[which](g)
        copy = remote(
            ref, ref, z_send.at[way, which, step], z_recv.at[way, which, step], dp=dp
        )
        return copy, (g >= 0) & (g < groups)

    inner = (dp > 0) & (dp < groups - 1)

    def start_hop(which):
        for way in range(2):
            copy, runs = hop(which, way, 0)
            pl.when(runs)(copy.start)

    def forward(which, step):
        for way in range(2):
            copy, comes = arrival(which, way, step)
            onward = hop(which, way, step + 1)[0]

            @pl.when(comes & inner)
            def _():
                copy.wait_recv()
                onward.start()

    def take(which, step):
        for way in range(2):
            copy, comes = arrival(which, way, step)
            pl.when(comes & jnp.logical_not(inner))(copy.wait_recv)

    def both(which, step):
        forward(which, step)
        take(which, step)

    def share(n, g):
        diagonal = core == 0
        q = [
            spot, spot, spot, jnp.where(diagonal, tx * ty_size + across, other * ty_size + ty),
            tx * ty_size + across, other * ty_size + ty, other * ty_size + across,
        ][n]
        where = [
            dict(ty=across), dict(tx=other), dict(ty=partner),
            dict(tx=jnp.where(diagonal, other, tx), ty=jnp.where(diagonal, ty, across)),
            dict(ty=partner), dict(ty=partner), dict(ty=partner),
        ][n]
        ref = a_part(g, q)
        return remote(ref, ref, a_send.at[n, g], a_recv.at[n, g], **where)

    def shared(n, g):
        q = [
            tx * ty_size + across, other * ty_size + ty, tx * ty_size + partner,
            other * ty_size + across, tx * ty_size + far, other * ty_size + partner,
            other * ty_size + far,
        ][n]
        ref = a_part(g, q)
        return remote(ref, ref, a_send.at[n, g], a_recv.at[n, g], ty=partner)

    def share_first(g):
        for n in (0, 1, 2):
            share(n, g).start()

    def share_second(g):
        shared(0, g).wait_recv()
        shared(1, g).wait_recv()
        for n in (3, 4, 5):
            share(n, g).start()

    def share_third(g):
        shared(3, g).wait_recv()
        share(6, g).start()

    def share_wait(g):
        for n in (2, 4, 5, 6):
            shared(n, g).wait_recv()

    def arrived(step, act):
        for way in range(2):
            g = dp - (1 - 2 * way) * (step + 1)

            @pl.when((g >= 0) & (g < groups))
            def _():
                act(g)

    for k in range(chunks):
        crossing(0, k, ty, tx).start()
    own_rows(0, ty).start()

    loads[0].wait()
    turned_a = wa_f[...].T
    wide_a = jnp.where(spot % 2 == 0, turned_a[:arows], turned_a[arows:]).astype(jnp.bfloat16)
    here = pl.ds(pl.multiple_of(spot * arows, arows), arows)
    was[dp, here, :LATENT] = wide_a[:, :LATENT]
    twice = (
        lax.broadcasted_iota(jnp.int32, (ROPE, 2 * ROPE), 0)
        == lax.broadcasted_iota(jnp.int32, (ROPE, 2 * ROPE), 1) % ROPE
    ).astype(jnp.bfloat16)
    was[dp, here, LATENT:] = dot32(wide_a[:, LATENT:], twice).astype(jnp.bfloat16)
    start_hop(A)
    loads[1].wait()
    wbs[dp] = wb_f[...].astype(jnp.bfloat16)
    start_hop(B)
    loads[2].wait()
    turned_q = pltpu.roll(wq_f[:, NOPE:], 2 * NOPE - ROPE, 1)
    wqs[dp, :, NOPE:] = turned_q[:, NOPE:].astype(jnp.bfloat16)
    wqs[dp, :, :NOPE] = wq_f[:, :NOPE].astype(jnp.bfloat16)
    start_hop(Q)
    wrs[dp] = turned_q[:, :NOPE].astype(jnp.bfloat16)
    share_first(dp)
    loads[3].wait()
    woz[dp] = wo_f[...].T.astype(jnp.bfloat16)

    def vocab_step(k, _):
        slot = k % 2

        @pl.when(k + 1 < count)
        def _():
            vocab_load(k + 1, 1 - slot).start()

        vocab_load(k, slot).wait()
        cols = pl.ds(pl.multiple_of(k * slab, slab), slab)
        table[:, cols] = stage[slot].astype(jnp.bfloat16)
        return 0

    part_rows = 32

    def norm(slot, prompt):
        def body(i, _):
            at = pl.multiple_of(i * part_rows, part_rows)
            value = normalize(xs[slot, prompt, pl.ds(at, part_rows)], again_ref[...])
            value = value.astype(jnp.bfloat16)
            to = pl.multiple_of(prompt * LEN + slot * quarter + at, part_rows)
            for b in range(groups):
                h[b, pl.ds(to, part_rows)] = value[:, b * block : (b + 1) * block]
            return 0

        lax.fori_loop(0, quarter // part_rows, body, 0)

    span_rows = 512

    def project(g, first):
        own = owner_ref[g]

        def body(i, _):
            at = pl.ds(pl.multiple_of(i * span_rows, span_rows), span_rows)
            rows_in = h[own, at]
            for low, high, weights in ((NOPE, QCOLS, wqs), (QCOLS, QCOLS + ACOLS, was)):
                term = dot32(rows_in, weights[g])
                acc[at, low:high] = term if first else acc[at, low:high] + term
            return 0

        lax.fori_loop(0, LEN // span_rows, body, 0)

    def project_step(step):
        def one(way, _):
            g = dp - (1 - 2 * way) * (step + 1)

            @pl.when((g >= 0) & (g < groups))
            def _():
                share_wait(g)
                project(g, False)

            return 0

        lax.fori_loop(0, 2, one, 0)

    def project_all(p, targets):
        def body(i, _):
            at = pl.ds(pl.multiple_of(p * LEN + i * span_rows, span_rows), span_rows)
            for low, high, weights in targets:
                total = dot32(h[owner_ref[0], at], weights[0])
                for g in range(1, groups):
                    total = total + dot32(h[owner_ref[g], at], weights[g])
                acc[at, low:high] = total
            return 0

        lax.fori_loop(0, LEN // span_rows, body, 0)

    lax.fori_loop(0, 7, vocab_step, 0)
    both(A, 0)
    arrived(0, share_first)
    crossing(1, 0, ty, tx).start()
    own_rows(1, ty).start()
    loads[4].wait()
    norm(ty, 0)
    cross_step(0, 0)
    both(B, 0)
    own_rows(0, partner).wait_recv()
    norm(partner, 0)
    both(Q, 0)
    cross_step(0, 1)
    lax.fori_loop(7, count, vocab_step, 0)
    side_step(0, 0)
    both(A, 1)
    arrived(1, share_first)
    share_second(dp)
    arrived(0, share_second)
    both(B, 1)
    norm(ty, 1)
    side_step(0, 1)
    norm(across, 0)
    share_third(dp)
    arrived(0, share_third)
    far_wait(0)
    norm(far, 0)
    cross_step(1, 0)
    both(Q, 1)
    start_hop(O)
    arrived(1, share_second)
    take(A, 2)
    arrived(2, share_first)
    crossing(1, 1, ty, tx).start()
    share_wait(dp)
    project(dp, True)
    arrived(1, share_third)
    project_step(0)
    forward(O, 0)
    start_hop(R)
    side_step(1, 0)
    arrived(2, share_second)
    project_step(1)
    cross_step(1, 1)
    arrived(2, share_third)
    forward(O, 1)
    own_rows(1, partner).wait_recv()
    norm(partner, 1)

    def stored(b):
        place = jnp.int32(0)
        for g in range(groups):
            place = jnp.where(owner_ref[g] == b, g, place)
        return place

    brows = LATENT // groups

    lane = lax.broadcasted_iota(jnp.int32, (TILE, 2 * ROPE), 1)

    def rotate(values, at):
        swapped = jnp.where(
            lane % ROPE < ROPE // 2,
            pltpu.roll(values, 2 * ROPE - ROPE // 2, 1),
            pltpu.roll(values, ROPE // 2, 1),
        )
        return values * cos_ref[at] + swapped * sin_ref[at]

    factor = (NOPE + ROPE) ** (-0.5) * 1.4426950408889634
    lives = [lengths_ref[deal_ref[dp * per_grp + p]] for p in range(per_grp)]

    def keys(p, tile, _):
        down = acc[pl.ds(pl.multiple_of(p * LEN + tile * TILE, TILE), TILE), QCOLS:]
        to = pl.ds(pl.multiple_of(tile * TILE, TILE), TILE)
        latent = normalize(down[:, :LATENT], lgain_ref[...]).astype(jnp.bfloat16)
        key_rope = rotate(down[:, LATENT:], to).astype(jnp.bfloat16)
        key_val = dot32(latent, wbl[...]).astype(jnp.bfloat16)
        for head in range(heads):
            k_ref[p, head, to, :NOPE] = key_val[:, 2 * head * NOPE : (2 * head + 1) * NOPE]
            k_ref[p, head, to, NOPE:] = key_rope
            v_ref[p, head, to] = key_val[:, (2 * head + 1) * NOPE : (2 * head + 2) * NOPE]
        return 0


    def hears(p, slot, head):
        return heard.at[p, slot * heads + head]

    def heads_of(head, p, tile, slot):
        return remote(
            o_ref.at[head, tile, p], hears(p, tx * ty_size + slot, head),
            o_send.at[head, p, tile], o_recv.at[head, p, slot], ty=tile,
        )

    def passed(head, p, slot, slot_tx, source=None):
        ref = hears(p, slot_tx * ty_size + slot, head)
        return remote(
            ref if source is None else source, ref,
            f_send.at[head, p, slot], f_recv.at[head, p, slot], tx=other,
        )

    def own_passed(head, p, tile):
        return passed(head, p, ty, tx, o_ref.at[head, tile, p])

    def relay(head, p):
        for k in range(1, ty_size):
            slot = (ty + k) % ty_size
            heads_of(head, p, ty, slot).wait_recv()
            passed(head, p, slot, tx).start()

    tile_order = (3, 1, 2, 0)

    def attention(head, p):
        live = jnp.where(p == 0, lives[0], lives[1])
        last = jnp.zeros((1, NOPE), jnp.float32)
        nope_at = (1 - head) * NOPE
        for t in tile_order:
            span = (t + 1) * TILE
            at = pl.ds(pl.multiple_of(p * LEN + t * TILE, TILE), TILE)
            turned = rotate(acc[at, 2 * NOPE : QCOLS], pl.ds(t * TILE, TILE))
            i = lax.broadcasted_iota(jnp.int32, (TILE, span), 0) + t * TILE
            j = lax.broadcasted_iota(jnp.int32, (TILE, span), 1)
            allowed = j <= jnp.minimum(i, live - 1)
            mine = jnp.where(lane // ROPE == 1 - head, turned, 0.0)
            query = jnp.concatenate([acc[at, nope_at : nope_at + NOPE], mine], axis=1)
            score = lax.dot_general(
                query.astype(jnp.bfloat16), k_ref[p, head, :span], (((1,), (1,)), ((), ())),
                preferred_element_type=jnp.float32,
            )
            score = jnp.where(allowed, score, -1e30)
            expo = jnp.exp2((score - jnp.max(score, axis=-1, keepdims=True)) * factor)
            prob = expo * (1.0 / jnp.sum(expo, axis=-1, keepdims=True))
            out = dot32(prob.astype(jnp.bfloat16), v_ref[p, head, :span]).astype(jnp.bfloat16)
            o_ref[head, t, p] = out
            at_last = lax.broadcasted_iota(jnp.int32, (TILE, NOPE), 0) + t * TILE == live - 1
            last = last + jnp.sum(
                jnp.where(at_last, out.astype(jnp.float32), 0.0), axis=0, keepdims=True
            )

            @pl.when(ty == t)
            def _():
                heard[p, spot * heads + head] = out
                own_passed(head, p, t).start()

            @pl.when(ty != t)
            def _():
                heads_of(head, p, t, ty).start()

        for k in range(per_grp):

            @pl.when(p == k)
            def _():
                ends_ref[spot, k : k + 1, head * NOPE : (head + 1) * NOPE] = last

    def wide(j, slot_tx, slot_ty):
        slot = slot_tx * ty_size + slot_ty
        return wos.at[j, pl.ds(pl.multiple_of(slot * piece, piece), piece)]

    def move(n, j, slot_tx, slot_ty, source=None, **where):
        ref = wide(j, slot_tx, slot_ty)
        return remote(
            ref if source is None else source, ref, w_send.at[n, j], w_recv.at[n, j], **where
        )

    early = [jnp.where(dp < groups // 2, k, groups - 1 - k) for k in range(steps)]
    late = jnp.where(dp < groups // 2, groups - 1, 0)

    def aim(g):
        return owner_ref[g] // (groups // tx_size)

    def first_for(side):
        found = early[-1]
        for g in early[-2::-1]:
            found = jnp.where(aim(g) == side, g, found)
        return found

    def first_rows(side):
        found = woz[early[-1]]
        for g in early[-2::-1]:
            found = jnp.where(aim(g) == side, woz[g], found)
        return found

    def second_for(side):
        found = late
        for g in early:
            found = jnp.where((aim(g) == side) & (g != first_for(side)), g, found)
        return found

    mine_at = pl.ds(pl.multiple_of(spot * piece, piece), piece)

    def spread(j, give_rows, keep_rows):
        give[j] = give_rows
        move(0, j, tx, ty, give.at[j], tx=other).start()
        wos[j, mine_at] = keep_rows
        move(1, j, tx, ty, ty=across).start()
        move(2, j, tx, ty, ty=partner).start()

    def spread_on(j):
        move(0, j, other, ty, tx=other).wait_recv()
        move(3, j, other, ty, ty=across).start()
        move(4, j, other, ty, ty=partner).start()

    def spread_in(j):
        move(1, j, tx, across, ty=across).wait_recv()
        move(5, j, tx, across, ty=partner).start()

    def spread_last(j):
        move(3, j, other, across, ty=across).wait_recv()
        move(6, j, other, across, ty=partner).start()

    def first_head(p, _):
        @pl.when(p == 0)
        def _():
            take(B, 2)
            take(Q, 2)
            project_step(2)
            for b in range(groups):
                wbl[b * brows : (b + 1) * brows] = wbs[stored(b)]

        @pl.when(p == 1)
        def _():
            side_step(1, 1)
            norm(across, 1)
            far_wait(1)
            norm(far, 1)
            relay(0, 0)
            project_all(1, ((NOPE, QCOLS, wqs), (QCOLS, QCOLS + ACOLS, was)))
            take(O, 0)
            take(O, 1)
            spread(0, first_rows(other), first_rows(tx))

        lax.fori_loop(0, LEN // TILE, functools.partial(keys, p), 0)
        attention(0, p)
        pl.when(p == 0)(lambda: forward(R, 0))
        return 0

    lax.fori_loop(0, per_grp, first_head, 0)
    forward(R, 1)
    take(O, 2)
    spread(1, woz[second_for(other)], woz[second_for(tx)])
    relay(0, 1)
    spread_on(0)
    spread_in(0)
    for step in range(steps):
        take(R, step)

    def second_head(p, _):
        project_all(p, ((0, NOPE, wrs),))
        attention(1, p)

        @pl.when(p == 0)
        def _():
            spread_on(1)
            spread_in(1)

        @pl.when(p == 1)
        def _():
            relay(1, 0)

        return 0

    lax.fori_loop(0, per_grp, second_head, 0)

    def row_of(k, slot):
        peer = (spot + k) % plane
        return remote(
            ends_ref.at[spot], ends_ref.at[slot], e_send.at[k], e_recv.at[k],
            tx=peer // ty_size, ty=peer % ty_size,
        )

    for k in range(1, plane):
        row_of(k, spot).start()
    relay(1, 1)
    for j in range(2):
        spread_last(j)
    for head in range(heads):
        for p in range(per_grp):
            for k in range(ty_size):
                passed(head, p, (ty + k) % ty_size, other).wait_recv()
    for p in range(per_grp):
        for n in range(plane * heads):
            mixed[p, :, n * NOPE : (n + 1) * NOPE] = heard[p, n]
    for p in range(per_grp):
        tile = (lives[p] - 1) // quarter
        inside = lax.broadcasted_iota(jnp.int32, (quarter, half), 0) + tile * quarter
        tokens = xs[jnp.maximum(tile, 0), p, :, pl.ds(pl.multiple_of(tx * half, half), half)]
        base_ref[p : p + 1] = jnp.sum(
            jnp.where(inside == lives[p] - 1, tokens.astype(jnp.float32), 0.0),
            axis=0, keepdims=True,
        )
    for k in range(1, plane):
        row_of(k, (spot + plane - k) % plane).wait_recv()
    line_ref[...] = jnp.zeros_like(line_ref)
    for slot in range(plane):
        line_ref[0:per_grp, slot * piece : (slot + 1) * piece] = ends_ref[slot]
    for j in range(2):
        move(2, j, tx, partner, ty=partner).wait_recv()
        move(4, j, other, partner, ty=partner).wait_recv()
        move(5, j, tx, far, ty=partner).wait_recv()
        move(6, j, other, far, ty=partner).wait_recv()

    spots = [jnp.where(owner_ref[first_for(tx)] % 2 == i, 0, 1) for i in range(2)]
    chosen = line_ref[...].astype(jnp.bfloat16)
    peers = groups * tx_size
    place = dp * tx_size + tx
    for i in range(2):
        cols = slice(i * block, (i + 1) * block)
        value = base_ref[:, cols] + dot32(chosen, wos[spots[i]])[:per_grp]
        full[place, :, cols] = value.astype(jnp.bfloat16).astype(jnp.float32)

    def along_peers(k, slot):
        peer = (place + k) % peers
        return remote(
            full.at[place], full.at[slot], r_send.at[k], r_recv.at[k],
            dp=peer // tx_size, tx=peer % tx_size,
        )

    for k in range(1, peers):
        along_peers(k, place).start()

    strip = 256

    def out_step(n, _):
        for i in range(2):

            @pl.when(n // 2 == i)
            def _():
                inside = pl.ds(pl.multiple_of((n % 2) * strip, strip), strip)
                cols = pl.ds(pl.multiple_of(n * strip, strip), strip)
                model = pl.ds(pl.multiple_of(tx * half + n * strip, strip), strip)
                for p in range(per_grp):
                    total = dot32(mixed[p], wos[spots[i], :, inside])
                    hidden_ref[p, :, cols] = (
                        xs[ty, p, :, model].astype(jnp.float32) + total
                    ).astype(jnp.bfloat16)

        return 0

    lax.fori_loop(0, 4, out_step, 0)

    for k in range(1, peers):
        along_peers(k, (place + peers - k) % peers).wait_recv()
    for g in range(groups):
        for t in range(tx_size):
            rows_ref[g * per_grp : (g + 1) * per_grp, t * half : (t + 1) * half] = full[
                g * tx_size + t
            ]
    final = normalize(rows_ref[...], fgain_ref[...])
    owner = owner_ref[dp]
    mine = jnp.zeros((groups * per_grp, block), jnp.float32)
    for g in range(groups):
        mine = jnp.where(owner == g, final[:, g * block : (g + 1) * block], mine)
    mine = mine.astype(jnp.bfloat16)

    def logit_step(k, _):
        cols = pl.ds(pl.multiple_of(k * slab, slab), slab)
        logits = dot32(mine, table[:, cols])
        for g in range(groups):
            part[g, :, cols] = logits[g * per_grp : (g + 1) * per_grp]
        return 0

    parts = 2
    share_words = words // parts

    def along_dp(n, k, slot):
        peer = (dp + k) % groups
        cols = pl.ds(n * share_words, share_words)
        return remote(
            part.at[peer, :, cols], incoming.at[slot, :, cols], l_send.at[n, k], l_recv.at[n, k],
            dp=peer,
        )

    for n in range(parts):
        lax.fori_loop(n * count // parts, (n + 1) * count // parts, logit_step, 0)
        for k in range(1, groups):
            along_dp(n, k, dp).start()
    for n in range(parts):
        cols = slice(n * share_words, (n + 1) * share_words)
        total = part[dp, :, cols]
        for k in range(1, groups):
            slot = (dp + groups - k) % groups
            along_dp(n, k, slot).wait_recv()
            total = total + incoming[slot, :, cols]
        out_ref[:, cols] = total

    for p in range(per_grp):
        for k in range(chunks):
            crossing(p, k, ty, tx).wait_send()
            sideways(p, k, tx).wait_send()
            inward(p, k, 0, across, tx).wait_send()
            inward(p, k, 1, across, other).wait_send()
        own_rows(p, ty).wait_send()
    for step in range(steps):
        for which in range(5):
            for way in range(2):
                copy, runs = hop(which, way, step)
                pl.when(runs)(copy.wait_send)
    for g in range(groups):
        for n in range(7):
            share(n, g).wait_send()
    for head in range(heads):
        for p in range(per_grp):
            own_passed(head, p, ty).wait_send()
            for k in range(1, ty_size):
                slot = (ty + k) % ty_size
                heads_of(head, p, slot, ty).wait_send()
                passed(head, p, slot, tx).wait_send()
    for j in range(2):
        move(0, j, tx, ty, give.at[j], tx=other).wait_send()
        move(1, j, tx, ty, ty=across).wait_send()
        move(2, j, tx, ty, ty=partner).wait_send()
        move(3, j, other, ty, ty=across).wait_send()
        move(4, j, other, ty, ty=partner).wait_send()
        move(5, j, tx, across, ty=partner).wait_send()
        move(6, j, other, across, ty=partner).wait_send()
    for k in range(1, plane):
        row_of(k, spot).wait_send()
    for k in range(1, peers):
        along_peers(k, place).wait_send()
    for n in range(parts):
        for k in range(1, groups):
            along_dp(n, k, dp).wait_send()


def hand_on_kernel(hidden_ref, logits_ref, hidden_out, logits_out, held, words, reads, writes):
    parts = [(hidden_ref.at[p], held.at[p], hidden_out.at[p]) for p in range(held.shape[0])]
    parts.append((logits_ref, words, logits_out))
    inward = [
        pltpu.make_async_copy(source, there, reads.at[n])
        for n, (source, there, _) in enumerate(parts)
    ]
    outward = [
        pltpu.make_async_copy(there, target, writes.at[n])
        for n, (_, there, target) in enumerate(parts)
    ]
    for copy in inward:
        copy.start()
    for first, second in zip(inward, outward):
        first.wait()
        second.start()
    for copy in outward:
        copy.wait()


def hand_on(hidden, logits):
    hbm = pl.BlockSpec(memory_space=pl.ANY)
    return pl.pallas_call(
        hand_on_kernel,
        in_specs=[hbm, hbm],
        out_specs=[hbm, hbm],
        out_shape=[
            jax.ShapeDtypeStruct(hidden.shape, hidden.dtype),
            jax.ShapeDtypeStruct(logits.shape, logits.dtype),
        ],
        scratch_shapes=[
            pltpu.VMEM(hidden.shape, hidden.dtype),
            pltpu.VMEM(logits.shape, logits.dtype),
            pltpu.SemaphoreType.DMA((hidden.shape[0] + 1,)),
            pltpu.SemaphoreType.DMA((hidden.shape[0] + 1,)),
        ],
    )(hidden, logits)


def layer(groups, owner, lengths, deal, x, again, lgain, fgain, wq, wa, wb, wo, vocab):
    per_grp, quarter, width = x.shape
    block, words = vocab.shape
    half = width // 2
    piece = 2 * NOPE
    slab = 512
    steps = groups - 1
    peers = 2 * groups
    position = np.arange(LEN, dtype=np.float32)
    frequency = np.power(
        np.float32(10000.0), -np.arange(ROPE // 2, dtype=np.float32) / np.float32(ROPE // 2)
    ).astype(np.float32)
    angles = (position[:, None] * frequency).astype(np.float32).astype(np.float64)
    cosine, sine = np.cos(angles), np.sin(angles)
    cosine = jnp.asarray(np.concatenate([cosine] * 4, axis=1).astype(np.float32))
    sine = jnp.asarray(np.concatenate([-sine, sine, -sine, sine], axis=1).astype(np.float32))
    dma = pltpu.SemaphoreType.DMA
    vmem = pl.BlockSpec(memory_space=pltpu.VMEM)
    smem = pl.BlockSpec(memory_space=pltpu.SMEM)
    hbm = pl.BlockSpec(memory_space=pl.ANY)
    bf16 = lambda *dims: pltpu.VMEM(dims, jnp.bfloat16)
    f32 = lambda *dims: pltpu.VMEM(dims, jnp.float32)
    return pl.pallas_call(
        functools.partial(layer_kernel, groups),
        in_specs=[smem, smem, smem, hbm, vmem, vmem, vmem, vmem, vmem, hbm, hbm, hbm, hbm, hbm],
        out_specs=[vmem, vmem],
        out_shape=[
            jax.ShapeDtypeStruct((per_grp, quarter, half), jnp.bfloat16),
            jax.ShapeDtypeStruct((per_grp, words), jnp.float32),
        ],
        scratch_shapes=[
            bf16(4, per_grp, quarter, width),
            bf16(groups, per_grp * LEN, block),
            bf16(groups, block, NOPE),
            bf16(groups, block, 2 * NOPE),
            bf16(groups, block, ACOLS),
            bf16(groups, LATENT // groups, 2 * piece),
            bf16(LATENT, 2 * piece),
            bf16(groups, piece, block),
            bf16(2, piece, block),
            bf16(2, 8 * piece, block),
            f32(per_grp * LEN, QCOLS + ACOLS),
            bf16(per_grp, 2, LEN, 2 * NOPE),
            bf16(per_grp, 2, LEN, NOPE),
            bf16(2, 4, per_grp, TILE, NOPE),
            bf16(per_grp, 16, TILE, NOPE),
            bf16(per_grp, TILE, 8 * piece),
            bf16(block, words),
            f32(2, block, slab),
            f32(*wq.shape),
            f32(wa.shape[1], block // 4),
            f32(*wb.shape),
            f32(block, piece),
            f32(8, per_grp, piece),
            f32(per_grp, half),
            f32(8, width),
            f32(peers, per_grp, half),
            f32(groups * per_grp, width),
            f32(groups, per_grp, words),
            f32(groups, per_grp, words),
            dma((5,)), dma((2,)),
            dma((per_grp, 2)), dma((per_grp, 2)), dma((per_grp, 2)), dma((per_grp, 2)),
            dma((2, per_grp, 2)), dma((2, per_grp, 2)), dma((per_grp,)), dma((per_grp,)),
            dma((2, 5, steps)), dma((2, 5, steps)), dma((7, groups)), dma((7, groups)),
            dma((2, per_grp, 4)), dma((2, per_grp, 4)), dma((2, per_grp, 4)),
            dma((2, per_grp, 4)), dma((7, 2)), dma((7, 2)),
            dma((8,)), dma((8,)), dma((peers,)), dma((peers,)), dma((2, groups)),
            dma((2, groups)),
        ],
        compiler_params=pltpu.CompilerParams(
            collective_id=0, has_side_effects=True, vmem_limit_bytes=60 * 1024 * 1024
        ),
        cost_estimate=pl.CostEstimate(
            flops=16_000_000_000, bytes_accessed=24_000_000, transcendentals=3_000_000
        ),
    )(owner, lengths, deal, x, again, lgain, fgain, cosine, sine, wq, wa.T, wb, wo, vocab)


def load_vocab(vocab_chunk, vocab_ref, table, v_sem):
    loads = []
    for k in range(vocab_ref.shape[1] // vocab_chunk):
        cols = pl.ds(k * vocab_chunk, vocab_chunk)
        loads.append(
            pltpu.make_async_copy(vocab_ref.at[:, cols], table.at[:, cols], v_sem.at[k])
        )
        loads[-1].start()
    return loads


def next_token(
    groups, tx_size, ty_size, vocab_chunk, loads, owner_ref, picked_ref, gain_ref, out_ref, seen, full,
    rows_ref, table, part, incoming, t_send, t_recv, r_send, r_recv, l_send, l_recv,
):
    dp, tx, ty = lax.axis_index("dp"), lax.axis_index("tx"), lax.axis_index("ty")
    per_grp, half = picked_ref.shape
    block = table.shape[0]
    peers = groups * tx_size
    place = dp * tx_size + tx
    count = len(loads)

    def along_ty(k, slot):
        return remote(
            picked_ref, seen.at[slot], t_send.at[k], t_recv.at[k], ty=(ty + k) % ty_size
        )

    for k in range(1, ty_size):
        along_ty(k, ty).start()
    merged = picked_ref[...]
    for k in range(1, ty_size):
        slot = (ty + ty_size - k) % ty_size
        along_ty(k, slot).wait_recv()
        merged = merged + seen[slot]
    full[place] = merged

    def along_peers(k, slot):
        peer = (place + k) % peers
        return remote(
            full.at[place], full.at[slot], r_send.at[k], r_recv.at[k],
            dp=peer // tx_size, tx=peer % tx_size,
        )

    for k in range(1, peers):
        along_peers(k, place).start()
    for k in range(1, peers):
        along_peers(k, (place + peers - k) % peers).wait_recv()
    for g in range(groups):
        for t in range(tx_size):
            rows_ref[g * per_grp : (g + 1) * per_grp, t * half : (t + 1) * half] = full[
                g * tx_size + t
            ]
    final = normalize(rows_ref[...], gain_ref[...])
    owner = owner_ref[dp]
    mine = jnp.zeros((groups * per_grp, block), jnp.float32)
    for g in range(groups):
        mine = jnp.where(owner == g, final[:, g * block : (g + 1) * block], mine)
    mine = mine.astype(jnp.bfloat16)
    for k in range(count):
        loads[k].wait()
        cols = slice(k * vocab_chunk, (k + 1) * vocab_chunk)
        logits = dot32(mine, table[:, cols].astype(jnp.bfloat16))
        for g in range(groups):
            part[g, :, cols] = logits[g * per_grp : (g + 1) * per_grp]

    def along_dp(k, slot):
        peer = (dp + k) % groups
        return remote(part.at[peer], incoming.at[slot], l_send.at[k], l_recv.at[k], dp=peer)

    for k in range(1, groups):
        along_dp(k, dp).start()
    total = part[dp]
    for k in range(1, groups):
        slot = (dp + groups - k) % groups
        along_dp(k, slot).wait_recv()
        total = total + incoming[slot]
    out_ref[...] = total
    for k in range(1, ty_size):
        along_ty(k, ty).wait_send()
    for k in range(1, peers):
        along_peers(k, place).wait_send()
    for k in range(1, groups):
        along_dp(k, dp).wait_send()


def tail_kernel(
    groups, tx_size, ty_size, vocab_chunk, owner_ref, picked_ref, gain_ref, vocab_ref, out_ref,
    seen, full, rows_ref, table, part, incoming, t_send, t_recv, r_send, r_recv, l_send, l_recv,
    v_sem,
):
    dp, tx, ty = lax.axis_index("dp"), lax.axis_index("tx"), lax.axis_index("ty")
    peers = groups * tx_size
    place = dp * tx_size + tx
    loads = load_vocab(vocab_chunk, vocab_ref, table, v_sem)
    for k in range(1, ty_size):
        greet(ty=(ty + k) % ty_size)
    for k in range(1, peers):
        peer = (place + k) % peers
        greet(dp=peer // tx_size, tx=peer % tx_size)
    pl.semaphore_wait(pltpu.get_barrier_semaphore(), ty_size + peers - 2)
    next_token(
        groups, tx_size, ty_size, vocab_chunk, loads, owner_ref, picked_ref, gain_ref, out_ref,
        seen, full, rows_ref, table, part, incoming, t_send, t_recv, r_send, r_recv, l_send,
        l_recv,
    )


def tail(groups, tx_size, ty_size, owner, picked, gain, vocab):
    per_grp, half = picked.shape
    block, words = vocab.shape
    vocab_chunk = 512
    peers = groups * tx_size
    dma = pltpu.SemaphoreType.DMA
    vmem = pl.BlockSpec(memory_space=pltpu.VMEM)
    return pl.pallas_call(
        functools.partial(tail_kernel, groups, tx_size, ty_size, vocab_chunk),
        in_specs=[
            pl.BlockSpec(memory_space=pltpu.SMEM), vmem, vmem, pl.BlockSpec(memory_space=pl.ANY),
        ],
        out_specs=vmem,
        out_shape=jax.ShapeDtypeStruct((per_grp, words), jnp.float32),
        scratch_shapes=[
            pltpu.VMEM((ty_size, per_grp, half), jnp.float32),
            pltpu.VMEM((peers, per_grp, half), jnp.float32),
            pltpu.VMEM((groups * per_grp, half * tx_size), jnp.float32),
            pltpu.VMEM((block, words), jnp.float32),
            pltpu.VMEM((groups, per_grp, words), jnp.float32),
            pltpu.VMEM((groups, per_grp, words), jnp.float32),
            dma((ty_size,)), dma((ty_size,)), dma((peers,)), dma((peers,)),
            dma((groups,)), dma((groups,)), dma((words // vocab_chunk,)),
        ],
        compiler_params=pltpu.CompilerParams(
            collective_id=1, has_side_effects=True, vmem_limit_bytes=40 * 1024 * 1024
        ),
        cost_estimate=pl.CostEstimate(
            flops=100_000_000, bytes_accessed=16_000_000, transcendentals=0
        ),
    )(owner, picked, gain, vocab)


def rotate_half(values, position):
    half_dim = values.shape[-1] // 2
    frequency = 10000.0 ** (-jnp.arange(half_dim, dtype=jnp.float32) / half_dim)
    angles = position.astype(jnp.float32)[..., None] * frequency
    cosine = jnp.cos(angles)
    sine = jnp.sin(angles)
    first_half = values[..., :half_dim]
    second_half = values[..., half_dim:]
    return jnp.concatenate(
        [first_half * cosine - second_half * sine, first_half * sine + second_half * cosine],
        axis=-1,
    )


def split_positions(
    inputs, inverse, live_len, attn_gain, latent_gain, w_query, w_down_kv, w_up_kv, w_out
):
    groups = lax.axis_size("dp")

    def arrange(gathered):
        block_rows = gathered.shape[0] // groups
        return jnp.concatenate(
            [
                lax.dynamic_slice_in_dim(gathered, inverse[g] * block_rows, block_rows, 0)
                for g in range(groups)
            ],
            axis=0,
        )

    query_w, down_w, up_w, out_w = (
        lax.all_gather(w_query.astype(jnp.bfloat16), "dp", axis=0, tiled=True),
        lax.all_gather(w_down_kv.astype(jnp.bfloat16), "dp", axis=0, tiled=True),
        lax.all_gather(w_up_kv.astype(jnp.bfloat16), "dp", axis=0, tiled=True),
        lax.all_gather(w_out.astype(jnp.bfloat16), "dp", axis=0, tiled=True),
    )
    query_w = arrange(query_w)
    down_w = arrange(down_w)
    up_w = arrange(up_w)
    out_w = arrange(out_w)
    query_w, up_w = (
        lax.all_gather(query_w, "ty", axis=1, tiled=True),
        lax.all_gather(up_w, "ty", axis=1, tiled=True),
    )
    per_grp, quarter, width = inputs.shape
    heads = query_w.shape[1] // (NOPE + ROPE)
    position = lax.axis_index("ty") * quarter + jnp.arange(quarter, dtype=jnp.int32)
    flat_rows = inputs.reshape(per_grp * quarter, width)
    normed = normalize(flat_rows, attn_gain).astype(jnp.bfloat16)
    queries = jnp.dot(normed, query_w, preferred_element_type=jnp.float32).reshape(
        per_grp, quarter, heads, NOPE + ROPE
    )
    queries = jnp.concatenate(
        [queries[..., :NOPE], rotate_half(queries[..., NOPE:], position[None, :, None])], axis=-1
    ).astype(jnp.bfloat16)
    down_proj = jnp.dot(normed, down_w, preferred_element_type=jnp.float32).reshape(
        per_grp, quarter, LATENT + ROPE
    )
    latent = normalize(down_proj[..., :LATENT], latent_gain).astype(jnp.bfloat16)
    key_rope = rotate_half(down_proj[..., LATENT:], position[None, :]).astype(jnp.bfloat16)
    gathered = lax.all_gather(
        jnp.concatenate([latent, key_rope], axis=-1), "ty", axis=1, tiled=True
    )
    key_val = jnp.dot(gathered[..., :LATENT], up_w, preferred_element_type=jnp.float32).astype(
        jnp.bfloat16
    )
    rope_all = gathered[..., LATENT:]
    key_val = key_val.reshape(per_grp, LEN, heads, 2, NOPE)
    key_nope = key_val[:, :, :, 0]
    values = key_val[:, :, :, 1]
    score_scale = (NOPE + ROPE) ** (-0.5)
    scores = (
        jnp.einsum(
            "pqhd,pkhd->phqk", queries[..., :NOPE], key_nope, preferred_element_type=jnp.float32
        )
        + jnp.einsum(
            "pqhd,pkd->phqk", queries[..., NOPE:], rope_all, preferred_element_type=jnp.float32
        )
    ) * score_scale
    key_pos = jnp.arange(LEN, dtype=jnp.int32)
    allowed = (key_pos[None, None, :] <= position[None, :, None]) & (
        key_pos[None, None, :] < live_len[:, None, None]
    )
    scores = jnp.where(allowed[:, None], scores, -1e30)
    top = jnp.max(scores, axis=-1, keepdims=True)
    expo = jnp.exp(scores - top)
    softmax_w = (expo / jnp.sum(expo, axis=-1, keepdims=True)).astype(jnp.bfloat16)
    attended = jnp.einsum(
        "phqk,pkhd->pqhd", softmax_w, values, preferred_element_type=jnp.float32
    ).astype(jnp.bfloat16)
    attended = attended.reshape(per_grp * quarter, heads * NOPE)
    own_width = width // lax.axis_size("tx")
    col_start = lax.axis_index("tx") * own_width
    partial_value = lax.dot_general(
        attended, out_w, (((1,), (1,)), ((), ())), preferred_element_type=jnp.float32
    ).reshape(per_grp, quarter, width)
    summed = lax.psum_scatter(partial_value, "tx", scatter_dimension=2, tiled=True)
    residual = lax.dynamic_slice_in_dim(inputs, col_start, own_width, 2)
    layer_out = (residual.astype(jnp.float32) + summed).astype(jnp.bfloat16)
    return layer_out


def shards(
    inputs,
    lengths,
    prompt_deal,
    block_owner,
    attn_gain,
    latent_gain,
    final_gain,
    w_query,
    w_down_kv,
    w_up_kv,
    w_out,
    w_vocab,
):
    groups = lax.axis_size("dp")
    dp, tx, ty = lax.axis_index("dp"), lax.axis_index("tx"), lax.axis_index("ty")
    per_grp, quarter, width = inputs.shape
    half = width // lax.axis_size("tx")
    whole_heads = w_query.shape[1] == QCOLS and w_up_kv.shape[1] == 4 * NOPE
    here = whole_heads and (lax.axis_size("tx"), lax.axis_size("ty"), per_grp) == (2, 4, 2)
    if here and groups == 4 and (quarter, width) == (TILE, 4 * w_query.shape[0]):
        return hand_on(
            *layer(
                groups, block_owner, lengths, prompt_deal, inputs, attn_gain[None],
                latent_gain[None], final_gain[None], w_query, w_down_kv, w_up_kv, w_out, w_vocab,
            )
        )

    order = jnp.arange(groups, dtype=jnp.int32)
    inverse = jnp.sum(
        jnp.where(block_owner[None, :] == order[:, None], order[None, :], 0), axis=1
    ).astype(jnp.int32)
    slots = dp * per_grp + jnp.arange(per_grp, dtype=jnp.int32)
    names = jnp.arange(lengths.shape[0], dtype=jnp.int32)

    def at_index(values, index):
        return jnp.sum(jnp.where(names[None] == index[:, None], values[None], 0), axis=1)

    live_len = at_index(lengths, at_index(prompt_deal, slots))
    layer_out = split_positions(
        inputs, inverse, live_len, attn_gain, latent_gain, w_query, w_down_kv, w_up_kv, w_out
    )

    at = live_len - 1 - ty * quarter
    picked = jnp.stack(
        [
            lax.dynamic_slice(
                layer_out, (i, jnp.clip(at[i], 0, quarter - 1), 0), (1, 1, half)
            ).reshape(half)
            for i in range(per_grp)
        ]
    ).astype(jnp.float32)
    inside = (at >= 0) & (at < quarter)
    picked = jnp.where(inside[:, None], picked, 0.0)
    logits = tail(
        groups, lax.axis_size("tx"), lax.axis_size("ty"), block_owner, picked, final_gain[None],
        w_vocab,
    )
    return (layer_out, logits)


def solution(mesh):
    placed = (
        P("dp", "ty", None),
        P(),
        P(),
        P(),
        P(),
        P(),
        P(),
        P("dp", ("tx", "ty")),
        P("dp", None),
        P("dp", ("tx", "ty")),
        P("dp", "tx"),
        P("dp", ("tx", "ty")),
    )
    return jax.shard_map(
        shards,
        mesh=mesh,
        in_specs=placed,
        out_specs=(P("dp", "ty", "tx"), P("dp", ("tx", "ty"))),
        check_vma=False,
    )
```

```python
import functools

import jax
import jax.numpy as jnp
import numpy as np
from jax import lax
from jax.experimental import pallas as pl
from jax.experimental.pallas import tpu as pltpu
from jax.sharding import PartitionSpec as P

NOPE = 128
ROPE = 64
LATENT = 512
LEN = 1024
TILE = 256
EPS = 1e-06
QCOLS = 384
ACOLS = 640


def normalize(values, gain):
    wide = values.astype(jnp.float32)
    return wide * lax.rsqrt(jnp.mean(wide * wide, axis=-1, keepdims=True) + EPS) * gain


def dot32(left, right):
    return jnp.dot(left, right, preferred_element_type=jnp.float32)


def remote(src, dst, send, recv, **where):
    return pltpu.make_async_remote_copy(
        src_ref=src,
        dst_ref=dst,
        send_sem=send,
        recv_sem=recv,
        device_id=where,
        device_id_type=pl.DeviceIdType.MESH,
    )


def greet(**where):
    pl.semaphore_signal(
        pltpu.get_barrier_semaphore(),
        inc=1,
        device_id=where,
        device_id_type=pl.DeviceIdType.MESH,
    )


def layer_kernel(
    groups, owner_ref, lengths_ref, deal_ref, x_ref, again_ref, lgain_ref, fgain_ref, cos_ref,
    sin_ref, wq_ref, wa_ref, wb_ref, wo_ref, vocab_ref, hidden_ref, out_ref,
    xs, h, wrs, wqs, was, wbs, wbl, woz, give, wos, acc, k_ref, v_ref, o_ref, heard, mixed, table, stage,
    wq_f, wa_f, wb_f, wo_f, ends_ref, base_ref, line_ref, full, rows_ref, part, incoming,
    local, v_sem, x_send, x_recv, y_send, y_recv, p_send, p_recv, b_send, b_recv,
    z_send, z_recv, a_send, a_recv, o_send, o_recv, f_send, f_recv, w_send, w_recv,
    e_send, e_recv, r_send, r_recv, l_send, l_recv,
):
    dp, tx, ty = lax.axis_index("dp"), lax.axis_index("tx"), lax.axis_index("ty")
    tx_size, ty_size = 2, 4
    per_grp = 2
    core = ty % 2
    partner = ty + 1 - 2 * core
    across = (ty + 2) % 4
    far = (partner + 2) % 4
    other = 1 - tx
    spot = tx * ty_size + ty
    plane = tx_size * ty_size
    steps = groups - 1
    chunks = 4
    quarter, width = x_ref.shape[1], x_ref.shape[2]
    half = width // tx_size
    block = width // groups
    rows = quarter // (2 * chunks)
    words = vocab_ref.shape[1]
    slab = stage.shape[-1]
    count = words // slab
    piece = 2 * NOPE
    heads = 2

    loads = [
        pltpu.make_async_copy(wa_ref.at[:, pl.ds(pl.multiple_of((spot // 2) * 128, 128), 128)], wa_f, local.at[0]),
        pltpu.make_async_copy(wb_ref, wb_f, local.at[1]),
        pltpu.make_async_copy(wq_ref, wq_f, local.at[2]),
        pltpu.make_async_copy(
            wo_ref.at[:, pl.ds(pl.multiple_of(ty * piece, piece), piece)], wo_f, local.at[3]
        ),
        pltpu.make_async_copy(x_ref, xs.at[ty], local.at[4]),
    ]
    for load in loads:
        load.start()

    def vocab_load(k, slot):
        cols = pl.ds(pl.multiple_of(k * slab, slab), slab)
        return pltpu.make_async_copy(vocab_ref.at[:, cols], stage.at[slot], v_sem.at[slot])

    vocab_load(0, 0).start()

    for k in range(1, plane):
        peer = (spot + k) % plane
        greet(tx=peer // ty_size, ty=peer % ty_size)
    for k in range(1, groups):
        for t in range(tx_size):
            greet(dp=(dp + k) % groups, tx=t)
    pl.semaphore_wait(pltpu.get_barrier_semaphore(), plane - 1 + (groups - 1) * tx_size)

    def cut(slot, p, side, k):
        at = pl.multiple_of(side * (quarter // 2) + k * rows, rows)
        return xs.at[slot, p, pl.ds(at, rows)]

    def crossing(p, k, slot, side):
        at = pl.multiple_of(side * (quarter // 2) + k * rows, rows)
        src = x_ref.at[p, pl.ds(at, rows)]
        return remote(src, cut(slot, p, side, k), x_send.at[p, k], x_recv.at[p, k], ty=across)

    def sideways(p, k, side):
        ref = cut(across, p, side, k)
        return remote(ref, ref, y_send.at[p, k], y_recv.at[p, k], tx=other)

    def inward(p, k, n, slot, side):
        ref = cut(slot, p, side, k)
        return remote(ref, ref, p_send.at[n, p, k], p_recv.at[n, p, k], ty=partner)

    def own_rows(p, slot):
        return remote(x_ref.at[p], xs.at[slot, p], b_send.at[p], b_recv.at[p], ty=partner)

    def cross_start(p, n):
        for k in (2 * n, 2 * n + 1):
            crossing(p, k, ty, tx).start()

    def cross_step(p, n):
        for k in (2 * n, 2 * n + 1):
            crossing(p, k, across, tx).wait_recv()
            sideways(p, k, tx).start()
            inward(p, k, 0, across, tx).start()

    def side_step(p, n):
        for k in (2 * n, 2 * n + 1):
            sideways(p, k, other).wait_recv()
            inward(p, k, 1, across, other).start()

    def far_wait(p):
        for k in range(chunks):
            inward(p, k, 0, far, tx).wait_recv()
            inward(p, k, 1, far, other).wait_recv()

    A, B, Q, R, O = range(5)
    arows = block // plane

    def a_part(g, q):
        return was.at[g, pl.ds(pl.multiple_of(q * arows, arows), arows)]

    slots = [
        lambda g: a_part(g, spot),
        lambda g: wbs.at[g],
        lambda g: wqs.at[g],
        lambda g: wrs.at[g],
        lambda g: woz.at[g],
    ]

    def hop(which, way, step):
        sign = 1 - 2 * way
        g = dp - sign * step
        runs = (g >= 0) & (g < groups) & (dp + sign >= 0) & (dp + sign < groups)
        ref = slots[which](g)
        copy = remote(
            ref, ref, z_send.at[way, which, step], z_recv.at[way, which, step], dp=dp + sign
        )
        return copy, runs

    def arrival(which, way, step):
        sign = 1 - 2 * way
        g = dp - sign * (step + 1)
        ref = slots[which](g)
        copy = remote(
            ref, ref, z_send.at[way, which, step], z_recv.at[way, which, step], dp=dp
        )
        return copy, (g >= 0) & (g < groups)

    inner = (dp > 0) & (dp < groups - 1)

    def start_hop(which):
        for way in range(2):
            copy, runs = hop(which, way, 0)
            pl.when(runs)(copy.start)

    def forward(which, step):
        for way in range(2):
            copy, comes = arrival(which, way, step)
            onward = hop(which, way, step + 1)[0]

            @pl.when(comes & inner)
            def _():
                copy.wait_recv()
                onward.start()

    def take(which, step):
        for way in range(2):
            copy, comes = arrival(which, way, step)
            pl.when(comes & jnp.logical_not(inner))(copy.wait_recv)

    def both(which, step):
        forward(which, step)
        take(which, step)

    def share(n, g):
        diagonal = core == 0
        q = [
            spot, spot, spot, jnp.where(diagonal, tx * ty_size + across, other * ty_size + ty),
            tx * ty_size + across, other * ty_size + ty, other * ty_size + across,
        ][n]
        where = [
            dict(ty=across), dict(tx=other), dict(ty=partner),
            dict(tx=jnp.where(diagonal, other, tx), ty=jnp.where(diagonal, ty, across)),
            dict(ty=partner), dict(ty=partner), dict(ty=partner),
        ][n]
        ref = a_part(g, q)
        return remote(ref, ref, a_send.at[n, g], a_recv.at[n, g], **where)

    def shared(n, g):
        q = [
            tx * ty_size + across, other * ty_size + ty, tx * ty_size + partner,
            other * ty_size + across, tx * ty_size + far, other * ty_size + partner,
            other * ty_size + far,
        ][n]
        ref = a_part(g, q)
        return remote(ref, ref, a_send.at[n, g], a_recv.at[n, g], ty=partner)

    def share_first(g):
        for n in (0, 1, 2):
            share(n, g).start()

    def share_second(g):
        shared(0, g).wait_recv()
        shared(1, g).wait_recv()
        for n in (3, 4, 5):
            share(n, g).start()

    def share_third(g):
        shared(3, g).wait_recv()
        share(6, g).start()

    def share_wait(g):
        for n in (2, 4, 5, 6):
            shared(n, g).wait_recv()

    def arrived(step, act):
        for way in range(2):
            g = dp - (1 - 2 * way) * (step + 1)

            @pl.when((g >= 0) & (g < groups))
            def _():
                act(g)

    for k in range(chunks):
        crossing(0, k, ty, tx).start()
    own_rows(0, ty).start()

    loads[0].wait()
    turned_a = wa_f[...].T
    wide_a = jnp.where(spot % 2 == 0, turned_a[:arows], turned_a[arows:]).astype(jnp.bfloat16)
    here = pl.ds(pl.multiple_of(spot * arows, arows), arows)
    was[dp, here, :LATENT] = wide_a[:, :LATENT]
    twice = (
        lax.broadcasted_iota(jnp.int32, (ROPE, 2 * ROPE), 0)
        == lax.broadcasted_iota(jnp.int32, (ROPE, 2 * ROPE), 1) % ROPE
    ).astype(jnp.bfloat16)
    was[dp, here, LATENT:] = dot32(wide_a[:, LATENT:], twice).astype(jnp.bfloat16)
    start_hop(A)
    loads[1].wait()
    wbs[dp] = wb_f[...].astype(jnp.bfloat16)
    start_hop(B)
    loads[2].wait()
    turned_q = pltpu.roll(wq_f[:, NOPE:], 2 * NOPE - ROPE, 1)
    wqs[dp, :, NOPE:] = turned_q[:, NOPE:].astype(jnp.bfloat16)
    wqs[dp, :, :NOPE] = wq_f[:, :NOPE].astype(jnp.bfloat16)
    start_hop(Q)
    wrs[dp] = turned_q[:, :NOPE].astype(jnp.bfloat16)
    share_first(dp)
    loads[3].wait()
    woz[dp] = wo_f[...].T.astype(jnp.bfloat16)

    def vocab_step(k, _):
        slot = k % 2

        @pl.when(k + 1 < count)
        def _():
            vocab_load(k + 1, 1 - slot).start()

        vocab_load(k, slot).wait()
        cols = pl.ds(pl.multiple_of(k * slab, slab), slab)
        table[:, cols] = stage[slot].astype(jnp.bfloat16)
        return 0

    part_rows = 32

    def norm(slot, prompt):
        def body(i, _):
            at = pl.multiple_of(i * part_rows, part_rows)
            value = normalize(xs[slot, prompt, pl.ds(at, part_rows)], again_ref[...])
            value = value.astype(jnp.bfloat16)
            to = pl.multiple_of(prompt * LEN + slot * quarter + at, part_rows)
            for b in range(groups):
                h[b, pl.ds(to, part_rows)] = value[:, b * block : (b + 1) * block]
            return 0

        lax.fori_loop(0, quarter // part_rows, body, 0)

    span_rows = 512

    def project(g, first):
        own = owner_ref[g]

        def body(i, _):
            at = pl.ds(pl.multiple_of(i * span_rows, span_rows), span_rows)
            rows_in = h[own, at]
            for low, high, weights in ((NOPE, QCOLS, wqs), (QCOLS, QCOLS + ACOLS, was)):
                term = dot32(rows_in, weights[g])
                acc[at, low:high] = term if first else acc[at, low:high] + term
            return 0

        lax.fori_loop(0, LEN // span_rows, body, 0)

    def project_step(step):
        def one(way, _):
            g = dp - (1 - 2 * way) * (step + 1)

            @pl.when((g >= 0) & (g < groups))
            def _():
                share_wait(g)
                project(g, False)

            return 0

        lax.fori_loop(0, 2, one, 0)

    def project_all(p, targets):
        def body(i, _):
            at = pl.ds(pl.multiple_of(p * LEN + i * span_rows, span_rows), span_rows)
            for low, high, weights in targets:
                total = dot32(h[owner_ref[0], at], weights[0])
                for g in range(1, groups):
                    total = total + dot32(h[owner_ref[g], at], weights[g])
                acc[at, low:high] = total
            return 0

        lax.fori_loop(0, LEN // span_rows, body, 0)

    lax.fori_loop(0, 7, vocab_step, 0)
    both(A, 0)
    arrived(0, share_first)
    cross_start(1, 0)
    own_rows(1, ty).start()
    loads[4].wait()
    norm(ty, 0)
    cross_step(0, 0)
    both(B, 0)
    own_rows(0, partner).wait_recv()
    norm(partner, 0)
    both(Q, 0)
    cross_step(0, 1)
    lax.fori_loop(7, count, vocab_step, 0)
    side_step(0, 0)
    both(A, 1)
    arrived(1, share_first)
    share_second(dp)
    arrived(0, share_second)
    both(B, 1)
    norm(ty, 1)
    side_step(0, 1)
    norm(across, 0)
    share_third(dp)
    arrived(0, share_third)
    far_wait(0)
    norm(far, 0)
    cross_step(1, 0)
    both(Q, 1)
    start_hop(O)
    arrived(1, share_second)
    take(A, 2)
    arrived(2, share_first)
    cross_start(1, 1)
    share_wait(dp)
    project(dp, True)
    arrived(1, share_third)
    project_step(0)
    forward(O, 0)
    start_hop(R)
    side_step(1, 0)
    arrived(2, share_second)
    project_step(1)
    cross_step(1, 1)
    arrived(2, share_third)
    forward(O, 1)

    def stored(b):
        place = jnp.int32(0)
        for g in range(groups):
            place = jnp.where(owner_ref[g] == b, g, place)
        return place

    brows = LATENT // groups

    lane = lax.broadcasted_iota(jnp.int32, (TILE, 2 * ROPE), 1)

    def rotate(values, at):
        swapped = jnp.where(
            lane % ROPE < ROPE // 2,
            pltpu.roll(values, 2 * ROPE - ROPE // 2, 1),
            pltpu.roll(values, ROPE // 2, 1),
        )
        return values * cos_ref[at] + swapped * sin_ref[at]

    factor = (NOPE + ROPE) ** (-0.5) * 1.4426950408889634
    lives = [lengths_ref[deal_ref[dp * per_grp + p]] for p in range(per_grp)]

    def keys(p, tile, _):
        down = acc[pl.ds(pl.multiple_of(p * LEN + tile * TILE, TILE), TILE), QCOLS:]
        to = pl.ds(pl.multiple_of(tile * TILE, TILE), TILE)
        latent = normalize(down[:, :LATENT], lgain_ref[...]).astype(jnp.bfloat16)
        key_rope = rotate(down[:, LATENT:], to).astype(jnp.bfloat16)
        key_val = dot32(latent, wbl[...]).astype(jnp.bfloat16)
        for head in range(heads):
            k_ref[p, head, to, :NOPE] = key_val[:, 2 * head * NOPE : (2 * head + 1) * NOPE]
            k_ref[p, head, to, NOPE:] = key_rope
            v_ref[p, head, to] = key_val[:, (2 * head + 1) * NOPE : (2 * head + 2) * NOPE]
        return 0


    def hears(p, slot, head):
        return heard.at[p, slot * heads + head]

    def heads_of(head, p, tile, slot):
        return remote(
            o_ref.at[head, tile, p], hears(p, tx * ty_size + slot, head),
            o_send.at[head, p, tile], o_recv.at[head, p, slot], ty=tile,
        )

    def passed(head, p, slot, slot_tx, source=None):
        ref = hears(p, slot_tx * ty_size + slot, head)
        return remote(
            ref if source is None else source, ref,
            f_send.at[head, p, slot], f_recv.at[head, p, slot], tx=other,
        )

    def own_passed(head, p, tile):
        return passed(head, p, ty, tx, o_ref.at[head, tile, p])

    def relay(head, p):
        for k in range(1, ty_size):
            slot = (ty + k) % ty_size
            heads_of(head, p, ty, slot).wait_recv()
            passed(head, p, slot, tx).start()

    tile_order = (3, 1, 2, 0)

    def attention(head, p):
        live = jnp.where(p == 0, lives[0], lives[1])
        last = jnp.zeros((1, NOPE), jnp.float32)
        nope_at = (1 - head) * NOPE
        for t in tile_order:
            span = (t + 1) * TILE
            at = pl.ds(pl.multiple_of(p * LEN + t * TILE, TILE), TILE)
            turned = rotate(acc[at, 2 * NOPE : QCOLS], pl.ds(t * TILE, TILE))
            i = lax.broadcasted_iota(jnp.int32, (TILE, span), 0) + t * TILE
            j = lax.broadcasted_iota(jnp.int32, (TILE, span), 1)
            allowed = j <= jnp.minimum(i, live - 1)
            mine = jnp.where(lane // ROPE == 1 - head, turned, 0.0)
            query = jnp.concatenate([acc[at, nope_at : nope_at + NOPE], mine], axis=1)
            score = lax.dot_general(
                query.astype(jnp.bfloat16), k_ref[p, head, :span], (((1,), (1,)), ((), ())),
                preferred_element_type=jnp.float32,
            )
            score = jnp.where(allowed, score, -1e30)
            expo = jnp.exp2((score - jnp.max(score, axis=-1, keepdims=True)) * factor)
            prob = expo * (1.0 / jnp.sum(expo, axis=-1, keepdims=True))
            out = dot32(prob.astype(jnp.bfloat16), v_ref[p, head, :span]).astype(jnp.bfloat16)
            o_ref[head, t, p] = out
            at_last = lax.broadcasted_iota(jnp.int32, (TILE, NOPE), 0) + t * TILE == live - 1
            last = last + jnp.sum(
                jnp.where(at_last, out.astype(jnp.float32), 0.0), axis=0, keepdims=True
            )

            @pl.when(ty == t)
            def _():
                heard[p, spot * heads + head] = out
                own_passed(head, p, t).start()

            @pl.when(ty != t)
            def _():
                heads_of(head, p, t, ty).start()

        for k in range(per_grp):

            @pl.when(p == k)
            def _():
                ends_ref[spot, k : k + 1, head * NOPE : (head + 1) * NOPE] = last

    pieces = 2
    rows_of = piece // pieces

    def wide(j, q, slot_tx, slot_ty):
        at = (slot_tx * ty_size + slot_ty) * piece + q * rows_of
        return wos.at[j, pl.ds(pl.multiple_of(at, rows_of), rows_of)]

    def move(n, j, q, slot_tx, slot_ty, source=None, **where):
        ref = wide(j, q, slot_tx, slot_ty)
        return remote(
            ref if source is None else source, ref, w_send.at[n, j, q], w_recv.at[n, j, q],
            **where,
        )

    def given(j, q):
        source = give.at[j, pl.ds(q * rows_of, rows_of)]
        return move(0, j, q, tx, ty, source, tx=other)

    early = [jnp.where(dp < groups // 2, k, groups - 1 - k) for k in range(steps)]
    late = jnp.where(dp < groups // 2, groups - 1, 0)

    def aim(g):
        return owner_ref[g] // (groups // tx_size)

    def first_for(side):
        found = early[-1]
        for g in early[-2::-1]:
            found = jnp.where(aim(g) == side, g, found)
        return found

    def first_rows(side):
        found = woz[early[-1]]
        for g in early[-2::-1]:
            found = jnp.where(aim(g) == side, woz[g], found)
        return found

    def second_for(side):
        found = late
        for g in early:
            found = jnp.where((aim(g) == side) & (g != first_for(side)), g, found)
        return found

    mine_at = pl.ds(pl.multiple_of(spot * piece, piece), piece)

    def spread(j, give_rows, keep_rows):
        give[j] = give_rows
        for q in range(pieces):
            given(j, q).start()
        wos[j, mine_at] = keep_rows
        for q in range(pieces):
            move(1, j, q, tx, ty, ty=across).start()
            move(2, j, q, tx, ty, ty=partner).start()

    def spread_on(j):
        for q in range(pieces):
            move(0, j, q, other, ty, tx=other).wait_recv()
            move(3, j, q, other, ty, ty=across).start()
            move(4, j, q, other, ty, ty=partner).start()

    def spread_in(j):
        for q in range(pieces):
            move(1, j, q, tx, across, ty=across).wait_recv()
            move(5, j, q, tx, across, ty=partner).start()

    def spread_last(j):
        for q in range(pieces):
            move(3, j, q, other, across, ty=across).wait_recv()
            move(6, j, q, other, across, ty=partner).start()

    def first_head(p, _):
        @pl.when(p == 0)
        def _():
            take(B, 2)
            take(Q, 2)
            project_step(2)
            for b in range(groups):
                wbl[b * brows : (b + 1) * brows] = wbs[stored(b)]

        @pl.when(p == 1)
        def _():
            side_step(1, 1)
            own_rows(1, partner).wait_recv()
            norm(partner, 1)
            norm(across, 1)
            far_wait(1)
            norm(far, 1)
            relay(0, 0)
            take(O, 0)
            take(O, 1)
            spread(0, first_rows(other), first_rows(tx))
            project_all(1, ((NOPE, QCOLS, wqs), (QCOLS, QCOLS + ACOLS, was)))

        lax.fori_loop(0, LEN // TILE, functools.partial(keys, p), 0)
        attention(0, p)
        pl.when(p == 0)(lambda: forward(R, 0))
        return 0

    lax.fori_loop(0, per_grp, first_head, 0)
    forward(R, 1)
    take(O, 2)
    spread(1, woz[second_for(other)], woz[second_for(tx)])
    relay(0, 1)
    spread_on(0)
    spread_in(0)
    for step in range(steps):
        take(R, step)

    def second_head(p, _):
        project_all(p, ((0, NOPE, wrs),))
        attention(1, p)

        @pl.when(p == 0)
        def _():
            spread_on(1)
            spread_in(1)

        @pl.when(p == 1)
        def _():
            relay(1, 0)

        return 0

    lax.fori_loop(0, per_grp, second_head, 0)

    def row_of(k, slot):
        peer = (spot + k) % plane
        return remote(
            ends_ref.at[spot], ends_ref.at[slot], e_send.at[k], e_recv.at[k],
            tx=peer // ty_size, ty=peer % ty_size,
        )

    for k in range(1, plane):
        row_of(k, spot).start()
    relay(1, 1)
    for j in range(2):
        spread_last(j)
    for head in range(heads):
        for p in range(per_grp):
            for k in range(ty_size):
                passed(head, p, (ty + k) % ty_size, other).wait_recv()
    for p in range(per_grp):
        for n in range(plane * heads):
            mixed[p, :, n * NOPE : (n + 1) * NOPE] = heard[p, n]
    for p in range(per_grp):
        tile = (lives[p] - 1) // quarter
        inside = lax.broadcasted_iota(jnp.int32, (quarter, half), 0) + tile * quarter
        tokens = xs[jnp.maximum(tile, 0), p, :, pl.ds(pl.multiple_of(tx * half, half), half)]
        base_ref[p : p + 1] = jnp.sum(
            jnp.where(inside == lives[p] - 1, tokens.astype(jnp.float32), 0.0),
            axis=0, keepdims=True,
        )
    for k in range(1, plane):
        row_of(k, (spot + plane - k) % plane).wait_recv()
    line_ref[...] = jnp.zeros_like(line_ref)
    for slot in range(plane):
        line_ref[0:per_grp, slot * piece : (slot + 1) * piece] = ends_ref[slot]
    for j in range(2):
        for q in range(pieces):
            move(2, j, q, tx, partner, ty=partner).wait_recv()
            move(4, j, q, other, partner, ty=partner).wait_recv()
            move(5, j, q, tx, far, ty=partner).wait_recv()
            move(6, j, q, other, far, ty=partner).wait_recv()

    spots = [jnp.where(owner_ref[first_for(tx)] % 2 == i, 0, 1) for i in range(2)]
    chosen = line_ref[...].astype(jnp.bfloat16)
    peers = groups * tx_size
    place = dp * tx_size + tx
    for i in range(2):
        cols = slice(i * block, (i + 1) * block)
        value = base_ref[:, cols] + dot32(chosen, wos[spots[i]])[:per_grp]
        full[place, :, cols] = value.astype(jnp.bfloat16).astype(jnp.float32)

    def along_peers(k, slot):
        peer = (place + k) % peers
        return remote(
            full.at[place], full.at[slot], r_send.at[k], r_recv.at[k],
            dp=peer // tx_size, tx=peer % tx_size,
        )

    for k in range(1, peers):
        along_peers(k, place).start()

    strip = 256

    def out_step(n, _):
        for i in range(2):

            @pl.when(n // 2 == i)
            def _():
                inside = pl.ds(pl.multiple_of((n % 2) * strip, strip), strip)
                cols = pl.ds(pl.multiple_of(n * strip, strip), strip)
                model = pl.ds(pl.multiple_of(tx * half + n * strip, strip), strip)
                for p in range(per_grp):
                    total = dot32(mixed[p], wos[spots[i], :, inside])
                    hidden_ref[p, :, cols] = (
                        xs[ty, p, :, model].astype(jnp.float32) + total
                    ).astype(jnp.bfloat16)

        return 0

    lax.fori_loop(0, 4, out_step, 0)

    for k in range(1, peers):
        along_peers(k, (place + peers - k) % peers).wait_recv()
    for g in range(groups):
        for t in range(tx_size):
            rows_ref[g * per_grp : (g + 1) * per_grp, t * half : (t + 1) * half] = full[
                g * tx_size + t
            ]
    final = normalize(rows_ref[...], fgain_ref[...])
    owner = owner_ref[dp]
    mine = jnp.zeros((groups * per_grp, block), jnp.float32)
    for g in range(groups):
        mine = jnp.where(owner == g, final[:, g * block : (g + 1) * block], mine)
    mine = mine.astype(jnp.bfloat16)

    def logit_step(k, _):
        cols = pl.ds(pl.multiple_of(k * slab, slab), slab)
        logits = dot32(mine, table[:, cols])
        for g in range(groups):
            part[g, :, cols] = logits[g * per_grp : (g + 1) * per_grp]
        return 0

    parts = 2
    share_words = words // parts

    def along_dp(n, k, slot):
        peer = (dp + k) % groups
        cols = pl.ds(n * share_words, share_words)
        return remote(
            part.at[peer, :, cols], incoming.at[slot, :, cols], l_send.at[n, k], l_recv.at[n, k],
            dp=peer,
        )

    for n in range(parts):
        lax.fori_loop(n * count // parts, (n + 1) * count // parts, logit_step, 0)
        for k in range(1, groups):
            along_dp(n, k, dp).start()
    for n in range(parts):
        cols = slice(n * share_words, (n + 1) * share_words)
        total = part[dp, :, cols]
        for k in range(1, groups):
            slot = (dp + groups - k) % groups
            along_dp(n, k, slot).wait_recv()
            total = total + incoming[slot, :, cols]
        out_ref[:, cols] = total

    for p in range(per_grp):
        for k in range(chunks):
            crossing(p, k, ty, tx).wait_send()
            sideways(p, k, tx).wait_send()
            inward(p, k, 0, across, tx).wait_send()
            inward(p, k, 1, across, other).wait_send()
        own_rows(p, ty).wait_send()
    for step in range(steps):
        for which in range(5):
            for way in range(2):
                copy, runs = hop(which, way, step)
                pl.when(runs)(copy.wait_send)
    for g in range(groups):
        for n in range(7):
            share(n, g).wait_send()
    for head in range(heads):
        for p in range(per_grp):
            own_passed(head, p, ty).wait_send()
            for k in range(1, ty_size):
                slot = (ty + k) % ty_size
                heads_of(head, p, slot, ty).wait_send()
                passed(head, p, slot, tx).wait_send()
    for j in range(2):
        for q in range(pieces):
            given(j, q).wait_send()
            move(1, j, q, tx, ty, ty=across).wait_send()
            move(2, j, q, tx, ty, ty=partner).wait_send()
            move(3, j, q, other, ty, ty=across).wait_send()
            move(4, j, q, other, ty, ty=partner).wait_send()
            move(5, j, q, tx, across, ty=partner).wait_send()
            move(6, j, q, other, across, ty=partner).wait_send()
    for k in range(1, plane):
        row_of(k, spot).wait_send()
    for k in range(1, peers):
        along_peers(k, place).wait_send()
    for n in range(parts):
        for k in range(1, groups):
            along_dp(n, k, dp).wait_send()


def hand_on_kernel(hidden_ref, logits_ref, hidden_out, logits_out, held, words, reads, writes):
    parts = [(hidden_ref.at[p], held.at[p], hidden_out.at[p]) for p in range(held.shape[0])]
    parts.append((logits_ref, words, logits_out))
    inward = [
        pltpu.make_async_copy(source, there, reads.at[n])
        for n, (source, there, _) in enumerate(parts)
    ]
    outward = [
        pltpu.make_async_copy(there, target, writes.at[n])
        for n, (_, there, target) in enumerate(parts)
    ]
    for copy in inward:
        copy.start()
    for first, second in zip(inward, outward):
        first.wait()
        second.start()
    for copy in outward:
        copy.wait()


def hand_on(hidden, logits):
    hbm = pl.BlockSpec(memory_space=pl.ANY)
    return pl.pallas_call(
        hand_on_kernel,
        in_specs=[hbm, hbm],
        out_specs=[hbm, hbm],
        out_shape=[
            jax.ShapeDtypeStruct(hidden.shape, hidden.dtype),
            jax.ShapeDtypeStruct(logits.shape, logits.dtype),
        ],
        scratch_shapes=[
            pltpu.VMEM(hidden.shape, hidden.dtype),
            pltpu.VMEM(logits.shape, logits.dtype),
            pltpu.SemaphoreType.DMA((hidden.shape[0] + 1,)),
            pltpu.SemaphoreType.DMA((hidden.shape[0] + 1,)),
        ],
    )(hidden, logits)


def layer(groups, owner, lengths, deal, x, again, lgain, fgain, wq, wa, wb, wo, vocab):
    per_grp, quarter, width = x.shape
    block, words = vocab.shape
    half = width // 2
    piece = 2 * NOPE
    slab = 512
    steps = groups - 1
    peers = 2 * groups
    position = np.arange(LEN, dtype=np.float32)
    frequency = np.power(
        np.float32(10000.0), -np.arange(ROPE // 2, dtype=np.float32) / np.float32(ROPE // 2)
    ).astype(np.float32)
    angles = (position[:, None] * frequency).astype(np.float32).astype(np.float64)
    cosine, sine = np.cos(angles), np.sin(angles)
    cosine = jnp.asarray(np.concatenate([cosine] * 4, axis=1).astype(np.float32))
    sine = jnp.asarray(np.concatenate([-sine, sine, -sine, sine], axis=1).astype(np.float32))
    dma = pltpu.SemaphoreType.DMA
    vmem = pl.BlockSpec(memory_space=pltpu.VMEM)
    smem = pl.BlockSpec(memory_space=pltpu.SMEM)
    hbm = pl.BlockSpec(memory_space=pl.ANY)
    bf16 = lambda *dims: pltpu.VMEM(dims, jnp.bfloat16)
    f32 = lambda *dims: pltpu.VMEM(dims, jnp.float32)
    return pl.pallas_call(
        functools.partial(layer_kernel, groups),
        in_specs=[smem, smem, smem, hbm, vmem, vmem, vmem, vmem, vmem, hbm, hbm, hbm, hbm, hbm],
        out_specs=[vmem, vmem],
        out_shape=[
            jax.ShapeDtypeStruct((per_grp, quarter, half), jnp.bfloat16),
            jax.ShapeDtypeStruct((per_grp, words), jnp.float32),
        ],
        scratch_shapes=[
            bf16(4, per_grp, quarter, width),
            bf16(groups, per_grp * LEN, block),
            bf16(groups, block, NOPE),
            bf16(groups, block, 2 * NOPE),
            bf16(groups, block, ACOLS),
            bf16(groups, LATENT // groups, 2 * piece),
            bf16(LATENT, 2 * piece),
            bf16(groups, piece, block),
            bf16(2, piece, block),
            bf16(2, 8 * piece, block),
            f32(per_grp * LEN, QCOLS + ACOLS),
            bf16(per_grp, 2, LEN, 2 * NOPE),
            bf16(per_grp, 2, LEN, NOPE),
            bf16(2, 4, per_grp, TILE, NOPE),
            bf16(per_grp, 16, TILE, NOPE),
            bf16(per_grp, TILE, 8 * piece),
            bf16(block, words),
            f32(2, block, slab),
            f32(*wq.shape),
            f32(wa.shape[1], block // 4),
            f32(*wb.shape),
            f32(block, piece),
            f32(8, per_grp, piece),
            f32(per_grp, half),
            f32(8, width),
            f32(peers, per_grp, half),
            f32(groups * per_grp, width),
            f32(groups, per_grp, words),
            f32(groups, per_grp, words),
            dma((5,)), dma((2,)),
            dma((per_grp, 4)), dma((per_grp, 4)), dma((per_grp, 4)), dma((per_grp, 4)),
            dma((2, per_grp, 4)), dma((2, per_grp, 4)), dma((per_grp,)), dma((per_grp,)),
            dma((2, 5, steps)), dma((2, 5, steps)), dma((7, groups)), dma((7, groups)),
            dma((2, per_grp, 4)), dma((2, per_grp, 4)), dma((2, per_grp, 4)),
            dma((2, per_grp, 4)), dma((7, 2, 2)), dma((7, 2, 2)),
            dma((8,)), dma((8,)), dma((peers,)), dma((peers,)), dma((2, groups)),
            dma((2, groups)),
        ],
        compiler_params=pltpu.CompilerParams(
            collective_id=0, has_side_effects=True, vmem_limit_bytes=60 * 1024 * 1024
        ),
        cost_estimate=pl.CostEstimate(
            flops=16_000_000_000, bytes_accessed=24_000_000, transcendentals=3_000_000
        ),
    )(owner, lengths, deal, x, again, lgain, fgain, cosine, sine, wq, wa.T, wb, wo, vocab)


def load_vocab(vocab_chunk, vocab_ref, table, v_sem):
    loads = []
    for k in range(vocab_ref.shape[1] // vocab_chunk):
        cols = pl.ds(k * vocab_chunk, vocab_chunk)
        loads.append(
            pltpu.make_async_copy(vocab_ref.at[:, cols], table.at[:, cols], v_sem.at[k])
        )
        loads[-1].start()
    return loads


def next_token(
    groups, tx_size, ty_size, vocab_chunk, loads, owner_ref, picked_ref, gain_ref, out_ref, seen, full,
    rows_ref, table, part, incoming, t_send, t_recv, r_send, r_recv, l_send, l_recv,
):
    dp, tx, ty = lax.axis_index("dp"), lax.axis_index("tx"), lax.axis_index("ty")
    per_grp, half = picked_ref.shape
    block = table.shape[0]
    peers = groups * tx_size
    place = dp * tx_size + tx
    count = len(loads)

    def along_ty(k, slot):
        return remote(
            picked_ref, seen.at[slot], t_send.at[k], t_recv.at[k], ty=(ty + k) % ty_size
        )

    for k in range(1, ty_size):
        along_ty(k, ty).start()
    merged = picked_ref[...]
    for k in range(1, ty_size):
        slot = (ty + ty_size - k) % ty_size
        along_ty(k, slot).wait_recv()
        merged = merged + seen[slot]
    full[place] = merged

    def along_peers(k, slot):
        peer = (place + k) % peers
        return remote(
            full.at[place], full.at[slot], r_send.at[k], r_recv.at[k],
            dp=peer // tx_size, tx=peer % tx_size,
        )

    for k in range(1, peers):
        along_peers(k, place).start()
    for k in range(1, peers):
        along_peers(k, (place + peers - k) % peers).wait_recv()
    for g in range(groups):
        for t in range(tx_size):
            rows_ref[g * per_grp : (g + 1) * per_grp, t * half : (t + 1) * half] = full[
                g * tx_size + t
            ]
    final = normalize(rows_ref[...], gain_ref[...])
    owner = owner_ref[dp]
    mine = jnp.zeros((groups * per_grp, block), jnp.float32)
    for g in range(groups):
        mine = jnp.where(owner == g, final[:, g * block : (g + 1) * block], mine)
    mine = mine.astype(jnp.bfloat16)
    for k in range(count):
        loads[k].wait()
        cols = slice(k * vocab_chunk, (k + 1) * vocab_chunk)
        logits = dot32(mine, table[:, cols].astype(jnp.bfloat16))
        for g in range(groups):
            part[g, :, cols] = logits[g * per_grp : (g + 1) * per_grp]

    def along_dp(k, slot):
        peer = (dp + k) % groups
        return remote(part.at[peer], incoming.at[slot], l_send.at[k], l_recv.at[k], dp=peer)

    for k in range(1, groups):
        along_dp(k, dp).start()
    total = part[dp]
    for k in range(1, groups):
        slot = (dp + groups - k) % groups
        along_dp(k, slot).wait_recv()
        total = total + incoming[slot]
    out_ref[...] = total
    for k in range(1, ty_size):
        along_ty(k, ty).wait_send()
    for k in range(1, peers):
        along_peers(k, place).wait_send()
    for k in range(1, groups):
        along_dp(k, dp).wait_send()


def tail_kernel(
    groups, tx_size, ty_size, vocab_chunk, owner_ref, picked_ref, gain_ref, vocab_ref, out_ref,
    seen, full, rows_ref, table, part, incoming, t_send, t_recv, r_send, r_recv, l_send, l_recv,
    v_sem,
):
    dp, tx, ty = lax.axis_index("dp"), lax.axis_index("tx"), lax.axis_index("ty")
    peers = groups * tx_size
    place = dp * tx_size + tx
    loads = load_vocab(vocab_chunk, vocab_ref, table, v_sem)
    for k in range(1, ty_size):
        greet(ty=(ty + k) % ty_size)
    for k in range(1, peers):
        peer = (place + k) % peers
        greet(dp=peer // tx_size, tx=peer % tx_size)
    pl.semaphore_wait(pltpu.get_barrier_semaphore(), ty_size + peers - 2)
    next_token(
        groups, tx_size, ty_size, vocab_chunk, loads, owner_ref, picked_ref, gain_ref, out_ref,
        seen, full, rows_ref, table, part, incoming, t_send, t_recv, r_send, r_recv, l_send,
        l_recv,
    )


def tail(groups, tx_size, ty_size, owner, picked, gain, vocab):
    per_grp, half = picked.shape
    block, words = vocab.shape
    vocab_chunk = 512
    peers = groups * tx_size
    dma = pltpu.SemaphoreType.DMA
    vmem = pl.BlockSpec(memory_space=pltpu.VMEM)
    return pl.pallas_call(
        functools.partial(tail_kernel, groups, tx_size, ty_size, vocab_chunk),
        in_specs=[
            pl.BlockSpec(memory_space=pltpu.SMEM), vmem, vmem, pl.BlockSpec(memory_space=pl.ANY),
        ],
        out_specs=vmem,
        out_shape=jax.ShapeDtypeStruct((per_grp, words), jnp.float32),
        scratch_shapes=[
            pltpu.VMEM((ty_size, per_grp, half), jnp.float32),
            pltpu.VMEM((peers, per_grp, half), jnp.float32),
            pltpu.VMEM((groups * per_grp, half * tx_size), jnp.float32),
            pltpu.VMEM((block, words), jnp.float32),
            pltpu.VMEM((groups, per_grp, words), jnp.float32),
            pltpu.VMEM((groups, per_grp, words), jnp.float32),
            dma((ty_size,)), dma((ty_size,)), dma((peers,)), dma((peers,)),
            dma((groups,)), dma((groups,)), dma((words // vocab_chunk,)),
        ],
        compiler_params=pltpu.CompilerParams(
            collective_id=1, has_side_effects=True, vmem_limit_bytes=40 * 1024 * 1024
        ),
        cost_estimate=pl.CostEstimate(
            flops=100_000_000, bytes_accessed=16_000_000, transcendentals=0
        ),
    )(owner, picked, gain, vocab)


def rotate_half(values, position):
    half_dim = values.shape[-1] // 2
    frequency = 10000.0 ** (-jnp.arange(half_dim, dtype=jnp.float32) / half_dim)
    angles = position.astype(jnp.float32)[..., None] * frequency
    cosine = jnp.cos(angles)
    sine = jnp.sin(angles)
    first_half = values[..., :half_dim]
    second_half = values[..., half_dim:]
    return jnp.concatenate(
        [first_half * cosine - second_half * sine, first_half * sine + second_half * cosine],
        axis=-1,
    )


def split_positions(
    inputs, inverse, live_len, attn_gain, latent_gain, w_query, w_down_kv, w_up_kv, w_out
):
    groups = lax.axis_size("dp")

    def arrange(gathered):
        block_rows = gathered.shape[0] // groups
        return jnp.concatenate(
            [
                lax.dynamic_slice_in_dim(gathered, inverse[g] * block_rows, block_rows, 0)
                for g in range(groups)
            ],
            axis=0,
        )

    query_w, down_w, up_w, out_w = (
        lax.all_gather(w_query.astype(jnp.bfloat16), "dp", axis=0, tiled=True),
        lax.all_gather(w_down_kv.astype(jnp.bfloat16), "dp", axis=0, tiled=True),
        lax.all_gather(w_up_kv.astype(jnp.bfloat16), "dp", axis=0, tiled=True),
        lax.all_gather(w_out.astype(jnp.bfloat16), "dp", axis=0, tiled=True),
    )
    query_w = arrange(query_w)
    down_w = arrange(down_w)
    up_w = arrange(up_w)
    out_w = arrange(out_w)
    query_w, up_w = (
        lax.all_gather(query_w, "ty", axis=1, tiled=True),
        lax.all_gather(up_w, "ty", axis=1, tiled=True),
    )
    per_grp, quarter, width = inputs.shape
    heads = query_w.shape[1] // (NOPE + ROPE)
    position = lax.axis_index("ty") * quarter + jnp.arange(quarter, dtype=jnp.int32)
    flat_rows = inputs.reshape(per_grp * quarter, width)
    normed = normalize(flat_rows, attn_gain).astype(jnp.bfloat16)
    queries = jnp.dot(normed, query_w, preferred_element_type=jnp.float32).reshape(
        per_grp, quarter, heads, NOPE + ROPE
    )
    queries = jnp.concatenate(
        [queries[..., :NOPE], rotate_half(queries[..., NOPE:], position[None, :, None])], axis=-1
    ).astype(jnp.bfloat16)
    down_proj = jnp.dot(normed, down_w, preferred_element_type=jnp.float32).reshape(
        per_grp, quarter, LATENT + ROPE
    )
    latent = normalize(down_proj[..., :LATENT], latent_gain).astype(jnp.bfloat16)
    key_rope = rotate_half(down_proj[..., LATENT:], position[None, :]).astype(jnp.bfloat16)
    gathered = lax.all_gather(
        jnp.concatenate([latent, key_rope], axis=-1), "ty", axis=1, tiled=True
    )
    key_val = jnp.dot(gathered[..., :LATENT], up_w, preferred_element_type=jnp.float32).astype(
        jnp.bfloat16
    )
    rope_all = gathered[..., LATENT:]
    key_val = key_val.reshape(per_grp, LEN, heads, 2, NOPE)
    key_nope = key_val[:, :, :, 0]
    values = key_val[:, :, :, 1]
    score_scale = (NOPE + ROPE) ** (-0.5)
    scores = (
        jnp.einsum(
            "pqhd,pkhd->phqk", queries[..., :NOPE], key_nope, preferred_element_type=jnp.float32
        )
        + jnp.einsum(
            "pqhd,pkd->phqk", queries[..., NOPE:], rope_all, preferred_element_type=jnp.float32
        )
    ) * score_scale
    key_pos = jnp.arange(LEN, dtype=jnp.int32)
    allowed = (key_pos[None, None, :] <= position[None, :, None]) & (
        key_pos[None, None, :] < live_len[:, None, None]
    )
    scores = jnp.where(allowed[:, None], scores, -1e30)
    top = jnp.max(scores, axis=-1, keepdims=True)
    expo = jnp.exp(scores - top)
    softmax_w = (expo / jnp.sum(expo, axis=-1, keepdims=True)).astype(jnp.bfloat16)
    attended = jnp.einsum(
        "phqk,pkhd->pqhd", softmax_w, values, preferred_element_type=jnp.float32
    ).astype(jnp.bfloat16)
    attended = attended.reshape(per_grp * quarter, heads * NOPE)
    own_width = width // lax.axis_size("tx")
    col_start = lax.axis_index("tx") * own_width
    partial_value = lax.dot_general(
        attended, out_w, (((1,), (1,)), ((), ())), preferred_element_type=jnp.float32
    ).reshape(per_grp, quarter, width)
    summed = lax.psum_scatter(partial_value, "tx", scatter_dimension=2, tiled=True)
    residual = lax.dynamic_slice_in_dim(inputs, col_start, own_width, 2)
    layer_out = (residual.astype(jnp.float32) + summed).astype(jnp.bfloat16)
    return layer_out


def shards(
    inputs,
    lengths,
    prompt_deal,
    block_owner,
    attn_gain,
    latent_gain,
    final_gain,
    w_query,
    w_down_kv,
    w_up_kv,
    w_out,
    w_vocab,
):
    groups = lax.axis_size("dp")
    dp, tx, ty = lax.axis_index("dp"), lax.axis_index("tx"), lax.axis_index("ty")
    per_grp, quarter, width = inputs.shape
    half = width // lax.axis_size("tx")
    whole_heads = w_query.shape[1] == QCOLS and w_up_kv.shape[1] == 4 * NOPE
    here = whole_heads and (lax.axis_size("tx"), lax.axis_size("ty"), per_grp) == (2, 4, 2)
    if here and groups == 4 and (quarter, width) == (TILE, 4 * w_query.shape[0]):
        return hand_on(
            *layer(
                groups, block_owner, lengths, prompt_deal, inputs, attn_gain[None],
                latent_gain[None], final_gain[None], w_query, w_down_kv, w_up_kv, w_out, w_vocab,
            )
        )

    order = jnp.arange(groups, dtype=jnp.int32)
    inverse = jnp.sum(
        jnp.where(block_owner[None, :] == order[:, None], order[None, :], 0), axis=1
    ).astype(jnp.int32)
    slots = dp * per_grp + jnp.arange(per_grp, dtype=jnp.int32)
    names = jnp.arange(lengths.shape[0], dtype=jnp.int32)

    def at_index(values, index):
        return jnp.sum(jnp.where(names[None] == index[:, None], values[None], 0), axis=1)

    live_len = at_index(lengths, at_index(prompt_deal, slots))
    layer_out = split_positions(
        inputs, inverse, live_len, attn_gain, latent_gain, w_query, w_down_kv, w_up_kv, w_out
    )

    at = live_len - 1 - ty * quarter
    picked = jnp.stack(
        [
            lax.dynamic_slice(
                layer_out, (i, jnp.clip(at[i], 0, quarter - 1), 0), (1, 1, half)
            ).reshape(half)
            for i in range(per_grp)
        ]
    ).astype(jnp.float32)
    inside = (at >= 0) & (at < quarter)
    picked = jnp.where(inside[:, None], picked, 0.0)
    logits = tail(
        groups, lax.axis_size("tx"), lax.axis_size("ty"), block_owner, picked, final_gain[None],
        w_vocab,
    )
    return (layer_out, logits)


def solution(mesh):
    placed = (
        P("dp", "ty", None),
        P(),
        P(),
        P(),
        P(),
        P(),
        P(),
        P("dp", ("tx", "ty")),
        P("dp", None),
        P("dp", ("tx", "ty")),
        P("dp", "tx"),
        P("dp", ("tx", "ty")),
    )
    return jax.shard_map(
        shards,
        mesh=mesh,
        in_specs=placed,
        out_specs=(P("dp", "ty", "tx"), P("dp", ("tx", "ty"))),
        check_vma=False,
    )
```

```python
import functools

import jax
import jax.numpy as jnp
import numpy as np
from jax import lax
from jax.experimental import pallas as pl
from jax.experimental.pallas import tpu as pltpu
from jax.sharding import PartitionSpec as P

NOPE = 128
ROPE = 64
LATENT = 512
LEN = 1024
TILE = 256
EPS = 1e-06
QCOLS = 384
ACOLS = 640


def normalize(values, gain):
    wide = values.astype(jnp.float32)
    return wide * lax.rsqrt(jnp.mean(wide * wide, axis=-1, keepdims=True) + EPS) * gain


def dot32(left, right):
    return jnp.dot(left, right, preferred_element_type=jnp.float32)


def remote(src, dst, send, recv, **where):
    return pltpu.make_async_remote_copy(
        src_ref=src,
        dst_ref=dst,
        send_sem=send,
        recv_sem=recv,
        device_id=where,
        device_id_type=pl.DeviceIdType.MESH,
    )


def greet(**where):
    pl.semaphore_signal(
        pltpu.get_barrier_semaphore(),
        inc=1,
        device_id=where,
        device_id_type=pl.DeviceIdType.MESH,
    )


def layer_kernel(
    groups, owner_ref, lengths_ref, deal_ref, x_ref, again_ref, lgain_ref, fgain_ref, cos_ref,
    sin_ref, wq_ref, wa_ref, wb_ref, wo_ref, vocab_ref, hidden_ref, out_ref,
    xs, h, wrs, wqs, was, wbs, wbl, woz, give, wos, acc, k_ref, v_ref, o_ref, heard, mixed, table, stage,
    wq_f, wa_f, wb_f, wo_f, ends_ref, base_ref, line_ref, full, rows_ref, part, incoming,
    local, v_sem, x_send, x_recv, y_send, y_recv, p_send, p_recv, b_send, b_recv,
    z_send, z_recv, a_send, a_recv, o_send, o_recv, f_send, f_recv, w_send, w_recv,
    e_send, e_recv, r_send, r_recv, l_send, l_recv,
):
    dp, tx, ty = lax.axis_index("dp"), lax.axis_index("tx"), lax.axis_index("ty")
    tx_size, ty_size = 2, 4
    per_grp = 2
    core = ty % 2
    partner = ty + 1 - 2 * core
    across = (ty + 2) % 4
    far = (partner + 2) % 4
    other = 1 - tx
    spot = tx * ty_size + ty
    plane = tx_size * ty_size
    steps = groups - 1
    chunks = 4
    quarter, width = x_ref.shape[1], x_ref.shape[2]
    half = width // tx_size
    block = width // groups
    rows = quarter // (2 * chunks)
    words = vocab_ref.shape[1]
    slab = stage.shape[-1]
    count = words // slab
    piece = 2 * NOPE
    heads = 2

    loads = [
        pltpu.make_async_copy(wa_ref.at[:, pl.ds(pl.multiple_of((spot // 2) * 128, 128), 128)], wa_f, local.at[0]),
        pltpu.make_async_copy(wb_ref, wb_f, local.at[1]),
        pltpu.make_async_copy(wq_ref, wq_f, local.at[2]),
        pltpu.make_async_copy(
            wo_ref.at[:, pl.ds(pl.multiple_of(ty * piece, piece), piece)], wo_f, local.at[3]
        ),
        pltpu.make_async_copy(x_ref, xs.at[ty], local.at[4]),
    ]
    for load in loads:
        load.start()

    def vocab_load(k, slot):
        cols = pl.ds(pl.multiple_of(k * slab, slab), slab)
        return pltpu.make_async_copy(vocab_ref.at[:, cols], stage.at[slot], v_sem.at[slot])

    vocab_load(0, 0).start()

    for k in range(1, plane):
        peer = (spot + k) % plane
        greet(tx=peer // ty_size, ty=peer % ty_size)
    for k in range(1, groups):
        for t in range(tx_size):
            greet(dp=(dp + k) % groups, tx=t)
    pl.semaphore_wait(pltpu.get_barrier_semaphore(), plane - 1 + (groups - 1) * tx_size)

    def cut(slot, p, side, k):
        at = pl.multiple_of(side * (quarter // 2) + k * rows, rows)
        return xs.at[slot, p, pl.ds(at, rows)]

    def crossing(p, k, slot, side):
        at = pl.multiple_of(side * (quarter // 2) + k * rows, rows)
        src = x_ref.at[p, pl.ds(at, rows)]
        return remote(src, cut(slot, p, side, k), x_send.at[p, k], x_recv.at[p, k], ty=across)

    def sideways(p, k, side):
        ref = cut(across, p, side, k)
        return remote(ref, ref, y_send.at[p, k], y_recv.at[p, k], tx=other)

    def inward(p, k, n, slot, side):
        ref = cut(slot, p, side, k)
        return remote(ref, ref, p_send.at[n, p, k], p_recv.at[n, p, k], ty=partner)

    def own_rows(p, slot):
        return remote(x_ref.at[p], xs.at[slot, p], b_send.at[p], b_recv.at[p], ty=partner)

    def cross_start(p, n):
        for k in (2 * n, 2 * n + 1):
            crossing(p, k, ty, tx).start()

    def cross_step(p, n):
        for k in (2 * n, 2 * n + 1):
            crossing(p, k, across, tx).wait_recv()
            sideways(p, k, tx).start()
            inward(p, k, 0, across, tx).start()

    def side_step(p, n):
        for k in (2 * n, 2 * n + 1):
            sideways(p, k, other).wait_recv()
            inward(p, k, 1, across, other).start()

    def far_wait(p):
        for k in range(chunks):
            inward(p, k, 0, far, tx).wait_recv()
            inward(p, k, 1, far, other).wait_recv()

    A, B, Q, R, O = range(5)
    arows = block // plane

    def a_part(g, q):
        return was.at[g, pl.ds(pl.multiple_of(q * arows, arows), arows)]

    slots = [
        lambda g: a_part(g, spot),
        lambda g: wbs.at[g],
        lambda g: wqs.at[g],
        lambda g: wrs.at[g],
        lambda g: woz.at[g],
    ]

    def hop(which, way, step):
        sign = 1 - 2 * way
        g = dp - sign * step
        runs = (g >= 0) & (g < groups) & (dp + sign >= 0) & (dp + sign < groups)
        ref = slots[which](g)
        copy = remote(
            ref, ref, z_send.at[way, which, step], z_recv.at[way, which, step], dp=dp + sign
        )
        return copy, runs

    def arrival(which, way, step):
        sign = 1 - 2 * way
        g = dp - sign * (step + 1)
        ref = slots[which](g)
        copy = remote(
            ref, ref, z_send.at[way, which, step], z_recv.at[way, which, step], dp=dp
        )
        return copy, (g >= 0) & (g < groups)

    inner = (dp > 0) & (dp < groups - 1)

    def start_hop(which):
        for way in range(2):
            copy, runs = hop(which, way, 0)
            pl.when(runs)(copy.start)

    def forward(which, step):
        for way in range(2):
            copy, comes = arrival(which, way, step)
            onward = hop(which, way, step + 1)[0]

            @pl.when(comes & inner)
            def _():
                copy.wait_recv()
                onward.start()

    def take(which, step):
        for way in range(2):
            copy, comes = arrival(which, way, step)
            pl.when(comes & jnp.logical_not(inner))(copy.wait_recv)

    def both(which, step):
        forward(which, step)
        take(which, step)

    def share(n, g):
        diagonal = core == 0
        q = [
            spot, spot, spot, jnp.where(diagonal, tx * ty_size + across, other * ty_size + ty),
            tx * ty_size + across, other * ty_size + ty, other * ty_size + across,
        ][n]
        where = [
            dict(ty=across), dict(tx=other), dict(ty=partner),
            dict(tx=jnp.where(diagonal, other, tx), ty=jnp.where(diagonal, ty, across)),
            dict(ty=partner), dict(ty=partner), dict(ty=partner),
        ][n]
        ref = a_part(g, q)
        return remote(ref, ref, a_send.at[n, g], a_recv.at[n, g], **where)

    def shared(n, g):
        q = [
            tx * ty_size + across, other * ty_size + ty, tx * ty_size + partner,
            other * ty_size + across, tx * ty_size + far, other * ty_size + partner,
            other * ty_size + far,
        ][n]
        ref = a_part(g, q)
        return remote(ref, ref, a_send.at[n, g], a_recv.at[n, g], ty=partner)

    def share_first(g):
        for n in (0, 1, 2):
            share(n, g).start()

    def share_second(g):
        shared(0, g).wait_recv()
        shared(1, g).wait_recv()
        for n in (3, 4, 5):
            share(n, g).start()

    def share_third(g):
        shared(3, g).wait_recv()
        share(6, g).start()

    def share_wait(g):
        for n in (2, 4, 5, 6):
            shared(n, g).wait_recv()

    def arrived(step, act):
        for way in range(2):
            g = dp - (1 - 2 * way) * (step + 1)

            @pl.when((g >= 0) & (g < groups))
            def _():
                act(g)

    for k in range(chunks):
        crossing(0, k, ty, tx).start()
    own_rows(0, ty).start()

    loads[0].wait()
    turned_a = wa_f[...].T
    wide_a = jnp.where(spot % 2 == 0, turned_a[:arows], turned_a[arows:]).astype(jnp.bfloat16)
    here = pl.ds(pl.multiple_of(spot * arows, arows), arows)
    was[dp, here, :LATENT] = wide_a[:, :LATENT]
    twice = (
        lax.broadcasted_iota(jnp.int32, (ROPE, 2 * ROPE), 0)
        == lax.broadcasted_iota(jnp.int32, (ROPE, 2 * ROPE), 1) % ROPE
    ).astype(jnp.bfloat16)
    was[dp, here, LATENT:] = dot32(wide_a[:, LATENT:], twice).astype(jnp.bfloat16)
    start_hop(A)
    loads[1].wait()
    wbs[dp] = wb_f[...].astype(jnp.bfloat16)
    start_hop(B)
    loads[2].wait()
    turned_q = pltpu.roll(wq_f[:, NOPE:], 2 * NOPE - ROPE, 1)
    wqs[dp, :, NOPE:] = turned_q[:, NOPE:].astype(jnp.bfloat16)
    wqs[dp, :, :NOPE] = wq_f[:, :NOPE].astype(jnp.bfloat16)
    start_hop(Q)
    wrs[dp] = turned_q[:, :NOPE].astype(jnp.bfloat16)
    share_first(dp)
    loads[3].wait()
    woz[dp] = wo_f[...].T.astype(jnp.bfloat16)

    def vocab_step(k, _):
        slot = k % 2

        @pl.when(k + 1 < count)
        def _():
            vocab_load(k + 1, 1 - slot).start()

        vocab_load(k, slot).wait()
        cols = pl.ds(pl.multiple_of(k * slab, slab), slab)
        table[:, cols] = stage[slot].astype(jnp.bfloat16)
        return 0

    part_rows = 32

    def norm(slot, prompt):
        def body(i, _):
            at = pl.multiple_of(i * part_rows, part_rows)
            value = normalize(xs[slot, prompt, pl.ds(at, part_rows)], again_ref[...])
            value = value.astype(jnp.bfloat16)
            to = pl.multiple_of(prompt * LEN + slot * quarter + at, part_rows)
            for b in range(groups):
                h[b, pl.ds(to, part_rows)] = value[:, b * block : (b + 1) * block]
            return 0

        lax.fori_loop(0, quarter // part_rows, body, 0)

    span_rows = 512

    def project(g, first):
        own = owner_ref[g]

        def body(i, _):
            at = pl.ds(pl.multiple_of(i * span_rows, span_rows), span_rows)
            rows_in = h[own, at]
            for low, high, weights in ((NOPE, QCOLS, wqs), (QCOLS, QCOLS + ACOLS, was)):
                term = dot32(rows_in, weights[g])
                acc[at, low:high] = term if first else acc[at, low:high] + term
            return 0

        lax.fori_loop(0, LEN // span_rows, body, 0)

    def project_step(step):
        def one(way, _):
            g = dp - (1 - 2 * way) * (step + 1)

            @pl.when((g >= 0) & (g < groups))
            def _():
                share_wait(g)
                project(g, False)

            return 0

        lax.fori_loop(0, 2, one, 0)

    def project_all(p, targets):
        def body(i, _):
            at = pl.ds(pl.multiple_of(p * LEN + i * span_rows, span_rows), span_rows)
            for low, high, weights in targets:
                total = dot32(h[owner_ref[0], at], weights[0])
                for g in range(1, groups):
                    total = total + dot32(h[owner_ref[g], at], weights[g])
                acc[at, low:high] = total
            return 0

        lax.fori_loop(0, LEN // span_rows, body, 0)

    lax.fori_loop(0, 7, vocab_step, 0)
    both(A, 0)
    arrived(0, share_first)
    cross_start(1, 0)
    own_rows(1, ty).start()
    loads[4].wait()
    norm(ty, 0)
    cross_step(0, 0)
    both(B, 0)
    own_rows(0, partner).wait_recv()
    norm(partner, 0)
    both(Q, 0)
    cross_step(0, 1)
    lax.fori_loop(7, count, vocab_step, 0)
    side_step(0, 0)
    both(A, 1)
    arrived(1, share_first)
    share_second(dp)
    arrived(0, share_second)
    both(B, 1)
    norm(ty, 1)
    side_step(0, 1)
    norm(across, 0)
    share_third(dp)
    arrived(0, share_third)
    far_wait(0)
    norm(far, 0)
    cross_step(1, 0)
    both(Q, 1)
    start_hop(O)
    arrived(1, share_second)
    take(A, 2)
    arrived(2, share_first)
    cross_start(1, 1)
    share_wait(dp)
    project(dp, True)
    arrived(1, share_third)
    project_step(0)
    forward(O, 0)
    start_hop(R)
    side_step(1, 0)
    arrived(2, share_second)
    project_step(1)
    cross_step(1, 1)
    arrived(2, share_third)
    forward(O, 1)

    def stored(b):
        place = jnp.int32(0)
        for g in range(groups):
            place = jnp.where(owner_ref[g] == b, g, place)
        return place

    brows = LATENT // groups

    lane = lax.broadcasted_iota(jnp.int32, (TILE, 2 * ROPE), 1)

    def rotate(values, at):
        swapped = jnp.where(
            lane % ROPE < ROPE // 2,
            pltpu.roll(values, 2 * ROPE - ROPE // 2, 1),
            pltpu.roll(values, ROPE // 2, 1),
        )
        return values * cos_ref[at] + swapped * sin_ref[at]

    factor = (NOPE + ROPE) ** (-0.5) * 1.4426950408889634
    lives = [lengths_ref[deal_ref[dp * per_grp + p]] for p in range(per_grp)]

    def keys(p, tile, _):
        down = acc[pl.ds(pl.multiple_of(p * LEN + tile * TILE, TILE), TILE), QCOLS:]
        to = pl.ds(pl.multiple_of(tile * TILE, TILE), TILE)
        latent = normalize(down[:, :LATENT], lgain_ref[...]).astype(jnp.bfloat16)
        key_rope = rotate(down[:, LATENT:], to).astype(jnp.bfloat16)
        key_val = dot32(latent, wbl[...]).astype(jnp.bfloat16)
        for head in range(heads):
            k_ref[p, head, to, :NOPE] = key_val[:, 2 * head * NOPE : (2 * head + 1) * NOPE]
            k_ref[p, head, to, NOPE:] = key_rope
            v_ref[p, head, to] = key_val[:, (2 * head + 1) * NOPE : (2 * head + 2) * NOPE]
        return 0


    def hears(p, slot, head):
        return heard.at[p, slot * heads + head]

    def heads_of(head, p, tile, slot):
        return remote(
            o_ref.at[head, tile, p], hears(p, tx * ty_size + slot, head),
            o_send.at[head, p, tile], o_recv.at[head, p, slot], ty=tile,
        )

    def passed(head, p, slot, slot_tx, source=None):
        ref = hears(p, slot_tx * ty_size + slot, head)
        return remote(
            ref if source is None else source, ref,
            f_send.at[head, p, slot], f_recv.at[head, p, slot], tx=other,
        )

    def own_passed(head, p, tile):
        return passed(head, p, ty, tx, o_ref.at[head, tile, p])

    def relay(head, p):
        for k in range(1, ty_size):
            slot = (ty + k) % ty_size
            heads_of(head, p, ty, slot).wait_recv()
            passed(head, p, slot, tx).start()

    tile_order = (3, 1, 2, 0)

    def attention(head, p):
        live = jnp.where(p == 0, lives[0], lives[1])
        last = jnp.zeros((1, NOPE), jnp.float32)
        nope_at = (1 - head) * NOPE
        for t in tile_order:
            span = (t + 1) * TILE
            at = pl.ds(pl.multiple_of(p * LEN + t * TILE, TILE), TILE)
            turned = rotate(acc[at, 2 * NOPE : QCOLS], pl.ds(t * TILE, TILE))
            i = lax.broadcasted_iota(jnp.int32, (TILE, span), 0) + t * TILE
            j = lax.broadcasted_iota(jnp.int32, (TILE, span), 1)
            allowed = j <= jnp.minimum(i, live - 1)
            mine = jnp.where(lane // ROPE == 1 - head, turned, 0.0)
            query = jnp.concatenate([acc[at, nope_at : nope_at + NOPE], mine], axis=1)
            score = lax.dot_general(
                query.astype(jnp.bfloat16), k_ref[p, head, :span], (((1,), (1,)), ((), ())),
                preferred_element_type=jnp.float32,
            )
            score = jnp.where(allowed, score, -1e30)
            expo = jnp.exp2((score - jnp.max(score, axis=-1, keepdims=True)) * factor)
            prob = expo * (1.0 / jnp.sum(expo, axis=-1, keepdims=True))
            out = dot32(prob.astype(jnp.bfloat16), v_ref[p, head, :span]).astype(jnp.bfloat16)
            o_ref[head, t, p] = out
            at_last = lax.broadcasted_iota(jnp.int32, (TILE, NOPE), 0) + t * TILE == live - 1
            last = last + jnp.sum(
                jnp.where(at_last, out.astype(jnp.float32), 0.0), axis=0, keepdims=True
            )

            @pl.when(ty == t)
            def _():
                heard[p, spot * heads + head] = out
                own_passed(head, p, t).start()

            @pl.when(ty != t)
            def _():
                heads_of(head, p, t, ty).start()

        for k in range(per_grp):

            @pl.when(p == k)
            def _():
                ends_ref[spot, k : k + 1, head * NOPE : (head + 1) * NOPE] = last

    pieces = 2
    rows_of = piece // pieces

    def wide(j, q, slot_tx, slot_ty):
        at = (slot_tx * ty_size + slot_ty) * piece + q * rows_of
        return wos.at[j, pl.ds(pl.multiple_of(at, rows_of), rows_of)]

    def move(n, j, q, slot_tx, slot_ty, source=None, **where):
        ref = wide(j, q, slot_tx, slot_ty)
        return remote(
            ref if source is None else source, ref, w_send.at[n, j, q], w_recv.at[n, j, q],
            **where,
        )

    def given(j, q):
        source = give.at[j, pl.ds(q * rows_of, rows_of)]
        return move(0, j, q, tx, ty, source, tx=other)

    early = [jnp.where(dp < groups // 2, k, groups - 1 - k) for k in range(steps)]
    late = jnp.where(dp < groups // 2, groups - 1, 0)

    def aim(g):
        return owner_ref[g] // (groups // tx_size)

    def first_for(side):
        found = early[-1]
        for g in early[-2::-1]:
            found = jnp.where(aim(g) == side, g, found)
        return found

    def first_rows(side):
        found = woz[early[-1]]
        for g in early[-2::-1]:
            found = jnp.where(aim(g) == side, woz[g], found)
        return found

    def second_for(side):
        found = late
        for g in early:
            found = jnp.where((aim(g) == side) & (g != first_for(side)), g, found)
        return found

    mine_at = pl.ds(pl.multiple_of(spot * piece, piece), piece)

    def spread(j, give_rows, keep_rows):
        give[j] = give_rows
        for q in range(pieces):
            given(j, q).start()
        wos[j, mine_at] = keep_rows
        for q in range(pieces):
            move(1, j, q, tx, ty, ty=across).start()
            move(2, j, q, tx, ty, ty=partner).start()

    def spread_on(j):
        for q in range(pieces):
            move(0, j, q, other, ty, tx=other).wait_recv()
            move(3, j, q, other, ty, ty=across).start()
            move(4, j, q, other, ty, ty=partner).start()

    def spread_in(j):
        for q in range(pieces):
            move(1, j, q, tx, across, ty=across).wait_recv()
            move(5, j, q, tx, across, ty=partner).start()

    def spread_last(j):
        for q in range(pieces):
            move(3, j, q, other, across, ty=across).wait_recv()
            move(6, j, q, other, across, ty=partner).start()

    def first_head(p, _):
        @pl.when(p == 0)
        def _():
            take(B, 2)
            take(Q, 2)
            project_step(2)
            for b in range(groups):
                wbl[b * brows : (b + 1) * brows] = wbs[stored(b)]

        @pl.when(p == 1)
        def _():
            side_step(1, 1)
            own_rows(1, partner).wait_recv()
            norm(partner, 1)
            norm(across, 1)
            far_wait(1)
            norm(far, 1)
            relay(0, 0)
            take(O, 0)
            take(O, 1)
            spread(0, first_rows(other), first_rows(tx))
            project_all(1, ((NOPE, QCOLS, wqs), (QCOLS, QCOLS + ACOLS, was)))
            take(O, 2)
            spread(1, woz[second_for(other)], woz[second_for(tx)])

        lax.fori_loop(0, LEN // TILE, functools.partial(keys, p), 0)
        attention(0, p)
        pl.when(p == 0)(lambda: forward(R, 0))
        return 0

    lax.fori_loop(0, per_grp, first_head, 0)
    forward(R, 1)
    relay(0, 1)
    spread_on(0)
    spread_in(0)
    for step in range(steps):
        take(R, step)

    def second_head(p, _):
        project_all(p, ((0, NOPE, wrs),))
        attention(1, p)

        @pl.when(p == 0)
        def _():
            spread_on(1)
            spread_in(1)

        @pl.when(p == 1)
        def _():
            relay(1, 0)

        return 0

    lax.fori_loop(0, per_grp, second_head, 0)

    def row_of(k, slot):
        peer = (spot + k) % plane
        return remote(
            ends_ref.at[spot], ends_ref.at[slot], e_send.at[k], e_recv.at[k],
            tx=peer // ty_size, ty=peer % ty_size,
        )

    for k in range(1, plane):
        row_of(k, spot).start()
    relay(1, 1)
    for j in range(2):
        spread_last(j)
    for head in range(heads):
        for p in range(per_grp):
            for k in range(ty_size):
                passed(head, p, (ty + k) % ty_size, other).wait_recv()
    for p in range(per_grp):
        for n in range(plane * heads):
            mixed[p, :, n * NOPE : (n + 1) * NOPE] = heard[p, n]
    for p in range(per_grp):
        tile = (lives[p] - 1) // quarter
        inside = lax.broadcasted_iota(jnp.int32, (quarter, half), 0) + tile * quarter
        tokens = xs[jnp.maximum(tile, 0), p, :, pl.ds(pl.multiple_of(tx * half, half), half)]
        base_ref[p : p + 1] = jnp.sum(
            jnp.where(inside == lives[p] - 1, tokens.astype(jnp.float32), 0.0),
            axis=0, keepdims=True,
        )
    for k in range(1, plane):
        row_of(k, (spot + plane - k) % plane).wait_recv()
    line_ref[...] = jnp.zeros_like(line_ref)
    for slot in range(plane):
        line_ref[0:per_grp, slot * piece : (slot + 1) * piece] = ends_ref[slot]
    for j in range(2):
        for q in range(pieces):
            move(2, j, q, tx, partner, ty=partner).wait_recv()
            move(4, j, q, other, partner, ty=partner).wait_recv()
            move(5, j, q, tx, far, ty=partner).wait_recv()
            move(6, j, q, other, far, ty=partner).wait_recv()

    spots = [jnp.where(owner_ref[first_for(tx)] % 2 == i, 0, 1) for i in range(2)]
    chosen = line_ref[...].astype(jnp.bfloat16)
    peers = groups * tx_size
    place = dp * tx_size + tx
    for i in range(2):
        cols = slice(i * block, (i + 1) * block)
        value = base_ref[:, cols] + dot32(chosen, wos[spots[i]])[:per_grp]
        full[place, :, cols] = value.astype(jnp.bfloat16).astype(jnp.float32)

    def along_peers(k, slot):
        peer = (place + k) % peers
        return remote(
            full.at[place], full.at[slot], r_send.at[k], r_recv.at[k],
            dp=peer // tx_size, tx=peer % tx_size,
        )

    for k in range(1, peers):
        along_peers(k, place).start()

    strip = 256

    def out_step(n, _):
        for i in range(2):

            @pl.when(n // 2 == i)
            def _():
                inside = pl.ds(pl.multiple_of((n % 2) * strip, strip), strip)
                cols = pl.ds(pl.multiple_of(n * strip, strip), strip)
                model = pl.ds(pl.multiple_of(tx * half + n * strip, strip), strip)
                for p in range(per_grp):
                    total = dot32(mixed[p], wos[spots[i], :, inside])
                    hidden_ref[p, :, cols] = (
                        xs[ty, p, :, model].astype(jnp.float32) + total
                    ).astype(jnp.bfloat16)

        return 0

    lax.fori_loop(0, 4, out_step, 0)

    for k in range(1, peers):
        along_peers(k, (place + peers - k) % peers).wait_recv()
    for g in range(groups):
        for t in range(tx_size):
            rows_ref[g * per_grp : (g + 1) * per_grp, t * half : (t + 1) * half] = full[
                g * tx_size + t
            ]
    final = normalize(rows_ref[...], fgain_ref[...])
    owner = owner_ref[dp]
    mine = jnp.zeros((groups * per_grp, block), jnp.float32)
    for g in range(groups):
        mine = jnp.where(owner == g, final[:, g * block : (g + 1) * block], mine)
    mine = mine.astype(jnp.bfloat16)

    def logit_step(k, _):
        cols = pl.ds(pl.multiple_of(k * slab, slab), slab)
        logits = dot32(mine, table[:, cols])
        for g in range(groups):
            part[g, :, cols] = logits[g * per_grp : (g + 1) * per_grp]
        return 0

    parts = 2
    share_words = words // parts

    def along_dp(n, k, slot):
        peer = (dp + k) % groups
        cols = pl.ds(n * share_words, share_words)
        return remote(
            part.at[peer, :, cols], incoming.at[slot, :, cols], l_send.at[n, k], l_recv.at[n, k],
            dp=peer,
        )

    for n in range(parts):
        lax.fori_loop(n * count // parts, (n + 1) * count // parts, logit_step, 0)
        for k in range(1, groups):
            along_dp(n, k, dp).start()
    for n in range(parts):
        cols = slice(n * share_words, (n + 1) * share_words)
        total = part[dp, :, cols]
        for k in range(1, groups):
            slot = (dp + groups - k) % groups
            along_dp(n, k, slot).wait_recv()
            total = total + incoming[slot, :, cols]
        out_ref[:, cols] = total

    for p in range(per_grp):
        for k in range(chunks):
            crossing(p, k, ty, tx).wait_send()
            sideways(p, k, tx).wait_send()
            inward(p, k, 0, across, tx).wait_send()
            inward(p, k, 1, across, other).wait_send()
        own_rows(p, ty).wait_send()
    for step in range(steps):
        for which in range(5):
            for way in range(2):
                copy, runs = hop(which, way, step)
                pl.when(runs)(copy.wait_send)
    for g in range(groups):
        for n in range(7):
            share(n, g).wait_send()
    for head in range(heads):
        for p in range(per_grp):
            own_passed(head, p, ty).wait_send()
            for k in range(1, ty_size):
                slot = (ty + k) % ty_size
                heads_of(head, p, slot, ty).wait_send()
                passed(head, p, slot, tx).wait_send()
    for j in range(2):
        for q in range(pieces):
            given(j, q).wait_send()
            move(1, j, q, tx, ty, ty=across).wait_send()
            move(2, j, q, tx, ty, ty=partner).wait_send()
            move(3, j, q, other, ty, ty=across).wait_send()
            move(4, j, q, other, ty, ty=partner).wait_send()
            move(5, j, q, tx, across, ty=partner).wait_send()
            move(6, j, q, other, across, ty=partner).wait_send()
    for k in range(1, plane):
        row_of(k, spot).wait_send()
    for k in range(1, peers):
        along_peers(k, place).wait_send()
    for n in range(parts):
        for k in range(1, groups):
            along_dp(n, k, dp).wait_send()


def hand_on_kernel(hidden_ref, logits_ref, hidden_out, logits_out, held, words, reads, writes):
    parts = [(hidden_ref.at[p], held.at[p], hidden_out.at[p]) for p in range(held.shape[0])]
    parts.append((logits_ref, words, logits_out))
    inward = [
        pltpu.make_async_copy(source, there, reads.at[n])
        for n, (source, there, _) in enumerate(parts)
    ]
    outward = [
        pltpu.make_async_copy(there, target, writes.at[n])
        for n, (_, there, target) in enumerate(parts)
    ]
    for copy in inward:
        copy.start()
    for first, second in zip(inward, outward):
        first.wait()
        second.start()
    for copy in outward:
        copy.wait()


def hand_on(hidden, logits):
    hbm = pl.BlockSpec(memory_space=pl.ANY)
    return pl.pallas_call(
        hand_on_kernel,
        in_specs=[hbm, hbm],
        out_specs=[hbm, hbm],
        out_shape=[
            jax.ShapeDtypeStruct(hidden.shape, hidden.dtype),
            jax.ShapeDtypeStruct(logits.shape, logits.dtype),
        ],
        scratch_shapes=[
            pltpu.VMEM(hidden.shape, hidden.dtype),
            pltpu.VMEM(logits.shape, logits.dtype),
            pltpu.SemaphoreType.DMA((hidden.shape[0] + 1,)),
            pltpu.SemaphoreType.DMA((hidden.shape[0] + 1,)),
        ],
    )(hidden, logits)


def layer(groups, owner, lengths, deal, x, again, lgain, fgain, wq, wa, wb, wo, vocab):
    per_grp, quarter, width = x.shape
    block, words = vocab.shape
    half = width // 2
    piece = 2 * NOPE
    slab = 512
    steps = groups - 1
    peers = 2 * groups
    position = np.arange(LEN, dtype=np.float32)
    frequency = np.power(
        np.float32(10000.0), -np.arange(ROPE // 2, dtype=np.float32) / np.float32(ROPE // 2)
    ).astype(np.float32)
    angles = (position[:, None] * frequency).astype(np.float32).astype(np.float64)
    cosine, sine = np.cos(angles), np.sin(angles)
    cosine = jnp.asarray(np.concatenate([cosine] * 4, axis=1).astype(np.float32))
    sine = jnp.asarray(np.concatenate([-sine, sine, -sine, sine], axis=1).astype(np.float32))
    dma = pltpu.SemaphoreType.DMA
    vmem = pl.BlockSpec(memory_space=pltpu.VMEM)
    smem = pl.BlockSpec(memory_space=pltpu.SMEM)
    hbm = pl.BlockSpec(memory_space=pl.ANY)
    bf16 = lambda *dims: pltpu.VMEM(dims, jnp.bfloat16)
    f32 = lambda *dims: pltpu.VMEM(dims, jnp.float32)
    return pl.pallas_call(
        functools.partial(layer_kernel, groups),
        in_specs=[smem, smem, smem, hbm, vmem, vmem, vmem, vmem, vmem, hbm, hbm, hbm, hbm, hbm],
        out_specs=[vmem, vmem],
        out_shape=[
            jax.ShapeDtypeStruct((per_grp, quarter, half), jnp.bfloat16),
            jax.ShapeDtypeStruct((per_grp, words), jnp.float32),
        ],
        scratch_shapes=[
            bf16(4, per_grp, quarter, width),
            bf16(groups, per_grp * LEN, block),
            bf16(groups, block, NOPE),
            bf16(groups, block, 2 * NOPE),
            bf16(groups, block, ACOLS),
            bf16(groups, LATENT // groups, 2 * piece),
            bf16(LATENT, 2 * piece),
            bf16(groups, piece, block),
            bf16(2, piece, block),
            bf16(2, 8 * piece, block),
            f32(per_grp * LEN, QCOLS + ACOLS),
            bf16(per_grp, 2, LEN, 2 * NOPE),
            bf16(per_grp, 2, LEN, NOPE),
            bf16(2, 4, per_grp, TILE, NOPE),
            bf16(per_grp, 16, TILE, NOPE),
            bf16(per_grp, TILE, 8 * piece),
            bf16(block, words),
            f32(2, block, slab),
            f32(*wq.shape),
            f32(wa.shape[1], block // 4),
            f32(*wb.shape),
            f32(block, piece),
            f32(8, per_grp, piece),
            f32(per_grp, half),
            f32(8, width),
            f32(peers, per_grp, half),
            f32(groups * per_grp, width),
            f32(groups, per_grp, words),
            f32(groups, per_grp, words),
            dma((5,)), dma((2,)),
            dma((per_grp, 4)), dma((per_grp, 4)), dma((per_grp, 4)), dma((per_grp, 4)),
            dma((2, per_grp, 4)), dma((2, per_grp, 4)), dma((per_grp,)), dma((per_grp,)),
            dma((2, 5, steps)), dma((2, 5, steps)), dma((7, groups)), dma((7, groups)),
            dma((2, per_grp, 4)), dma((2, per_grp, 4)), dma((2, per_grp, 4)),
            dma((2, per_grp, 4)), dma((7, 2, 2)), dma((7, 2, 2)),
            dma((8,)), dma((8,)), dma((peers,)), dma((peers,)), dma((2, groups)),
            dma((2, groups)),
        ],
        compiler_params=pltpu.CompilerParams(
            collective_id=0, has_side_effects=True, vmem_limit_bytes=60 * 1024 * 1024
        ),
        cost_estimate=pl.CostEstimate(
            flops=16_000_000_000, bytes_accessed=24_000_000, transcendentals=3_000_000
        ),
    )(owner, lengths, deal, x, again, lgain, fgain, cosine, sine, wq, wa.T, wb, wo, vocab)


def load_vocab(vocab_chunk, vocab_ref, table, v_sem):
    loads = []
    for k in range(vocab_ref.shape[1] // vocab_chunk):
        cols = pl.ds(k * vocab_chunk, vocab_chunk)
        loads.append(
            pltpu.make_async_copy(vocab_ref.at[:, cols], table.at[:, cols], v_sem.at[k])
        )
        loads[-1].start()
    return loads


def next_token(
    groups, tx_size, ty_size, vocab_chunk, loads, owner_ref, picked_ref, gain_ref, out_ref, seen, full,
    rows_ref, table, part, incoming, t_send, t_recv, r_send, r_recv, l_send, l_recv,
):
    dp, tx, ty = lax.axis_index("dp"), lax.axis_index("tx"), lax.axis_index("ty")
    per_grp, half = picked_ref.shape
    block = table.shape[0]
    peers = groups * tx_size
    place = dp * tx_size + tx
    count = len(loads)

    def along_ty(k, slot):
        return remote(
            picked_ref, seen.at[slot], t_send.at[k], t_recv.at[k], ty=(ty + k) % ty_size
        )

    for k in range(1, ty_size):
        along_ty(k, ty).start()
    merged = picked_ref[...]
    for k in range(1, ty_size):
        slot = (ty + ty_size - k) % ty_size
        along_ty(k, slot).wait_recv()
        merged = merged + seen[slot]
    full[place] = merged

    def along_peers(k, slot):
        peer = (place + k) % peers
        return remote(
            full.at[place], full.at[slot], r_send.at[k], r_recv.at[k],
            dp=peer // tx_size, tx=peer % tx_size,
        )

    for k in range(1, peers):
        along_peers(k, place).start()
    for k in range(1, peers):
        along_peers(k, (place + peers - k) % peers).wait_recv()
    for g in range(groups):
        for t in range(tx_size):
            rows_ref[g * per_grp : (g + 1) * per_grp, t * half : (t + 1) * half] = full[
                g * tx_size + t
            ]
    final = normalize(rows_ref[...], gain_ref[...])
    owner = owner_ref[dp]
    mine = jnp.zeros((groups * per_grp, block), jnp.float32)
    for g in range(groups):
        mine = jnp.where(owner == g, final[:, g * block : (g + 1) * block], mine)
    mine = mine.astype(jnp.bfloat16)
    for k in range(count):
        loads[k].wait()
        cols = slice(k * vocab_chunk, (k + 1) * vocab_chunk)
        logits = dot32(mine, table[:, cols].astype(jnp.bfloat16))
        for g in range(groups):
            part[g, :, cols] = logits[g * per_grp : (g + 1) * per_grp]

    def along_dp(k, slot):
        peer = (dp + k) % groups
        return remote(part.at[peer], incoming.at[slot], l_send.at[k], l_recv.at[k], dp=peer)

    for k in range(1, groups):
        along_dp(k, dp).start()
    total = part[dp]
    for k in range(1, groups):
        slot = (dp + groups - k) % groups
        along_dp(k, slot).wait_recv()
        total = total + incoming[slot]
    out_ref[...] = total
    for k in range(1, ty_size):
        along_ty(k, ty).wait_send()
    for k in range(1, peers):
        along_peers(k, place).wait_send()
    for k in range(1, groups):
        along_dp(k, dp).wait_send()


def tail_kernel(
    groups, tx_size, ty_size, vocab_chunk, owner_ref, picked_ref, gain_ref, vocab_ref, out_ref,
    seen, full, rows_ref, table, part, incoming, t_send, t_recv, r_send, r_recv, l_send, l_recv,
    v_sem,
):
    dp, tx, ty = lax.axis_index("dp"), lax.axis_index("tx"), lax.axis_index("ty")
    peers = groups * tx_size
    place = dp * tx_size + tx
    loads = load_vocab(vocab_chunk, vocab_ref, table, v_sem)
    for k in range(1, ty_size):
        greet(ty=(ty + k) % ty_size)
    for k in range(1, peers):
        peer = (place + k) % peers
        greet(dp=peer // tx_size, tx=peer % tx_size)
    pl.semaphore_wait(pltpu.get_barrier_semaphore(), ty_size + peers - 2)
    next_token(
        groups, tx_size, ty_size, vocab_chunk, loads, owner_ref, picked_ref, gain_ref, out_ref,
        seen, full, rows_ref, table, part, incoming, t_send, t_recv, r_send, r_recv, l_send,
        l_recv,
    )


def tail(groups, tx_size, ty_size, owner, picked, gain, vocab):
    per_grp, half = picked.shape
    block, words = vocab.shape
    vocab_chunk = 512
    peers = groups * tx_size
    dma = pltpu.SemaphoreType.DMA
    vmem = pl.BlockSpec(memory_space=pltpu.VMEM)
    return pl.pallas_call(
        functools.partial(tail_kernel, groups, tx_size, ty_size, vocab_chunk),
        in_specs=[
            pl.BlockSpec(memory_space=pltpu.SMEM), vmem, vmem, pl.BlockSpec(memory_space=pl.ANY),
        ],
        out_specs=vmem,
        out_shape=jax.ShapeDtypeStruct((per_grp, words), jnp.float32),
        scratch_shapes=[
            pltpu.VMEM((ty_size, per_grp, half), jnp.float32),
            pltpu.VMEM((peers, per_grp, half), jnp.float32),
            pltpu.VMEM((groups * per_grp, half * tx_size), jnp.float32),
            pltpu.VMEM((block, words), jnp.float32),
            pltpu.VMEM((groups, per_grp, words), jnp.float32),
            pltpu.VMEM((groups, per_grp, words), jnp.float32),
            dma((ty_size,)), dma((ty_size,)), dma((peers,)), dma((peers,)),
            dma((groups,)), dma((groups,)), dma((words // vocab_chunk,)),
        ],
        compiler_params=pltpu.CompilerParams(
            collective_id=1, has_side_effects=True, vmem_limit_bytes=40 * 1024 * 1024
        ),
        cost_estimate=pl.CostEstimate(
            flops=100_000_000, bytes_accessed=16_000_000, transcendentals=0
        ),
    )(owner, picked, gain, vocab)


def rotate_half(values, position):
    half_dim = values.shape[-1] // 2
    frequency = 10000.0 ** (-jnp.arange(half_dim, dtype=jnp.float32) / half_dim)
    angles = position.astype(jnp.float32)[..., None] * frequency
    cosine = jnp.cos(angles)
    sine = jnp.sin(angles)
    first_half = values[..., :half_dim]
    second_half = values[..., half_dim:]
    return jnp.concatenate(
        [first_half * cosine - second_half * sine, first_half * sine + second_half * cosine],
        axis=-1,
    )


def split_positions(
    inputs, inverse, live_len, attn_gain, latent_gain, w_query, w_down_kv, w_up_kv, w_out
):
    groups = lax.axis_size("dp")

    def arrange(gathered):
        block_rows = gathered.shape[0] // groups
        return jnp.concatenate(
            [
                lax.dynamic_slice_in_dim(gathered, inverse[g] * block_rows, block_rows, 0)
                for g in range(groups)
            ],
            axis=0,
        )

    query_w, down_w, up_w, out_w = (
        lax.all_gather(w_query.astype(jnp.bfloat16), "dp", axis=0, tiled=True),
        lax.all_gather(w_down_kv.astype(jnp.bfloat16), "dp", axis=0, tiled=True),
        lax.all_gather(w_up_kv.astype(jnp.bfloat16), "dp", axis=0, tiled=True),
        lax.all_gather(w_out.astype(jnp.bfloat16), "dp", axis=0, tiled=True),
    )
    query_w = arrange(query_w)
    down_w = arrange(down_w)
    up_w = arrange(up_w)
    out_w = arrange(out_w)
    query_w, up_w = (
        lax.all_gather(query_w, "ty", axis=1, tiled=True),
        lax.all_gather(up_w, "ty", axis=1, tiled=True),
    )
    per_grp, quarter, width = inputs.shape
    heads = query_w.shape[1] // (NOPE + ROPE)
    position = lax.axis_index("ty") * quarter + jnp.arange(quarter, dtype=jnp.int32)
    flat_rows = inputs.reshape(per_grp * quarter, width)
    normed = normalize(flat_rows, attn_gain).astype(jnp.bfloat16)
    queries = jnp.dot(normed, query_w, preferred_element_type=jnp.float32).reshape(
        per_grp, quarter, heads, NOPE + ROPE
    )
    queries = jnp.concatenate(
        [queries[..., :NOPE], rotate_half(queries[..., NOPE:], position[None, :, None])], axis=-1
    ).astype(jnp.bfloat16)
    down_proj = jnp.dot(normed, down_w, preferred_element_type=jnp.float32).reshape(
        per_grp, quarter, LATENT + ROPE
    )
    latent = normalize(down_proj[..., :LATENT], latent_gain).astype(jnp.bfloat16)
    key_rope = rotate_half(down_proj[..., LATENT:], position[None, :]).astype(jnp.bfloat16)
    gathered = lax.all_gather(
        jnp.concatenate([latent, key_rope], axis=-1), "ty", axis=1, tiled=True
    )
    key_val = jnp.dot(gathered[..., :LATENT], up_w, preferred_element_type=jnp.float32).astype(
        jnp.bfloat16
    )
    rope_all = gathered[..., LATENT:]
    key_val = key_val.reshape(per_grp, LEN, heads, 2, NOPE)
    key_nope = key_val[:, :, :, 0]
    values = key_val[:, :, :, 1]
    score_scale = (NOPE + ROPE) ** (-0.5)
    scores = (
        jnp.einsum(
            "pqhd,pkhd->phqk", queries[..., :NOPE], key_nope, preferred_element_type=jnp.float32
        )
        + jnp.einsum(
            "pqhd,pkd->phqk", queries[..., NOPE:], rope_all, preferred_element_type=jnp.float32
        )
    ) * score_scale
    key_pos = jnp.arange(LEN, dtype=jnp.int32)
    allowed = (key_pos[None, None, :] <= position[None, :, None]) & (
        key_pos[None, None, :] < live_len[:, None, None]
    )
    scores = jnp.where(allowed[:, None], scores, -1e30)
    top = jnp.max(scores, axis=-1, keepdims=True)
    expo = jnp.exp(scores - top)
    softmax_w = (expo / jnp.sum(expo, axis=-1, keepdims=True)).astype(jnp.bfloat16)
    attended = jnp.einsum(
        "phqk,pkhd->pqhd", softmax_w, values, preferred_element_type=jnp.float32
    ).astype(jnp.bfloat16)
    attended = attended.reshape(per_grp * quarter, heads * NOPE)
    own_width = width // lax.axis_size("tx")
    col_start = lax.axis_index("tx") * own_width
    partial_value = lax.dot_general(
        attended, out_w, (((1,), (1,)), ((), ())), preferred_element_type=jnp.float32
    ).reshape(per_grp, quarter, width)
    summed = lax.psum_scatter(partial_value, "tx", scatter_dimension=2, tiled=True)
    residual = lax.dynamic_slice_in_dim(inputs, col_start, own_width, 2)
    layer_out = (residual.astype(jnp.float32) + summed).astype(jnp.bfloat16)
    return layer_out


def shards(
    inputs,
    lengths,
    prompt_deal,
    block_owner,
    attn_gain,
    latent_gain,
    final_gain,
    w_query,
    w_down_kv,
    w_up_kv,
    w_out,
    w_vocab,
):
    groups = lax.axis_size("dp")
    dp, tx, ty = lax.axis_index("dp"), lax.axis_index("tx"), lax.axis_index("ty")
    per_grp, quarter, width = inputs.shape
    half = width // lax.axis_size("tx")
    whole_heads = w_query.shape[1] == QCOLS and w_up_kv.shape[1] == 4 * NOPE
    here = whole_heads and (lax.axis_size("tx"), lax.axis_size("ty"), per_grp) == (2, 4, 2)
    if here and groups == 4 and (quarter, width) == (TILE, 4 * w_query.shape[0]):
        return hand_on(
            *layer(
                groups, block_owner, lengths, prompt_deal, inputs, attn_gain[None],
                latent_gain[None], final_gain[None], w_query, w_down_kv, w_up_kv, w_out, w_vocab,
            )
        )

    order = jnp.arange(groups, dtype=jnp.int32)
    inverse = jnp.sum(
        jnp.where(block_owner[None, :] == order[:, None], order[None, :], 0), axis=1
    ).astype(jnp.int32)
    slots = dp * per_grp + jnp.arange(per_grp, dtype=jnp.int32)
    names = jnp.arange(lengths.shape[0], dtype=jnp.int32)

    def at_index(values, index):
        return jnp.sum(jnp.where(names[None] == index[:, None], values[None], 0), axis=1)

    live_len = at_index(lengths, at_index(prompt_deal, slots))
    layer_out = split_positions(
        inputs, inverse, live_len, attn_gain, latent_gain, w_query, w_down_kv, w_up_kv, w_out
    )

    at = live_len - 1 - ty * quarter
    picked = jnp.stack(
        [
            lax.dynamic_slice(
                layer_out, (i, jnp.clip(at[i], 0, quarter - 1), 0), (1, 1, half)
            ).reshape(half)
            for i in range(per_grp)
        ]
    ).astype(jnp.float32)
    inside = (at >= 0) & (at < quarter)
    picked = jnp.where(inside[:, None], picked, 0.0)
    logits = tail(
        groups, lax.axis_size("tx"), lax.axis_size("ty"), block_owner, picked, final_gain[None],
        w_vocab,
    )
    return (layer_out, logits)


def solution(mesh):
    placed = (
        P("dp", "ty", None),
        P(),
        P(),
        P(),
        P(),
        P(),
        P(),
        P("dp", ("tx", "ty")),
        P("dp", None),
        P("dp", ("tx", "ty")),
        P("dp", "tx"),
        P("dp", ("tx", "ty")),
    )
    return jax.shard_map(
        shards,
        mesh=mesh,
        in_specs=placed,
        out_specs=(P("dp", "ty", "tx"), P("dp", ("tx", "ty"))),
        check_vma=False,
    )
```
